32 devices in a mesh: section: 8 (over y, x, core), rep: 4 (over z).
Axes of the slice: x: 2, y: 2, z: 4, core: 2. Of those that a mesh axis runs over, the one named last changes fastest.
Arguments:
- features: bfloat16 [16384, 128], P('section'), may hold values from -6 to 6
- order: int32 [16384], P('section'), may hold values from 0 to 2047, as said below
- tiles: bfloat16 [8, 4, 2, 96, 128, 128], P('section', 'rep'), may hold values from -0.125 to 0.125
- tile_rows: int32 [8, 4, 2, 96], P('section', 'rep'), may hold values from 0 to 15, as said below
- tile_cols: int32 [8, 4, 2, 96], P('section', 'rep'), may hold values from 0 to 15, as said below
- live: int32 [8, 4, 2], P('section', 'rep'), may hold values from 1 to 96, as said below
- weight: bfloat16 [128, 128], replicated, may hold values from -0.5 to 0.5
- cotangent: bfloat16 [16384, 128], P('section'), may hold values from -6 to 6
Outputs:
- hidden: bfloat16 [16384, 128], P('section')
- weight_grad: float32 [128, 128], replicated
- feature_grad: bfloat16 [16384, 128], P('section')
The draws below stay inside these ranges and needn't reach their ends.
Inputs may be any that keep to these rules, and one draw needn't show every extreme that they name: `order`: within each panel of 2048 rows, a permutation of the local row numbers. For one section, replica and round, the 96 pairs (tile_rows, tile_cols) are distinct. `tile_cols`: block column within the panel j * 4 + r for replica r and round j. Some section, replica and round has all 96 slots live.
All inputs are finite; a program needn't handle non-finite values.
Results may differ from the reference program's by a relative error of at most 0.012.
Values may be sent and summed in bfloat16 or wider, within the bound.
No kernel may reach another device: no remote copies, remote signals or barrier semaphores. Data moves between devices by JAX's collectives and lax.ppermute only.
A program may use at most 192 MiB of HBM per device.

```python
import math
import jax
import jax.numpy as jnp
from jax import lax

F = 128
BLK = 128
PB = 16
SLOTS = 96
NJ = 2
PANEL = 2048
NODES = 16384
N_SECTION = 8
N_REP = 4


def draw_order(key, part):
    key_list = jax.random.split(key, NODES // PANEL)
    permuted = jax.vmap(lambda subkey: jax.random.permutation(subkey, PANEL))(key_list)
    return permuted.reshape(-1).astype(jnp.int32)


def block_positions(key):
    sections = NODES // PANEL
    key_list = jax.random.split(jax.random.fold_in(key, 7), sections * sections)
    positions = jax.vmap(lambda subkey: jax.random.permutation(subkey, PB * PB)[:SLOTS])(key_list)
    return positions.reshape(sections, sections // NJ, NJ, SLOTS).astype(jnp.int32)


def draw_tile_rows(key, part):
    return block_positions(key) // PB


def draw_tile_cols(key, part):
    return block_positions(key) % PB


def draw_live(key, part):
    sections = NODES // PANEL
    shape_all = (sections, sections // NJ, NJ)
    draw_one = jax.random.randint(jax.random.fold_in(key, 1), shape_all, 1, SLOTS + 1)
    draw_two = jax.random.randint(jax.random.fold_in(key, 2), shape_all, 1, SLOTS + 1)
    counts = jnp.minimum(draw_one, draw_two).reshape(-1)
    full_at = jax.random.randint(jax.random.fold_in(key, 3), (), 0, counts.shape[0])
    counts = counts.at[full_at].set(SLOTS)
    return counts.reshape(shape_all).astype(jnp.int32)


def block_levels(stream_key, dims, cuts, least, top_value):
    level = 1.0
    for dim, blocks in cuts:
        steps = jax.random.uniform(jax.random.fold_in(jax.random.fold_in(stream_key, 6), dim), (blocks,), jnp.float32, least / len(cuts), top_value / len(cuts))
        level = level * jnp.repeat(jnp.exp(steps), dims[dim] // blocks).reshape((-1,) + (1,) * (len(dims) - 1 - dim))
    return level


def scatter_about(key, dims, width, most, cuts=(), kind=jnp.bfloat16):
    array = width * jax.random.normal(key, dims, jnp.float32)
    if cuts:
        array = array * block_levels(key, dims, cuts, -0.22, 0.18)
    return jnp.clip(array, -most, most).astype(kind)


def setup_inputs(seed: int = 0) -> dict:
    seeds = jax.random.split(jax.random.key(seed), 9)
    return {
        "features": scatter_about(seeds[0], (NODES, F), 1.0, 6.0, ((0, 8),)),
        "order": draw_order(jax.random.fold_in(seeds[8], 71), 0),
        "tiles": scatter_about(seeds[2], (N_SECTION, N_REP, NJ, SLOTS, BLK, BLK), (BLK * N_SECTION * SLOTS // (3 * PB)) ** -0.5, 0.125, ((0, 8), (1, 4))),
        "tile_rows": draw_tile_rows(jax.random.fold_in(seeds[8], 71), 0),
        "tile_cols": draw_tile_cols(jax.random.fold_in(seeds[8], 71), 0),
        "live": draw_live(jax.random.fold_in(seeds[8], 71), 0),
        "weight": scatter_about(seeds[6], (F, F), F ** -0.5, 0.5),
        "cotangent": scatter_about(seeds[7], (NODES, F), 1.0, 6.0, ((0, 8),)),
    }


def reference(features, order, tiles, tile_rows, tile_cols, live, weight, cotangent):
    sections = NODES // PANEL
    panel_base = jnp.arange(NODES, dtype=jnp.int32) // PANEL * PANEL
    source = panel_base + order
    reordered = jnp.take(features, source, axis=0)
    blocks_in = reordered.reshape(sections, PB, BLK, F)
    slot_ids = jnp.arange(SLOTS, dtype=jnp.int32)
    block_ids = jnp.arange(PB, dtype=jnp.int32)

    def pair_data(section_no, pair_no):
        rep_no = pair_no % N_REP
        round_no = pair_no // N_REP
        tile_set = tiles[section_no, rep_no, round_no].astype(jnp.float32)
        row_ids = tile_rows[section_no, rep_no, round_no]
        col_ids = tile_cols[section_no, rep_no, round_no]
        alive_mask = slot_ids < live[section_no, rep_no, round_no]
        return (tile_set, row_ids, col_ids, alive_mask)

    def forward_section(section_no):

        def add_pair(pair_no, running):
            tile_set, row_ids, col_ids, alive_mask = pair_data(section_no, pair_no)
            picked = jnp.take(blocks_in[pair_no], col_ids, axis=0).astype(jnp.float32)
            products = jnp.einsum('kab,kbf->kaf', tile_set, picked)
            select = ((row_ids[None, :] == block_ids[:, None]) & alive_mask[None, :]).astype(jnp.float32)
            return running + jnp.einsum('pk,kaf->paf', select, products, precision=lax.Precision.HIGHEST)
        return lax.fori_loop(0, sections, add_pair, jnp.zeros((PB, BLK, F), jnp.float32))
    summed = lax.map(forward_section, jnp.arange(sections, dtype=jnp.int32))
    aggregated = summed.reshape(NODES, F).astype(jnp.bfloat16)
    preact = jnp.dot(aggregated, weight, preferred_element_type=jnp.float32)
    hidden = jax.nn.silu(preact).astype(jnp.bfloat16)
    sigmoid_part = jax.nn.sigmoid(preact)
    grad_pre = (cotangent.astype(jnp.float32) * sigmoid_part * (1.0 + preact * (1.0 - sigmoid_part))).astype(jnp.bfloat16)
    weight_grad = jnp.dot(aggregated.T, grad_pre, preferred_element_type=jnp.float32) * (1.0 / math.sqrt(NODES))
    upstream = jnp.dot(grad_pre, weight.T, preferred_element_type=jnp.float32).astype(jnp.bfloat16)
    up_blocks = upstream.reshape(sections, PB, BLK, F)

    def backward_section(carry, section_no):
        own_rows = up_blocks[section_no]

        def add_pair(pair_no, running):
            tile_set, row_ids, col_ids, alive_mask = pair_data(section_no, pair_no)
            picked = jnp.take(own_rows, row_ids, axis=0).astype(jnp.float32)
            products = jnp.einsum('kab,kaf->kbf', tile_set, picked)
            select = ((col_ids[None, :] == block_ids[:, None]) & alive_mask[None, :]).astype(jnp.float32)
            term = jnp.einsum('pk,kbf->pbf', select, products, precision=lax.Precision.HIGHEST)
            term = lax.optimization_barrier(term.astype(jnp.bfloat16)).astype(jnp.float32)
            return running.at[pair_no].add(term)
        return (lax.fori_loop(0, sections, add_pair, carry), None)
    grad_total, _ = lax.scan(backward_section, jnp.zeros((sections, PB, BLK, F), jnp.float32), jnp.arange(sections, dtype=jnp.int32))
    reordered_grad = grad_total.reshape(NODES, F).astype(jnp.bfloat16)
    feature_grad = jnp.zeros((NODES, F), jnp.bfloat16).at[source].set(reordered_grad)
    return (hidden, weight_grad, feature_grad)
```

```python
import functools
import math

import jax
import jax.numpy as jnp
from jax import lax
from jax.experimental import pallas as pl
from jax.experimental.pallas import tpu as pltpu
from jax.sharding import PartitionSpec as P

F32 = jnp.float32
BF16 = jnp.bfloat16
MIB = 1 << 20


def params(mib):
    return pltpu.CompilerParams(vmem_limit_bytes=mib * MIB)


def cost(flops, nbytes):
    return pl.CostEstimate(flops=int(flops), bytes_accessed=int(nbytes), transcendentals=0)


def whole_spec(array):
    zeros = (0,) * array.ndim
    return pl.BlockSpec(array.shape, lambda *_: zeros)


def reorder_body(order_ref, feat_ref, out_ref):
    rows, panel = order_ref.shape[0], feat_ref.shape[0]
    hot = lax.broadcasted_iota(jnp.int32, (rows, panel), 1) == order_ref[...]
    hot = jnp.where(hot, 1.0, 0.0).astype(BF16)
    out_ref[...] = jnp.dot(hot, feat_ref[...], preferred_element_type=F32).astype(BF16)


def reorder(order_col, features, part, parts):
    panel, width = features.shape
    rows = panel // parts
    step = min(256, rows)
    first = part * (rows // step)
    return pl.pallas_call(
        reorder_body,
        out_shape=jax.ShapeDtypeStruct((rows, width), BF16),
        grid=(rows // step,),
        in_specs=[
            pl.BlockSpec((step, 1), lambda i: (first + i, 0)),
            whole_spec(features),
        ],
        out_specs=pl.BlockSpec((step, width), lambda i: (i, 0)),
        compiler_params=params(32),
        cost_estimate=cost(2 * rows * panel * width, 4 * rows * width),
        name="reorder",
    )(order_col, features)


def lay_body(rows_ref, cols_ref, live_ref, tile_ref, out_ref):
    j, g = pl.program_id(0), pl.program_id(1)
    group, block = tile_ref.shape[1], tile_ref.shape[2]
    panel = out_ref.shape[1]

    @pl.when(g == 0)
    def _():
        @pl.loop(0, panel // block)
        def _(i):
            at = pl.multiple_of(i * block, block)
            out_ref[0, pl.ds(at, block), :] = jnp.zeros((block, panel), BF16)

    for k in range(group):
        slot = g * group + k

        @pl.when(slot < live_ref[j])
        def _():
            row = pl.multiple_of(rows_ref[j, slot] * block, block)
            col = pl.multiple_of(cols_ref[j, slot] * block, block)
            out_ref[0, pl.ds(row, block), pl.ds(col, block)] = tile_ref[0, k]


def lay_out(tiles, rows, cols, live, panel):
    rounds, slots, block, _ = tiles.shape
    group = math.gcd(slots, 16)
    return pl.pallas_call(
        lay_body,
        out_shape=jax.ShapeDtypeStruct((rounds, panel, panel), BF16),
        grid_spec=pltpu.PrefetchScalarGridSpec(
            num_scalar_prefetch=3,
            grid=(rounds, slots // group),
            in_specs=[pl.BlockSpec((1, group, block, block), lambda j, g, *_: (j, g, 0, 0))],
            out_specs=pl.BlockSpec((1, panel, panel), lambda j, g, *_: (j, 0, 0)),
        ),
        compiler_params=params(40),
        cost_estimate=cost(0, 2 * rounds * panel * panel * 2),
        name="lay_out",
    )(rows, cols, live, tiles)


def forward_body(ids_ref, a_ref, *refs):
    xs, out_ref = refs[:-1], refs[-1]
    halves = len(xs) // a_ref.shape[0]
    acc = None
    for n, x_ref in enumerate(xs):
        slot, half = n // halves, n % halves
        rows = x_ref.shape[0]
        left = a_ref[ids_ref[1 + slot], :, half * rows : (half + 1) * rows]
        term = jnp.dot(left, x_ref[...], preferred_element_type=F32)
        acc = term if acc is None else acc + term
    out_ref[...] = acc.astype(out_ref.dtype)


def forward_share(ids, dense, xs, share_rows, dtype):
    rounds, panel, _ = dense.shape
    width = xs[0].shape[1]
    step = 128
    per = share_rows // step
    return pl.pallas_call(
        forward_body,
        out_shape=jax.ShapeDtypeStruct((share_rows, width), dtype),
        grid_spec=pltpu.PrefetchScalarGridSpec(
            num_scalar_prefetch=1,
            grid=(per,),
            in_specs=[
                pl.BlockSpec((rounds, step, panel), lambda i, ids: (0, ids[0] * per + i, 0))
            ]
            + [whole_spec(x) for x in xs],
            out_specs=pl.BlockSpec((step, width), lambda i, ids: (i, 0)),
        ),
        compiler_params=params(32),
        cost_estimate=cost(
            2 * rounds * share_rows * panel * width, 2 * rounds * share_rows * panel
        ),
        name="forward_share",
    )(ids, dense, *xs)


def middle_body(ids_ref, w_ref, co_ref, *refs):
    count = len(refs) - 5
    shares = refs[:count]
    hidden_ref, up_ref, grad_ref, agg_all, pre_all = refs[count:]
    weight = w_ref[...]
    rows = shares[0].shape[0]
    for n, share in enumerate(shares):
        at = pl.multiple_of(ids_ref[n] * rows, rows)
        agg = share[...]
        agg_all[pl.ds(at, rows), :] = agg
        pre = jnp.dot(agg, weight, preferred_element_type=F32)
        gate = 1.0 / (1.0 + jnp.exp(-pre))
        hidden_ref[pl.ds(at, rows), :] = (pre * gate).astype(BF16)
        co = co_ref[pl.ds(at, rows), :].astype(F32)
        grad_pre = (co * gate * (1.0 + pre * (1.0 - gate))).astype(BF16)
        pre_all[pl.ds(at, rows), :] = grad_pre
        up_ref[:, pl.ds(at, rows)] = lax.dot_general(
            weight, grad_pre, (((1,), (1,)), ((), ())), preferred_element_type=F32
        ).astype(BF16)
    grad_ref[...] = lax.dot_general(
        agg_all[...], pre_all[...], (((0,), (0,)), ((), ())), preferred_element_type=F32
    )


def middle(ids, weight, cotangent, shares):
    panel, width = cotangent.shape
    operands = (weight, cotangent, *shares)
    return pl.pallas_call(
        middle_body,
        out_shape=(
            jax.ShapeDtypeStruct((panel, width), BF16),
            jax.ShapeDtypeStruct((width, panel), BF16),
            jax.ShapeDtypeStruct((width, width), F32),
        ),
        grid_spec=pltpu.PrefetchScalarGridSpec(
            num_scalar_prefetch=1,
            grid=(1,),
            in_specs=[whole_spec(x) for x in operands],
            out_specs=[
                pl.BlockSpec((panel, width), lambda *_: (0, 0)),
                pl.BlockSpec((width, panel), lambda *_: (0, 0)),
                pl.BlockSpec((width, width), lambda *_: (0, 0)),
            ],
            scratch_shapes=[pltpu.VMEM((panel, width), BF16)] * 2,
        ),
        compiler_params=params(32),
        cost_estimate=cost(6 * panel * width * width, 8 * panel * width),
        name="middle",
    )(ids, *operands)


def backward_body(ids_ref, up_ref, a_ref, out_ref):
    out_ref[0, 0] = jnp.dot(up_ref[...], a_ref[0], preferred_element_type=F32).astype(
        out_ref.dtype
    )


def backward(ids, dense, upstream, pairs, chips, dtype):
    panel = dense.shape[1]
    width = upstream.shape[0]
    length = panel // chips
    return pl.pallas_call(
        backward_body,
        out_shape=jax.ShapeDtypeStruct((chips, pairs, width, length), dtype),
        grid_spec=pltpu.PrefetchScalarGridSpec(
            num_scalar_prefetch=1,
            grid=(chips, pairs),
            in_specs=[
                whole_spec(upstream),
                pl.BlockSpec((1, panel, length), lambda d, p, ids: (ids[chips + p], 0, ids[d])),
            ],
            out_specs=pl.BlockSpec((1, 1, width, length), lambda d, p, ids: (d, p, 0, 0)),
        ),
        compiler_params=params(32),
        cost_estimate=cost(2 * pairs * panel * panel * width, 2 * pairs * panel * panel),
        name="backward",
    )(ids, upstream, dense)


def restore_body(ids_ref, order_ref, *refs):
    parts, out_ref = refs[:-1], refs[-1]
    rows = out_ref.shape[0]
    length = parts[0].shape[1]
    base = pl.program_id(0) * rows
    acc = None
    for n, part in enumerate(parts):
        at = pl.multiple_of(ids_ref[n] * length, length)
        target = order_ref[:, pl.ds(at, length)]
        hot = lax.broadcasted_iota(jnp.int32, (rows, length), 0) + base == target
        hot = jnp.where(hot, 1.0, 0.0).astype(BF16)
        term = lax.dot_general(
            hot, part[...], (((1,), (1,)), ((), ())), preferred_element_type=F32
        )
        acc = term if acc is None else acc + term
    out_ref[...] = acc.astype(BF16)


def restore(ids, order_row, parts, panel):
    width = parts[0].shape[0]
    rows = 256
    return pl.pallas_call(
        restore_body,
        out_shape=jax.ShapeDtypeStruct((panel, width), BF16),
        grid_spec=pltpu.PrefetchScalarGridSpec(
            num_scalar_prefetch=1,
            grid=(panel // rows,),
            in_specs=[whole_spec(order_row)] + [whole_spec(p) for p in parts],
            out_specs=pl.BlockSpec((rows, width), lambda i, ids: (i, 0)),
        ),
        compiler_params=params(32),
        cost_estimate=cost(2 * panel * panel * width, 4 * panel * width),
        name="restore",
    )(ids, order_row, *parts)


def tree_sum(terms):
    while len(terms) > 1:
        terms = [terms[i] + terms[i + 1] for i in range(0, len(terms), 2)]
    return terms[0]


def shards(features, order, tiles, tile_rows, tile_cols, live, weight, cotangent):
    reps = lax.axis_size("rep")
    sections = lax.axis_size("section")
    rep = lax.axis_index("rep")
    section = lax.axis_index("section")
    panel, width = features.shape
    rounds = tiles.shape[2]
    chips = sections // 2
    pairs = rounds // 2
    near = reps // 2
    share_rows = panel // reps
    length = panel // chips
    chip, core = section // 2, section % 2

    def over_chips(x, d):
        return lax.ppermute(x, "section", [(s, s ^ (2 * d)) for s in range(sections)])

    def over_cores(x):
        return lax.ppermute(x, "section", [(s, s ^ 1) for s in range(sections)])

    def over_reps(x, d):
        return lax.ppermute(x, "rep", [(r, r ^ d) for r in range(reps)])

    def from_owner(x, d):
        moves = []
        for r in range(reps):
            for j in range(rounds):
                source = j * reps + r
                target = (source ^ (2 * d)) ^ ((d // near) & 1)
                moves.append((source * reps + r, target * reps + r))
        return lax.ppermute(x, ("section", "rep"), moves)

    side = core ^ (rep % 2)
    low = (chip % near) ^ (rep // 2)
    row_of_chip = chip // near
    order_col = order.reshape(panel, 1)
    halves = 2
    mine = [[] for _ in range(pairs)]
    mate = [[] for _ in range(pairs)]
    for h in range(halves):
        own = reorder(order_col, features, h, halves)
        got = [own] + [from_owner(own, d) for d in range(1, chips)]
        for p in range(pairs):
            picked = got[2 * p * near]
            for e in range(2):
                for l in range(near):
                    if e or l:
                        picked = jnp.where(
                            (side == e) & (low == l), got[(2 * p + e) * near + l], picked
                        )
            mine[p].append(picked)
            mate[p].append(over_cores(picked))
    dense = lay_out(tiles[0, 0], tile_rows[0, 0], tile_cols[0, 0], live[0, 0], panel)
    xs, slot_ids = [], []
    for p in range(pairs):
        xs += mine[p] + mate[p]
        slot_ids += [row_of_chip ^ (2 * p + side), row_of_chip ^ (2 * p + 1 - side)]

    def share_of(d, dtype):
        ids = jnp.stack([rep ^ d] + slot_ids).astype(jnp.int32)
        return forward_share(ids, dense, xs, share_rows, dtype)

    sent = {d: over_reps(share_of(d, BF16), d) for d in reversed(range(1, reps))}
    total = share_of(0, F32)
    for d in range(1, reps):
        total = total + sent[d].astype(F32)
    aggregated = total.astype(BF16)
    shares = [aggregated] + [over_reps(aggregated, d) for d in range(1, reps)]
    share_ids = jnp.stack([rep ^ d for d in range(reps)]).astype(jnp.int32)
    hidden, upstream, grad_part = middle(share_ids, weight, cotangent, shares)

    chunk_ids = [chip ^ d for d in range(chips)]
    give = jnp.stack(chunk_ids + [2 * p + 1 - core for p in range(pairs)]).astype(jnp.int32)
    keep = jnp.stack(chunk_ids + [2 * p + core for p in range(pairs)]).astype(jnp.int32)
    given = over_cores(backward(give, dense, upstream, pairs, chips, BF16))
    kept = backward(keep, dense, upstream, pairs, chips, F32)
    chunks = [kept[d] + given[d].astype(F32) for d in range(chips)]
    arrived = [over_chips(chunks[d].astype(BF16), d).astype(F32) for d in range(1, chips)]
    reduced = tree_sum([chunks[0]] + arrived).astype(BF16)

    grad_part = grad_part + over_cores(grad_part)
    weight_grad = tree_sum([grad_part] + [over_chips(grad_part, d) for d in range(1, chips)])
    weight_grad = weight_grad * (1.0 / math.sqrt(panel * sections))

    spread = [reduced] + [over_reps(reduced, d) for d in range(1, reps)]
    stacked = jnp.stack(spread)

    def to_owner(k):
        moves = []
        for s in range(sections):
            u = (s // 2) ^ k
            moves.append((s, (2 * (u // reps) + s % 2) * reps + u % reps))
        u = chip ^ k
        block = stacked[(u % reps) ^ rep, u // reps]
        return lax.ppermute(block, "section", moves)

    parts = [to_owner(k) for k in range(chips)]
    mine_u = (section // reps // 2) * reps + section % reps
    part_ids = jnp.stack([mine_u ^ k for k in range(chips)]).astype(jnp.int32)
    feature_grad = restore(part_ids, order.reshape(1, panel), parts, panel)
    return (hidden, weight_grad, feature_grad)


def solution(mesh):
    placed = (
        P("section", None),
        P("section"),
        P("section", "rep", None, None, None, None),
        P("section", "rep", None, None),
        P("section", "rep", None, None),
        P("section", "rep", None),
        P(),
        P("section", None),
    )
    return jax.shard_map(
        shards,
        mesh=mesh,
        in_specs=placed,
        out_specs=(P("section", None), P(), P("section", None)),
        check_vma=False,
    )
```

```python
import functools
import math

import jax
import jax.numpy as jnp
from jax import lax
from jax.experimental import pallas as pl
from jax.experimental.pallas import tpu as pltpu
from jax.sharding import PartitionSpec as P

F32 = jnp.float32
BF16 = jnp.bfloat16
MIB = 1 << 20


def params(mib):
    return pltpu.CompilerParams(vmem_limit_bytes=mib * MIB)


def cost(flops, nbytes):
    return pl.CostEstimate(flops=int(flops), bytes_accessed=int(nbytes), transcendentals=0)


def whole_spec(array):
    zeros = (0,) * array.ndim
    return pl.BlockSpec(array.shape, lambda *_: zeros)


def streamed(array):
    return pltpu.with_memory_space_constraint(array, pltpu.HBM)


def reorder_body(order_ref, feat_ref, out_ref):
    rows, panel = order_ref.shape[0], feat_ref.shape[0]
    hot = lax.broadcasted_iota(jnp.int32, (rows, panel), 1) == order_ref[...]
    hot = jnp.where(hot, 1.0, 0.0).astype(BF16)
    out_ref[...] = jnp.dot(hot, feat_ref[...], preferred_element_type=F32).astype(BF16)


def reorder(order_col, features, part, parts):
    panel, width = features.shape
    rows = panel // parts
    step = min(256, rows)
    first = part * (rows // step)
    return pl.pallas_call(
        reorder_body,
        out_shape=jax.ShapeDtypeStruct((rows, width), BF16),
        grid=(rows // step,),
        in_specs=[
            pl.BlockSpec((step, 1), lambda i: (first + i, 0)),
            whole_spec(features),
        ],
        out_specs=pl.BlockSpec((step, width), lambda i: (i, 0)),
        compiler_params=params(12),
        cost_estimate=cost(2 * rows * panel * width, 4 * rows * width),
        name="reorder",
    )(order_col, features)


def plan_body(rows_ref, cols_ref, live_ref, _, out_ref, *, lists, cap, span, bits):
    rounds, slots = rows_ref.shape

    @pl.loop(0, lists * (cap + 1) // 8)
    def _(n):
        for t in range(8):
            out_ref[n * 8 + t] = 0

    for j in range(rounds):

        @pl.loop(0, live_ref[j])
        def _(k):
            row, col = rows_ref[j, k], cols_ref[j, k]
            name = (row // span) * rounds + j
            count = out_ref[lists * cap + name]
            out_ref[name * cap + count] = (((j * slots + k) << bits | row) << bits) | col
            out_ref[lists * cap + name] = count + 1


def make_plan(rows, cols, live, blocks, reps, after):
    rounds = rows.shape[0]
    lists, span = reps * rounds, blocks // reps
    cap = span * blocks
    body = functools.partial(
        plan_body, lists=lists, cap=cap, span=span, bits=(blocks - 1).bit_length()
    )
    smem = pl.BlockSpec(memory_space=pltpu.SMEM)
    return pl.pallas_call(
        body,
        out_shape=jax.ShapeDtypeStruct((lists * cap + lists,), jnp.int32),
        in_specs=[smem, smem, smem, pl.BlockSpec(memory_space=pl.ANY)],
        out_specs=smem,
        cost_estimate=cost(0, 8 * MIB),
        name="make_plan",
    )(rows, cols, live, after)


UNROLL = 8


def fetch(table_ref, tiles_ref, buf, sems, names, cap, bits):
    for m, name in enumerate(names):

        @pl.loop(0, table_ref[table_ref.shape[0] - lists_in(table_ref, cap) + name])
        def _(i):
            slot = table_ref[name * cap + i] >> (2 * bits)
            pltpu.make_async_copy(
                tiles_ref.at[slot], buf.at[m * cap + i], sems.at[m, i // UNROLL]
            ).start()


def lists_in(table_ref, cap):
    return table_ref.shape[0] // (cap + 1)


def each_group(table_ref, tiles_ref, buf, sems, names, cap, bits, step):
    base = table_ref.shape[0] - lists_in(table_ref, cap)
    for m, name in enumerate(names):
        count = table_ref[base + name]

        @pl.loop(0, (count + UNROLL - 1) // UNROLL)
        def _(g):
            for t in range(UNROLL):

                @pl.when(g * UNROLL + t < count)
                def _():
                    at = m * cap + g * UNROLL + t
                    pltpu.make_async_copy(tiles_ref.at[0], buf.at[at], sems.at[m, g]).wait()

            entries = [table_ref[name * cap + g * UNROLL + t] for t in range(UNROLL)]
            alive = [g * UNROLL + t < count for t in range(UNROLL)]
            step(m, m * cap + g * UNROLL, entries, alive)


def forward_body(ids_ref, table_ref, tiles_ref, *refs, cap, bits, rounds, span):
    xs, (out_ref, x_all, acc, buf, sems) = refs[:-5], refs[-5:]
    halves = len(xs) // rounds
    block = buf.shape[1]
    blocks = 1 << bits
    names = [ids_ref[0] * rounds + j for j in range(rounds)]
    fetch(table_ref, tiles_ref, buf, sems, names, cap, bits)
    for n, x_ref in enumerate(xs):
        slot, half = n // halves, n % halves
        rows = x_ref.shape[0]
        at = pl.multiple_of(ids_ref[1 + slot] * (rows * halves) + half * rows, rows)
        x_all[pl.ds(at, rows), :] = x_ref[...]
    acc[...] = jnp.zeros_like(acc)

    def step(m, first, entries, alive):
        terms = []
        for t in range(UNROLL):
            col = entries[t] & (blocks - 1)
            at = pl.multiple_of((m * blocks + col) * block, block)
            terms.append(
                jnp.dot(buf[first + t], x_all[pl.ds(at, block), :], preferred_element_type=F32)
            )
        for t in range(UNROLL):
            row = (entries[t] >> bits) & (span - 1)
            row = jnp.where(alive[t], row, span)
            acc[row] += terms[t]

    each_group(table_ref, tiles_ref, buf, sems, names, cap, bits, step)
    for i in range(span):
        out_ref[i * block : (i + 1) * block, :] = acc[i].astype(out_ref.dtype)


def forward_share(ids, table, tiles, xs, reps, dtype):
    rounds, slots, block, _ = tiles.shape
    width = xs[0].shape[1]
    panel = sum(x.shape[0] for x in xs) // rounds
    blocks = panel // block
    bits, span = (blocks - 1).bit_length(), blocks // reps
    cap = span * blocks
    return pl.pallas_call(
        functools.partial(forward_body, cap=cap, bits=bits, rounds=rounds, span=span),
        out_shape=jax.ShapeDtypeStruct((span * block, width), dtype),
        grid_spec=pltpu.PrefetchScalarGridSpec(
            num_scalar_prefetch=2,
            grid=(1,),
            in_specs=[pl.BlockSpec(memory_space=pltpu.HBM)] + [whole_spec(x) for x in xs],
            out_specs=pl.BlockSpec((span * block, width), lambda *_: (0, 0)),
            scratch_shapes=[
                pltpu.VMEM((rounds * panel, width), BF16),
                pltpu.VMEM((span + 1, block, width), F32),
                pltpu.VMEM((rounds * cap, block, block), BF16),
                pltpu.SemaphoreType.DMA((rounds, -(-cap // UNROLL))),
            ],
        ),
        compiler_params=params(24),
        cost_estimate=cost(2 * 64 * block * block * width, 6 * MIB),
        name="forward_share",
    )(ids, table, tiles.reshape(rounds * slots, block, block), *xs)


def gradient_of(agg, co, weight):
    pre = jnp.dot(agg, weight, preferred_element_type=F32)
    gate = 1.0 / (1.0 + jnp.exp(-pre))
    grad_pre = (co.astype(F32) * gate * (1.0 + pre * (1.0 - gate))).astype(BF16)
    return pre, gate, grad_pre


def up_body(ids_ref, w_ref, co_ref, *refs):
    shares, out_ref = refs[:-1], refs[-1]
    weight = w_ref[...]
    rows = shares[0].shape[0]
    for n, share in enumerate(shares):
        at = pl.multiple_of(ids_ref[n] * rows, rows)
        _, _, grad_pre = gradient_of(share[...], co_ref[pl.ds(at, rows), :], weight)
        out_ref[n] = lax.dot_general(
            weight, grad_pre, (((1,), (1,)), ((), ())), preferred_element_type=F32
        ).astype(BF16)


def up_shares(ids, weight, cotangent, shares):
    rows, width = shares[0].shape
    shape = (len(shares), width, rows)
    operands = (weight, cotangent, *shares)
    return pl.pallas_call(
        up_body,
        out_shape=jax.ShapeDtypeStruct(shape, BF16),
        grid_spec=pltpu.PrefetchScalarGridSpec(
            num_scalar_prefetch=1,
            grid=(1,),
            in_specs=[whole_spec(x) for x in operands],
            out_specs=pl.BlockSpec(shape, lambda *_: (0, 0, 0)),
        ),
        compiler_params=params(16),
        cost_estimate=cost(4 * len(shares) * rows * width * width, 2 * MIB),
        name="up_shares",
    )(ids, *operands)


def finish_body(ids_ref, w_ref, co_ref, *refs):
    shares, (_, hidden_ref, grad_ref, agg_all, pre_all) = refs[:-5], refs[-5:]
    weight = w_ref[...]
    rows = shares[0].shape[0]
    for n, share in enumerate(shares):
        at = pl.multiple_of(ids_ref[n] * rows, rows)
        agg = share[...]
        pre, gate, grad_pre = gradient_of(agg, co_ref[pl.ds(at, rows), :], weight)
        hidden_ref[pl.ds(at, rows), :] = (pre * gate).astype(BF16)
        agg_all[pl.ds(at, rows), :] = agg
        pre_all[pl.ds(at, rows), :] = grad_pre
    grad_ref[...] = lax.dot_general(
        agg_all[...], pre_all[...], (((0,), (0,)), ((), ())), preferred_element_type=F32
    )


def finish(ids, weight, cotangent, shares, after):
    panel, width = cotangent.shape
    operands = (weight, cotangent, *shares)
    return pl.pallas_call(
        finish_body,
        out_shape=(
            jax.ShapeDtypeStruct((panel, width), BF16),
            jax.ShapeDtypeStruct((width, width), F32),
        ),
        grid_spec=pltpu.PrefetchScalarGridSpec(
            num_scalar_prefetch=1,
            grid=(1,),
            in_specs=[whole_spec(x) for x in operands] + [pl.BlockSpec(memory_space=pl.ANY)],
            out_specs=[
                pl.BlockSpec((panel, width), lambda *_: (0, 0)),
                pl.BlockSpec((width, width), lambda *_: (0, 0)),
            ],
            scratch_shapes=[pltpu.VMEM((panel, width), BF16)] * 2,
        ),
        compiler_params=params(16),
        cost_estimate=cost(6 * panel * width * width, 8 * panel * width),
        name="finish",
    )(ids, *operands, after)


def backward_body(ids_ref, table_ref, tiles_ref, *refs, cap, bits, rounds, span, count, pairs):
    ups, rest = refs[: len(refs) - 4], refs[len(refs) - 4 :]
    out_ref, acc, buf, sems = rest
    start = None
    if len(ups) > 1:
        ups, start = ups[:-1], ups[-1]
    up = ups[0]
    block = buf.shape[1]
    blocks = 1 << bits
    names = [ids_ref[n] * rounds + ids_ref[count + p] for n in range(count) for p in range(pairs)]
    fetch(table_ref, tiles_ref, buf, sems, names, cap, bits)
    dump = pairs * blocks
    if start is None:
        acc[...] = jnp.zeros_like(acc)
    else:
        acc[pl.ds(0, dump)] = start[...]
        acc[dump] = jnp.zeros(acc.shape[1:], F32)

    def step(m, first, entries, alive):
        n, p = m // pairs, m % pairs
        terms = []
        for t in range(UNROLL):
            row = (entries[t] >> bits) & (span - 1)
            at = pl.multiple_of(row * block, block)
            terms.append(
                jnp.dot(up[n, :, pl.ds(at, block)], buf[first + t], preferred_element_type=F32)
            )
        for t in range(UNROLL):
            col = entries[t] & (blocks - 1)
            to = jnp.where(alive[t], p * blocks + col, dump)
            acc[to] += terms[t]

    each_group(table_ref, tiles_ref, buf, sems, names, cap, bits, step)
    if out_ref.shape == start_shape(acc):
        out_ref[...] = acc[pl.ds(0, dump)].astype(out_ref.dtype)
    else:
        chips, _, per = out_ref.shape[:3]
        for d in range(chips):
            for p in range(pairs):
                at = p * blocks + ids_ref[count + pairs + d] * per
                out_ref[d, p] = acc[pl.ds(at, per)].astype(out_ref.dtype)


def start_shape(acc):
    return (acc.shape[0] - 1,) + acc.shape[1:]


def backward(ids, table, tiles, up, start, reps, pairs, chips, dtype):
    rounds, slots, block, _ = tiles.shape
    count, width, rows = up.shape
    span = rows // block
    blocks = span * reps
    bits = (blocks - 1).bit_length()
    cap = span * blocks
    shape = (chips, pairs, blocks // chips, width, block) if chips else (pairs * blocks, width, block)
    zeros = (0,) * len(shape)
    operands = (up,) if start is None else (up, start)
    return pl.pallas_call(
        functools.partial(
            backward_body, cap=cap, bits=bits, rounds=rounds, span=span, count=count, pairs=pairs
        ),
        out_shape=jax.ShapeDtypeStruct(shape, dtype),
        grid_spec=pltpu.PrefetchScalarGridSpec(
            num_scalar_prefetch=2,
            grid=(1,),
            in_specs=[pl.BlockSpec(memory_space=pltpu.HBM)] + [whole_spec(x) for x in operands],
            out_specs=pl.BlockSpec(shape, lambda *_: zeros),
            scratch_shapes=[
                pltpu.VMEM((pairs * blocks + 1, width, block), F32),
                pltpu.VMEM((count * pairs * cap, block, block), BF16),
                pltpu.SemaphoreType.DMA((count * pairs, -(-cap // UNROLL))),
            ],
        ),
        compiler_params=params(40),
        cost_estimate=cost(2 * 64 * block * block * width, 6 * MIB),
        name="backward",
    )(ids, table, tiles.reshape(rounds * slots, block, block), *operands)


def restore_body(ids_ref, order_ref, *refs, count):
    parts, out_ref = refs[:count], refs[-1]
    rows = out_ref.shape[0]
    per, _, block = parts[0].shape
    base = pl.program_id(0) * rows
    acc = refs[count][...] if len(refs) > count + 1 else None
    for n, part in enumerate(parts):
        length = per * block
        at = pl.multiple_of(ids_ref[n] * length, length)
        target = order_ref[:, pl.ds(at, length)]
        hot = lax.broadcasted_iota(jnp.int32, (rows, length), 0) + base == target
        hot = jnp.where(hot, 1.0, 0.0).astype(BF16)
        columns = jnp.concatenate([part[b] for b in range(per)], axis=1)
        term = lax.dot_general(
            hot, columns, (((1,), (1,)), ((), ())), preferred_element_type=F32
        )
        acc = term if acc is None else acc + term
    out_ref[...] = acc.astype(out_ref.dtype)


def restore(ids, order_row, parts, start, dtype):
    panel = order_row.shape[1]
    width = parts[0].shape[1]
    rows = 512
    row_spec = pl.BlockSpec((rows, width), lambda i, ids: (i, 0))
    extra = () if start is None else (start,)
    return pl.pallas_call(
        functools.partial(restore_body, count=len(parts)),
        out_shape=jax.ShapeDtypeStruct((panel, width), dtype),
        grid_spec=pltpu.PrefetchScalarGridSpec(
            num_scalar_prefetch=1,
            grid=(panel // rows,),
            in_specs=[whole_spec(order_row)]
            + [whole_spec(p) for p in parts]
            + [row_spec for _ in extra],
            out_specs=row_spec,
        ),
        compiler_params=params(24),
        cost_estimate=cost(2 * panel * panel * width, 4 * panel * width),
        name="restore",
    )(ids, order_row, *parts, *extra)


def tree_sum(terms):
    while len(terms) > 1:
        terms = [terms[i] + terms[i + 1] for i in range(0, len(terms), 2)]
    return terms[0]


def shards(features, order, tiles, tile_rows, tile_cols, live, weight, cotangent):
    reps = lax.axis_size("rep")
    sections = lax.axis_size("section")
    rep = lax.axis_index("rep")
    section = lax.axis_index("section")
    panel, width = features.shape
    rounds = tiles.shape[2]
    chips = sections // 2
    pairs = rounds // 2
    near = reps // 2
    share_rows = panel // reps
    length = panel // chips
    chip, core = section // 2, section % 2

    def over_chips(x, d):
        return lax.ppermute(x, "section", [(s, s ^ (2 * d)) for s in range(sections)])

    def over_cores(x):
        return lax.ppermute(x, "section", [(s, s ^ 1) for s in range(sections)])

    def over_reps(x, d):
        return lax.ppermute(x, "rep", [(r, r ^ d) for r in range(reps)])

    def from_owner(x, d):
        moves = []
        for r in range(reps):
            for j in range(rounds):
                source = j * reps + r
                target = (source ^ (2 * d)) ^ ((d // near) & 1)
                moves.append((source * reps + r, target * reps + r))
        return lax.ppermute(x, ("section", "rep"), moves)

    side = core ^ (rep % 2)
    low = (chip % near) ^ (rep // 2)
    row_of_chip = chip // near
    order_col = order.reshape(panel, 1)
    halves = 2
    mine = [[] for _ in range(pairs)]
    mate = [[] for _ in range(pairs)]
    owns = [reorder(order_col, features, h, halves) for h in range(halves)]
    gots = [[own] + [from_owner(own, d) for d in range(1, chips)] for own in owns]
    own_tiles = tiles[0, 0]
    blocks = panel // own_tiles.shape[2]
    table = make_plan(tile_rows[0, 0], tile_cols[0, 0], live[0, 0], blocks, reps, owns[-1])
    for h in range(halves):
        got = gots[h]
        for p in range(pairs):
            picked = got[2 * p * near]
            for e in range(2):
                for l in range(near):
                    if e or l:
                        picked = jnp.where(
                            (side == e) & (low == l), got[(2 * p + e) * near + l], picked
                        )
            mine[p].append(picked)
            mate[p].append(over_cores(picked))
    xs, slot_ids = [], []
    for p in range(pairs):
        xs += mine[p] + mate[p]
        slot_ids += [row_of_chip ^ (2 * p + side), row_of_chip ^ (2 * p + 1 - side)]

    def share_of(d, dtype):
        ids = jnp.stack([rep ^ d] + slot_ids).astype(jnp.int32)
        return forward_share(ids, table, own_tiles, xs, reps, dtype)

    sent = {d: over_reps(share_of(d, BF16), d) for d in reversed(range(1, reps))}
    total = share_of(0, F32)
    for d in range(1, reps):
        total = total + sent[d].astype(F32)
    aggregated = total.astype(BF16)
    shares = [aggregated] + [over_reps(aggregated, d) for d in range(1, reps)]

    give = [2 * p + 1 - core for p in range(pairs)]
    keep = [2 * p + core for p in range(pairs)]
    chunk_ids = [chip ^ d for d in range(chips)]
    early, late = list(range(reps // 2)), list(range(reps // 2, reps))

    def id_list(*parts):
        return jnp.stack([x for part in parts for x in part]).astype(jnp.int32)

    early_ids, late_ids = [rep ^ d for d in early], [rep ^ d for d in late]
    up_early = up_shares(id_list(early_ids), weight, cotangent, [shares[d] for d in early])
    up_late = up_shares(id_list(late_ids), weight, cotangent, [shares[d] for d in late])

    def first_half(panels):
        ids = id_list(early_ids, panels)
        return backward(ids, table, own_tiles, up_early, None, reps, pairs, 0, F32)

    def second_half(panels, start, dtype):
        ids = id_list(late_ids, panels, chunk_ids)
        return backward(ids, table, own_tiles, up_late, start, reps, pairs, chips, dtype)

    started_give, started_keep = first_half(give), first_half(keep)
    given = over_cores(second_half(give, started_give, BF16))
    kept = second_half(keep, started_keep, F32)
    hidden, grad_part = finish(
        id_list(early_ids, late_ids), weight, cotangent, shares, kept
    )
    chunks = [kept[d] + given[d].astype(F32) for d in range(chips)]
    arrived = [over_chips(chunks[d].astype(BF16), d).astype(F32) for d in range(1, chips)]
    reduced = tree_sum([chunks[0]] + arrived).astype(BF16)

    grad_part = grad_part + over_cores(grad_part)
    weight_grad = tree_sum([grad_part] + [over_chips(grad_part, d) for d in range(1, chips)])
    weight_grad = weight_grad * (1.0 / math.sqrt(panel * sections))

    spread = [reduced] + [over_reps(reduced, d) for d in range(1, reps)]
    stacked = jnp.stack(spread)

    def to_owner(k):
        moves = []
        for s in range(sections):
            u = (s // 2) ^ k
            moves.append((s, (2 * (u // reps) + s % 2) * reps + u % reps))
        u = chip ^ k
        block = stacked[(u % reps) ^ rep, u // reps]
        return lax.ppermute(block, "section", moves)

    parts = [to_owner(k) for k in range(chips)]
    mine_u = (section // reps // 2) * reps + section % reps
    part_ids = [mine_u ^ k for k in range(chips)]
    order_row = order.reshape(1, panel)
    cut = chips // 2
    started = restore(id_list(part_ids[:cut]), order_row, parts[:cut], None, F32)
    feature_grad = restore(id_list(part_ids[cut:]), order_row, parts[cut:], started, BF16)
    return (hidden, weight_grad, feature_grad)


def solution(mesh):
    placed = (
        P("section", None),
        P("section"),
        P("section", "rep", None, None, None, None),
        P("section", "rep", None, None),
        P("section", "rep", None, None),
        P("section", "rep", None),
        P(),
        P("section", None),
    )
    return jax.shard_map(
        shards,
        mesh=mesh,
        in_specs=placed,
        out_specs=(P("section", None), P(), P("section", None)),
        check_vma=False,
    )
```

```python
import functools
import math

import jax
import jax.numpy as jnp
from jax import lax
from jax.experimental import pallas as pl
from jax.experimental.pallas import tpu as pltpu
from jax.sharding import PartitionSpec as P

F32 = jnp.float32
BF16 = jnp.bfloat16
MIB = 1 << 20


def params(mib):
    return pltpu.CompilerParams(vmem_limit_bytes=mib * MIB)


def cost(flops, nbytes):
    return pl.CostEstimate(flops=int(flops), bytes_accessed=int(nbytes), transcendentals=0)


def whole_spec(array):
    zeros = (0,) * array.ndim
    return pl.BlockSpec(array.shape, lambda *_: zeros)


def reorder_body(order_ref, feat_ref, out_ref):
    rows, panel = order_ref.shape[0], feat_ref.shape[0]
    hot = lax.broadcasted_iota(jnp.int32, (rows, panel), 1) == order_ref[...]
    hot = jnp.where(hot, 1.0, 0.0).astype(BF16)
    out_ref[...] = jnp.dot(hot, feat_ref[...], preferred_element_type=F32).astype(BF16)


def reorder(order_col, features, part, parts):
    panel, width = features.shape
    rows = panel // parts
    step = min(256, rows)
    first = part * (rows // step)
    return pl.pallas_call(
        reorder_body,
        out_shape=jax.ShapeDtypeStruct((rows, width), BF16),
        grid=(rows // step,),
        in_specs=[
            pl.BlockSpec((step, 1), lambda i: (first + i, 0)),
            whole_spec(features),
        ],
        out_specs=pl.BlockSpec((step, width), lambda i: (i, 0)),
        compiler_params=params(12),
        cost_estimate=cost(2 * rows * panel * width, 4 * rows * width),
        name="reorder",
    )(order_col, features)


REP, CHIP, CORE, SIDE, ROW, LOW, LIVE = range(7)
HALVES = 2
GROUP = 16


def in_vmem(array):
    return pltpu.with_memory_space_constraint(array, pltpu.VMEM)


def call(body, meta, operands, outs, scratch=(), vmem=(), mib=12, estimate=None, name=None):
    specs = [
        pl.BlockSpec(memory_space=pltpu.VMEM) if n in vmem else whole_spec(x)
        for n, x in enumerate(operands)
    ]
    operands = [in_vmem(x) if n in vmem else x for n, x in enumerate(operands)]
    return pl.pallas_call(
        body,
        out_shape=outs,
        grid_spec=pltpu.PrefetchScalarGridSpec(
            num_scalar_prefetch=1,
            grid=(1,),
            in_specs=specs,
            out_specs=jax.tree.map(whole_spec, outs),
            scratch_shapes=list(scratch),
        ),
        compiler_params=params(mib),
        cost_estimate=estimate or cost(0, MIB),
        name=name,
    )(meta, *operands)


def pick_body(meta_ref, *refs, near):
    options, out_ref = refs[:-1], refs[-1]
    for n, option in enumerate(options):

        @pl.when((meta_ref[SIDE] == n // near) & (meta_ref[LOW] == n % near))
        def _():
            out_ref[...] = option[...]


def pick(meta, options, near):
    out = jax.ShapeDtypeStruct(options[0].shape, options[0].dtype)
    return call(functools.partial(pick_body, near=near), meta, options, out, name="pick")


def walk(meta_ref, j, rounds, slots, step):
    count = meta_ref[LIVE + j]

    @pl.loop(0, (count + GROUP - 1) // GROUP)
    def _(g):
        first = j * slots + g * GROUP
        entries = [meta_ref[LIVE + rounds + first + t] for t in range(GROUP)]
        step(first, entries, [g * GROUP + t < count for t in range(GROUP)])


def forward_body(meta_ref, tiles_ref, *refs, rounds, slots, pairs, last):
    xs, rest = refs[: pairs * HALVES], refs[pairs * HALVES :]
    panel_ref, acc = rest[-2:]
    blocks, block, width = panel_ref.shape
    bits = (blocks - 1).bit_length()
    if last:
        start, outs = rest[0], rest[1:-2]
        acc[pl.ds(0, blocks)] = start[...]
        acc[blocks] = jnp.zeros((block, width), F32)
    else:
        outs = rest[:-2]
        acc[...] = jnp.zeros_like(acc)
    per = blocks // HALVES
    for p in range(pairs):
        for h in range(HALVES):
            panel_ref[h * per : (h + 1) * per] = xs[p * HALVES + h][...].reshape(per, block, width)

        def step(first, entries, alive):
            terms = []
            for t in range(GROUP):
                x = panel_ref[entries[t] & (blocks - 1)]
                terms.append(jnp.dot(tiles_ref[first + t], x, preferred_element_type=F32))
            for t in range(GROUP):
                acc[jnp.where(alive[t], entries[t] >> bits, blocks)] += terms[t]

        side = meta_ref[SIDE]
        j = meta_ref[ROW] ^ (2 * p + (1 - side if last else side))
        walk(meta_ref, j, rounds, slots, step)
    if last:
        span = blocks // len(outs)
        for d, out in enumerate(outs):
            at = (meta_ref[REP] ^ d) * span
            out[...] = acc[pl.ds(at, span)].reshape(out.shape).astype(out.dtype)
    else:
        outs[0][...] = acc[pl.ds(0, blocks)]


def forward(meta, tiles, rounds, xs, start, reps):
    block = tiles.shape[1]
    width = xs[0].shape[1]
    pairs = len(xs) // HALVES
    blocks = xs[0].shape[0] * HALVES // block
    last = start is not None
    if last:
        rows = blocks * block // reps
        outs = [jax.ShapeDtypeStruct((rows, width), BF16 if d else F32) for d in range(reps)]
    else:
        outs = [jax.ShapeDtypeStruct((blocks, block, width), F32)]
    body = functools.partial(
        forward_body, rounds=rounds, slots=tiles.shape[0] // rounds, pairs=pairs, last=last
    )
    got = call(
        body,
        meta,
        [tiles, *xs] + ([start] if last else []),
        outs,
        scratch=[pltpu.VMEM((blocks, block, width), BF16), pltpu.VMEM((blocks + 1, block, width), F32)],
        vmem=(0,),
        estimate=cost(2 * 64 * block * block * width, 12 * MIB),
        name="forward",
    )
    return got if last else got[0]


def total_body(_, own_ref, *refs):
    total = own_ref[...]
    for ref in refs[:-1]:
        total = total + ref[...].astype(F32)
    refs[-1][...] = total.astype(BF16)


def total_of(meta, own, others):
    out = jax.ShapeDtypeStruct(own.shape, BF16)
    return call(total_body, meta, [own, *others], out, name="total_of")


def gradient_of(agg, co, weight):
    pre = jnp.dot(agg, weight, preferred_element_type=F32)
    gate = 1.0 / (1.0 + jnp.exp(-pre))
    grad_pre = (co.astype(F32) * gate * (1.0 + pre * (1.0 - gate))).astype(BF16)
    return pre, gate, grad_pre


def up_body(meta_ref, w_ref, co_ref, *refs, first):
    shares, out_ref = refs[:-1], refs[-1]
    weight = w_ref[...]
    rows = shares[0].shape[0]
    for n, share in enumerate(shares):
        at = pl.multiple_of((meta_ref[REP] ^ (first + n)) * rows, rows)
        _, _, grad_pre = gradient_of(share[...], co_ref[pl.ds(at, rows), :], weight)
        out_ref[n] = lax.dot_general(
            weight, grad_pre, (((1,), (1,)), ((), ())), preferred_element_type=F32
        ).astype(BF16)


def up_shares(meta, weight, cotangent, shares, first):
    rows, width = shares[0].shape
    out = jax.ShapeDtypeStruct((len(shares), width, rows), BF16)
    return call(
        functools.partial(up_body, first=first),
        meta,
        [weight, cotangent, *shares],
        out,
        estimate=cost(4 * len(shares) * rows * width * width, 2 * MIB),
        name="up_shares",
    )


def finish_body(meta_ref, w_ref, co_ref, *refs):
    shares, (hidden_ref, grad_ref, agg_all, pre_all) = refs[:-5], refs[-4:]
    weight = w_ref[...]
    rows = shares[0].shape[0]
    for n, share in enumerate(shares):
        at = pl.multiple_of((meta_ref[REP] ^ n) * rows, rows)
        agg = share[...]
        pre, gate, grad_pre = gradient_of(agg, co_ref[pl.ds(at, rows), :], weight)
        hidden_ref[pl.ds(at, rows), :] = (pre * gate).astype(BF16)
        agg_all[pl.ds(at, rows), :] = agg
        pre_all[pl.ds(at, rows), :] = grad_pre
    grad_ref[...] = lax.dot_general(
        agg_all[...], pre_all[...], (((0,), (0,)), ((), ())), preferred_element_type=F32
    )


def finish(meta, weight, cotangent, shares, after):
    panel, width = cotangent.shape
    outs = (
        jax.ShapeDtypeStruct((panel, width), BF16),
        jax.ShapeDtypeStruct((width, width), F32),
    )
    after = after.reshape(-1, after.shape[-1])[:8]
    return call(
        finish_body,
        meta,
        [weight, cotangent, *shares, after],
        outs,
        scratch=[pltpu.VMEM((panel, width), BF16)] * 2,
        estimate=cost(6 * panel * width * width, 8 * panel * width),
        name="finish",
    )


def backward_body(meta_ref, tiles_ref, *refs, rounds, slots, pairs, keep):
    ups, (out_ref, up_all, acc) = refs[:-3], refs[-3:]
    chips, _, per, width, block = out_ref.shape
    blocks = chips * per
    bits = (blocks - 1).bit_length()
    count, _, rows = ups[0].shape
    for m, up in enumerate(ups):
        for n in range(count):
            at = pl.multiple_of((meta_ref[REP] ^ (m * count + n)) * rows, rows)
            up_all[:, pl.ds(at, rows)] = up[n]
    core = meta_ref[CORE]
    for p in range(pairs):
        acc[...] = jnp.zeros_like(acc)

        def step(first, entries, alive):
            terms = []
            for t in range(GROUP):
                at = pl.multiple_of((entries[t] >> bits) * block, block)
                terms.append(
                    jnp.dot(
                        up_all[:, pl.ds(at, block)],
                        tiles_ref[first + t],
                        preferred_element_type=F32,
                    )
                )
            for t in range(GROUP):
                acc[jnp.where(alive[t], entries[t] & (blocks - 1), blocks)] += terms[t]

        walk(meta_ref, 2 * p + (core if keep else 1 - core), rounds, slots, step)
        for d in range(chips):
            at = (meta_ref[CHIP] ^ d) * per
            out_ref[d, p] = acc[pl.ds(at, per)].astype(out_ref.dtype)


def backward(meta, tiles, rounds, ups, pairs, chips, keep):
    block = tiles.shape[1]
    count, width, rows = ups[0].shape
    panel = len(ups) * count * rows
    blocks = panel // block
    out = jax.ShapeDtypeStruct((chips, pairs, blocks // chips, width, block), F32 if keep else BF16)
    body = functools.partial(
        backward_body, rounds=rounds, slots=tiles.shape[0] // rounds, pairs=pairs, keep=keep
    )
    return call(
        body,
        meta,
        [tiles, *ups],
        out,
        scratch=[pltpu.VMEM((width, panel), BF16), pltpu.VMEM((blocks + 1, width, block), F32)],
        vmem=(0,),
        estimate=cost(2 * 64 * block * block * width, 12 * MIB),
        name="backward",
    )


def route_body(meta_ref, *refs, reps, chips):
    spread, outs = refs[:reps], refs[reps:]
    for k in range(chips):
        u = meta_ref[CHIP] ^ k
        p = u // reps
        for d in range(reps):

            @pl.when(((u % reps) ^ meta_ref[REP]) == d)
            def _():
                outs[k][...] = spread[d][p]


def route(meta, spread, chips):
    outs = [jax.ShapeDtypeStruct(spread[0].shape[1:], BF16)] * chips
    body = functools.partial(route_body, reps=len(spread), chips=chips)
    return call(body, meta, spread, outs, name="route")


def restore_body(ids_ref, order_ref, *refs, count):
    parts, out_ref = refs[:count], refs[-1]
    rows = out_ref.shape[0]
    per, _, block = parts[0].shape
    base = pl.program_id(0) * rows
    acc = refs[count][...] if len(refs) > count + 1 else None
    for n, part in enumerate(parts):
        length = per * block
        at = pl.multiple_of(ids_ref[n] * length, length)
        target = order_ref[:, pl.ds(at, length)]
        hot = lax.broadcasted_iota(jnp.int32, (rows, length), 0) + base == target
        hot = jnp.where(hot, 1.0, 0.0).astype(BF16)
        columns = jnp.concatenate([part[b] for b in range(per)], axis=1)
        term = lax.dot_general(
            hot, columns, (((1,), (1,)), ((), ())), preferred_element_type=F32
        )
        acc = term if acc is None else acc + term
    out_ref[...] = acc.astype(out_ref.dtype)


def restore(ids, order_row, parts, start, dtype):
    panel = order_row.shape[1]
    width = parts[0].shape[1]
    rows = 512
    row_spec = pl.BlockSpec((rows, width), lambda i, ids: (i, 0))
    extra = () if start is None else (start,)
    return pl.pallas_call(
        functools.partial(restore_body, count=len(parts)),
        out_shape=jax.ShapeDtypeStruct((panel, width), dtype),
        grid_spec=pltpu.PrefetchScalarGridSpec(
            num_scalar_prefetch=1,
            grid=(panel // rows,),
            in_specs=[whole_spec(order_row)]
            + [whole_spec(p) for p in parts]
            + [row_spec for _ in extra],
            out_specs=row_spec,
        ),
        compiler_params=params(24),
        cost_estimate=cost(2 * panel * panel * width, 4 * panel * width),
        name="restore",
    )(ids, order_row, *parts, *extra)


def tree_sum(terms):
    while len(terms) > 1:
        terms = [terms[i] + terms[i + 1] for i in range(0, len(terms), 2)]
    return terms[0]


def shards(features, order, tiles, tile_rows, tile_cols, live, weight, cotangent):
    reps = lax.axis_size("rep")
    sections = lax.axis_size("section")
    rep = lax.axis_index("rep")
    section = lax.axis_index("section")
    panel, width = features.shape
    rounds, slots, block, _ = tiles.shape[2:]
    blocks = panel // block
    chips = sections // 2
    pairs = rounds // 2
    near = reps // 2
    chip, core = section // 2, section % 2

    def over_chips(x, d):
        return lax.ppermute(x, "section", [(s, s ^ (2 * d)) for s in range(sections)])

    def over_cores(x):
        return lax.ppermute(x, "section", [(s, s ^ 1) for s in range(sections)])

    def over_reps(x, d):
        return lax.ppermute(x, "rep", [(r, r ^ d) for r in range(reps)])

    def from_owner(x, d):
        moves = []
        for r in range(reps):
            for j in range(rounds):
                source = j * reps + r
                target = (source ^ (2 * d)) ^ ((d // near) & 1)
                moves.append((source * reps + r, target * reps + r))
        return lax.ppermute(x, ("section", "rep"), moves)

    order_col = order.reshape(panel, 1)
    owns = [reorder(order_col, features, h, HALVES) for h in range(HALVES)]
    gots = [[own] + [from_owner(own, d) for d in range(1, chips)] for own in owns]
    side = core ^ (rep % 2)
    low = (chip % near) ^ (rep // 2)
    rows_in, cols_in, live_in, _ = lax.optimization_barrier(
        (tile_rows, tile_cols, live, owns[-1])
    )
    place = jnp.stack([rep, chip, core, side, chip // near, low])
    entries = (rows_in << (blocks - 1).bit_length()) | cols_in
    meta = jnp.concatenate([place, live_in.reshape(-1), entries.reshape(-1)]).astype(jnp.int32)
    own_tiles = tiles.reshape(rounds * slots, block, block)

    mine, mate = [], []
    for p in range(pairs):
        for h in range(HALVES):
            picked = pick(meta, gots[h][2 * p * near : 2 * (p + 1) * near], near)
            mine.append(picked)
            mate.append(over_cores(picked))

    started = forward(meta, own_tiles, rounds, mine, None, reps)
    own, *others = forward(meta, own_tiles, rounds, mate, started, reps)
    sent = {d: over_reps(others[d - 1], d) for d in reversed(range(1, reps))}
    aggregated = total_of(meta, own, [sent[d] for d in range(1, reps)])
    shares = [aggregated] + [over_reps(aggregated, d) for d in range(1, reps)]

    cut = reps // 2
    ups = [
        up_shares(meta, weight, cotangent, shares[:cut], 0),
        up_shares(meta, weight, cotangent, shares[cut:], cut),
    ]
    given = over_cores(backward(meta, own_tiles, rounds, ups, pairs, chips, False))
    kept = backward(meta, own_tiles, rounds, ups, pairs, chips, True)
    hidden, grad_part = finish(meta, weight, cotangent, shares, kept)
    chunks = [kept[d] + given[d].astype(F32) for d in range(chips)]
    arrived = [over_chips(chunks[d].astype(BF16), d).astype(F32) for d in range(1, chips)]
    reduced = tree_sum([chunks[0]] + arrived).astype(BF16)

    grad_part = grad_part + over_cores(grad_part)
    weight_grad = tree_sum([grad_part] + [over_chips(grad_part, d) for d in range(1, chips)])
    weight_grad = weight_grad * (1.0 / math.sqrt(panel * sections))

    spread = [reduced] + [over_reps(reduced, d) for d in range(1, reps)]
    routed = route(meta, spread, chips)

    def to_owner(k):
        moves = []
        for s in range(sections):
            u = (s // 2) ^ k
            moves.append((s, (2 * (u // reps) + s % 2) * reps + u % reps))
        return lax.ppermute(routed[k], "section", moves)

    parts = [to_owner(k) for k in range(chips)]
    mine_u = (section // reps // 2) * reps + section % reps
    part_ids = jnp.stack([mine_u ^ k for k in range(chips)]).astype(jnp.int32)
    order_row = order.reshape(1, panel)
    cut = chips // 2
    begun = restore(part_ids[:cut], order_row, parts[:cut], None, F32)
    feature_grad = restore(part_ids[cut:], order_row, parts[cut:], begun, BF16)
    return (hidden, weight_grad, feature_grad)


def solution(mesh):
    placed = (
        P("section", None),
        P("section"),
        P("section", "rep", None, None, None, None),
        P("section", "rep", None, None),
        P("section", "rep", None, None),
        P("section", "rep", None),
        P(),
        P("section", None),
    )
    return jax.shard_map(
        shards,
        mesh=mesh,
        in_specs=placed,
        out_specs=(P("section", None), P(), P("section", None)),
        check_vma=False,
    )
```

```python
import functools
import math

import jax
import jax.numpy as jnp
from jax import lax
from jax.experimental import pallas as pl
from jax.experimental.pallas import tpu as pltpu
from jax.sharding import PartitionSpec as P

F32 = jnp.float32
BF16 = jnp.bfloat16
MIB = 1 << 20


def params(mib):
    return pltpu.CompilerParams(vmem_limit_bytes=mib * MIB)


def cost(flops, nbytes):
    return pl.CostEstimate(flops=int(flops), bytes_accessed=int(nbytes), transcendentals=0)


def whole_spec(array):
    zeros = (0,) * array.ndim
    return pl.BlockSpec(array.shape, lambda *_: zeros)


HALVES = 2
GROUP = 16


class Place:
    def __init__(self):
        reps = lax.axis_size("rep")
        section = lax.axis_index("section")
        self.rep = lax.axis_index("rep")
        self.chip = section // 2
        self.core = section % 2
        self.side = (section + self.rep) % 2
        self.row = section // reps
        self.low = ((section % reps) // 2) ^ (self.rep // 2)


def in_vmem(array):
    return pltpu.with_memory_space_constraint(array, pltpu.VMEM)


def call(body, operands, outs, scalars=(), scratch=(), vmem=(), mib=12, estimate=None, name=None):
    specs = [
        pl.BlockSpec(memory_space=pltpu.VMEM) if n in vmem else whole_spec(x)
        for n, x in enumerate(operands)
    ]
    operands = [in_vmem(x) if n in vmem else x for n, x in enumerate(operands)]
    return pl.pallas_call(
        body,
        out_shape=outs,
        grid_spec=pltpu.PrefetchScalarGridSpec(
            num_scalar_prefetch=len(scalars),
            grid=(1,),
            in_specs=specs,
            out_specs=jax.tree.map(whole_spec, outs),
            scratch_shapes=list(scratch),
        ),
        compiler_params=params(mib),
        cost_estimate=estimate or cost(0, MIB),
        name=name,
    )(*scalars, *operands)


def like(array, dtype=None):
    return jax.ShapeDtypeStruct(array.shape, dtype or array.dtype)


def reorder_body(order_ref, feat_ref, *outs):
    panel = feat_ref.shape[0]
    rows = outs[0].shape[0]
    step = min(256, rows)
    for i in range(panel // step):
        hot = lax.broadcasted_iota(jnp.int32, (step, panel), 1) == order_ref[pl.ds(i * step, step), :]
        hot = jnp.where(hot, 1.0, 0.0).astype(BF16)
        at = i * step % rows
        outs[i * step // rows][at : at + step, :] = jnp.dot(
            hot, feat_ref[...], preferred_element_type=F32
        ).astype(BF16)


def reorder(order_col, features):
    panel, width = features.shape
    outs = [jax.ShapeDtypeStruct((panel // HALVES, width), BF16)] * HALVES
    return call(
        reorder_body,
        [order_col, features],
        outs,
        estimate=cost(2 * panel * panel * width, 4 * panel * width),
        name="reorder",
    )


def entry_body(rows_ref, cols_ref, _, out_ref, *, bits):
    out_ref[...] = (rows_ref[0, 0] << bits) | cols_ref[0, 0]


def entries_of(rows, cols, bits, after):
    out = jax.ShapeDtypeStruct(rows.shape[2:], jnp.int32)
    return call(
        functools.partial(entry_body, bits=bits), [rows, cols, after], out, name="entries_of"
    )


def pick_body(*refs, near):
    options, out_ref = refs[:-1], refs[-1]
    place = Place()
    for n, option in enumerate(options):

        @pl.when((place.side == n // near) & (place.low == n % near))
        def _():
            out_ref[...] = option[...]


def pick(options, near):
    return call(functools.partial(pick_body, near=near), options, like(options[0]), name="pick")


def walk(live_ref, entry_ref, j, slots, step):
    count = live_ref[j]

    @pl.loop(0, (count + GROUP - 1) // GROUP)
    def _(g):
        entries = [entry_ref[j, g * GROUP + t] for t in range(GROUP)]
        alive = [g * GROUP + t < count for t in range(GROUP)]
        step(j * slots + g * GROUP, entries, alive)


def forward_body(live_ref, entry_ref, tiles_ref, *refs, slots, pairs, last):
    place = Place()
    xs, rest = refs[: pairs * HALVES], refs[pairs * HALVES :]
    panel_ref, acc = rest[-2:]
    blocks, block, width = panel_ref.shape
    bits = (blocks - 1).bit_length()
    if last:
        start, outs = rest[0], rest[1:-2]
        acc[pl.ds(0, blocks)] = start[...]
        acc[blocks] = jnp.zeros((block, width), F32)
    else:
        outs = rest[:-2]
        acc[...] = jnp.zeros_like(acc)
    per = blocks // HALVES
    for p in range(pairs):
        for h in range(HALVES):
            panel_ref[h * per : (h + 1) * per] = xs[p * HALVES + h][...].reshape(per, block, width)

        def step(first, entries, alive):
            terms = []
            for t in range(GROUP):
                x = panel_ref[entries[t] & (blocks - 1)]
                terms.append(jnp.dot(tiles_ref[first + t], x, preferred_element_type=F32))
            for t in range(GROUP):
                acc[jnp.where(alive[t], entries[t] >> bits, blocks)] += terms[t]

        j = place.row ^ (2 * p + (1 - place.side if last else place.side))
        walk(live_ref, entry_ref, j, slots, step)
    if last:
        span = blocks // len(outs)
        for d, out in enumerate(outs):
            at = (place.rep ^ d) * span
            out[...] = acc[pl.ds(at, span)].reshape(out.shape).astype(out.dtype)
    else:
        outs[0][...] = acc[pl.ds(0, blocks)]


def forward(plan, tiles, xs, start, reps):
    block = tiles.shape[1]
    width = xs[0].shape[1]
    pairs = len(xs) // HALVES
    blocks = xs[0].shape[0] * HALVES // block
    last = start is not None
    if last:
        rows = blocks * block // reps
        outs = [jax.ShapeDtypeStruct((rows, width), BF16 if d else F32) for d in range(reps)]
    else:
        outs = [jax.ShapeDtypeStruct((blocks, block, width), F32)]
    body = functools.partial(
        forward_body, slots=plan[1].shape[1], pairs=pairs, last=last
    )
    got = call(
        body,
        [tiles, *xs] + ([start] if last else []),
        outs,
        scalars=plan,
        scratch=[pltpu.VMEM((blocks, block, width), BF16), pltpu.VMEM((blocks + 1, block, width), F32)],
        vmem=(0,),
        estimate=cost(2 * 64 * block * block * width, 12 * MIB),
        name="forward",
    )
    return got if last else got[0]


def total_body(own_ref, *refs):
    total = own_ref[...]
    for ref in refs[:-1]:
        total = total + ref[...].astype(F32)
    refs[-1][...] = total.astype(BF16)


def total_of(own, others):
    return call(total_body, [own, *others], like(own, BF16), name="total_of")


def gradient_of(agg, co, weight):
    pre = jnp.dot(agg, weight, preferred_element_type=F32)
    gate = 1.0 / (1.0 + jnp.exp(-pre))
    grad_pre = (co.astype(F32) * gate * (1.0 + pre * (1.0 - gate))).astype(BF16)
    return pre, gate, grad_pre


def up_body(w_ref, co_ref, *refs, first):
    place = Place()
    shares, out_ref = refs[:-1], refs[-1]
    weight = w_ref[...]
    rows = shares[0].shape[0]
    for n, share in enumerate(shares):
        at = pl.multiple_of((place.rep ^ (first + n)) * rows, rows)
        _, _, grad_pre = gradient_of(share[...], co_ref[pl.ds(at, rows), :], weight)
        out_ref[n] = lax.dot_general(
            weight, grad_pre, (((1,), (1,)), ((), ())), preferred_element_type=F32
        ).astype(BF16)


def up_shares(weight, cotangent, shares, first):
    rows, width = shares[0].shape
    out = jax.ShapeDtypeStruct((len(shares), width, rows), BF16)
    return call(
        functools.partial(up_body, first=first),
        [weight, cotangent, *shares],
        out,
        estimate=cost(4 * len(shares) * rows * width * width, 2 * MIB),
        name="up_shares",
    )


def finish_body(w_ref, co_ref, *refs):
    place = Place()
    shares, (hidden_ref, grad_ref, agg_all, pre_all) = refs[:-4], refs[-4:]
    weight = w_ref[...]
    rows = shares[0].shape[0]
    for n, share in enumerate(shares):
        at = pl.multiple_of((place.rep ^ n) * rows, rows)
        agg = share[...]
        pre, gate, grad_pre = gradient_of(agg, co_ref[pl.ds(at, rows), :], weight)
        hidden_ref[pl.ds(at, rows), :] = (pre * gate).astype(BF16)
        agg_all[pl.ds(at, rows), :] = agg
        pre_all[pl.ds(at, rows), :] = grad_pre
    grad_ref[...] = lax.dot_general(
        agg_all[...], pre_all[...], (((0,), (0,)), ((), ())), preferred_element_type=F32
    )


def finish(weight, cotangent, shares):
    panel, width = cotangent.shape
    outs = (like(cotangent), jax.ShapeDtypeStruct((width, width), F32))
    return call(
        finish_body,
        [weight, cotangent, *shares],
        outs,
        scratch=[pltpu.VMEM((panel, width), BF16)] * 2,
        estimate=cost(6 * panel * width * width, 8 * panel * width),
        name="finish",
    )


def backward_body(live_ref, entry_ref, tiles_ref, *refs, slots, keep):
    ups, (out_ref, up_all, acc) = refs[:-3], refs[-3:]
    place = Place()
    cuts, chips, pairs, per, width, block = out_ref.shape
    blocks = cuts * chips * per
    bits = (blocks - 1).bit_length()
    count, _, rows = ups[0].shape
    for m, up in enumerate(ups):
        for n in range(count):
            at = pl.multiple_of((place.rep ^ (m * count + n)) * rows, rows)
            up_all[:, pl.ds(at, rows)] = up[n]
    for p in range(pairs):
        acc[...] = jnp.zeros_like(acc)

        def step(first, entries, alive):
            terms = []
            for t in range(GROUP):
                at = pl.multiple_of((entries[t] >> bits) * block, block)
                terms.append(
                    jnp.dot(
                        up_all[:, pl.ds(at, block)],
                        tiles_ref[first + t],
                        preferred_element_type=F32,
                    )
                )
            for t in range(GROUP):
                acc[jnp.where(alive[t], entries[t] & (blocks - 1), blocks)] += terms[t]

        core = place.core
        walk(live_ref, entry_ref, 2 * p + (core if keep else 1 - core), slots, step)
        for h in range(cuts):
            for d in range(chips):
                at = ((place.chip ^ d) * cuts + h) * per
                out_ref[h, d, p] = acc[pl.ds(at, per)].astype(out_ref.dtype)


def backward(plan, tiles, ups, pairs, chips, cuts, keep):
    block = tiles.shape[1]
    count, width, rows = ups[0].shape
    panel = len(ups) * count * rows
    blocks = panel // block
    shape = (cuts, chips, pairs, blocks // chips // cuts, width, block)
    return call(
        functools.partial(backward_body, slots=plan[1].shape[1], keep=keep),
        [tiles, *ups],
        jax.ShapeDtypeStruct(shape, F32 if keep else BF16),
        scalars=plan,
        scratch=[pltpu.VMEM((width, panel), BF16), pltpu.VMEM((blocks + 1, width, block), F32)],
        vmem=(0,),
        estimate=cost(2 * 64 * block * block * width, 12 * MIB),
        name="backward",
    )


def join_body(kept_ref, given_ref, *outs):
    cuts, chips = kept_ref.shape[:2]
    for h in range(cuts):
        for d in range(chips):
            out = outs[h * chips + d]
            out[...] = (kept_ref[h, d] + given_ref[h, d].astype(F32)).astype(out.dtype)


def join(kept, given):
    cuts, chips = kept.shape[:2]
    outs = [
        jax.ShapeDtypeStruct(kept.shape[2:], BF16 if d else F32)
        for _ in range(cuts)
        for d in range(chips)
    ]
    got = call(join_body, [kept, given], outs, name="join")
    return [got[h * chips : (h + 1) * chips] for h in range(cuts)]


def gather_body(*refs, count):
    terms = [ref[...].astype(F32) for ref in refs[:count]]
    refs[-1][...] = tree_sum(terms).astype(BF16)


def gather_sum(terms, after):
    return call(
        functools.partial(gather_body, count=len(terms)),
        [*terms, *after],
        like(terms[0], BF16),
        name="gather_sum",
    )


def route_body(*refs, reps, chips):
    spread, outs = refs[:reps], refs[reps:]
    place = Place()
    for k in range(chips):
        u = place.chip ^ k
        for d in range(reps):

            @pl.when(((u % reps) ^ place.rep) == d)
            def _():
                outs[k][...] = spread[d][u // reps]


def route(spread, chips):
    outs = [jax.ShapeDtypeStruct(spread[0].shape[1:], BF16)] * chips
    body = functools.partial(route_body, reps=len(spread), chips=chips)
    return call(body, spread, outs, name="route")


def restore_body(ids_ref, order_ref, *refs, count):
    parts, out_ref = refs[:count], refs[-1]
    rows = out_ref.shape[0]
    per, _, block = parts[0].shape
    base = pl.program_id(0) * rows
    acc = refs[count][...] if len(refs) > count + 1 else None
    for n, part in enumerate(parts):
        length = per * block
        at = pl.multiple_of(ids_ref[n] * length, length)
        target = order_ref[:, pl.ds(at, length)]
        hot = lax.broadcasted_iota(jnp.int32, (rows, length), 0) + base == target
        hot = jnp.where(hot, 1.0, 0.0).astype(BF16)
        columns = jnp.concatenate([part[b] for b in range(per)], axis=1)
        term = lax.dot_general(
            hot, columns, (((1,), (1,)), ((), ())), preferred_element_type=F32
        )
        acc = term if acc is None else acc + term
    out_ref[...] = acc.astype(out_ref.dtype)


def restore(ids, order_row, parts, start, dtype):
    panel = order_row.shape[1]
    width = parts[0].shape[1]
    rows = 512
    row_spec = pl.BlockSpec((rows, width), lambda i, ids: (i, 0))
    extra = () if start is None else (start,)
    return pl.pallas_call(
        functools.partial(restore_body, count=len(parts)),
        out_shape=jax.ShapeDtypeStruct((panel, width), dtype),
        grid_spec=pltpu.PrefetchScalarGridSpec(
            num_scalar_prefetch=1,
            grid=(panel // rows,),
            in_specs=[whole_spec(order_row)]
            + [whole_spec(p) for p in parts]
            + [row_spec for _ in extra],
            out_specs=row_spec,
        ),
        compiler_params=params(24),
        cost_estimate=cost(2 * panel * panel * width, 4 * panel * width),
        name="restore",
    )(ids, order_row, *parts, *extra)


def tree_sum(terms):
    while len(terms) > 1:
        terms = [terms[i] + terms[i + 1] for i in range(0, len(terms), 2)]
    return terms[0]


def shards(features, order, tiles, tile_rows, tile_cols, live, weight, cotangent):
    reps = lax.axis_size("rep")
    sections = lax.axis_size("section")
    section = lax.axis_index("section")
    panel, width = features.shape
    rounds, slots, block, _ = tiles.shape[2:]
    blocks = panel // block
    chips = sections // 2
    pairs = rounds // 2
    near = reps // 2

    def over_chips(x, d):
        return lax.ppermute(x, "section", [(s, s ^ (2 * d)) for s in range(sections)])

    def over_cores(x):
        return lax.ppermute(x, "section", [(s, s ^ 1) for s in range(sections)])

    def over_reps(x, d):
        return lax.ppermute(x, "rep", [(r, r ^ d) for r in range(reps)])

    def from_owner(x, d):
        moves = []
        for r in range(reps):
            for j in range(rounds):
                source = j * reps + r
                target = (source ^ (2 * d)) ^ ((d // near) & 1)
                moves.append((source * reps + r, target * reps + r))
        return lax.ppermute(x, ("section", "rep"), moves)

    order_col = order.reshape(panel, 1)
    owns = reorder(order_col, features)
    gots = [[own] + [from_owner(own, d) for d in range(1, chips)] for own in owns]
    bits = (blocks - 1).bit_length()
    plan = (live.reshape(rounds), entries_of(tile_rows, tile_cols, bits, owns[-1][:16]))
    own_tiles = tiles.reshape(rounds * slots, block, block)

    mine, mate = [], []
    for p in range(pairs):
        for h in range(HALVES):
            picked = pick(gots[h][2 * p * near : 2 * (p + 1) * near], near)
            mine.append(picked)
            mate.append(over_cores(picked))

    started = forward(plan, own_tiles, mine, None, reps)
    own, *others = forward(plan, own_tiles, mate, started, reps)
    sent = {d: over_reps(others[d - 1], d) for d in reversed(range(1, reps))}
    aggregated = total_of(own, [sent[d] for d in range(1, reps)])
    shares = [aggregated] + [over_reps(aggregated, d) for d in range(1, reps)]

    ups = [
        up_shares(weight, cotangent, shares[:near], 0),
        up_shares(weight, cotangent, shares[near:], near),
    ]
    cuts = math.gcd(2, blocks // chips)
    given = over_cores(backward(plan, own_tiles, ups, pairs, chips, cuts, False))
    kept = backward(plan, own_tiles, ups, pairs, chips, cuts, True)
    chunks = join(kept, given)
    arrived = [[over_chips(c[d], d) for d in range(1, chips)] for c in chunks]
    late_shares = lax.optimization_barrier((shares, chunks[-1][-1]))[0]
    hidden, grad_part = finish(weight, cotangent, late_shares)
    reduced = [
        gather_sum([c[0], *a], [grad_part] if h == 0 else [])
        for h, (c, a) in enumerate(zip(chunks, arrived, strict=True))
    ]

    def to_owner(block, k):
        moves = []
        for s in range(sections):
            u = (s // 2) ^ k
            moves.append((s, (2 * (u // reps) + s % 2) * reps + u % reps))
        return lax.ppermute(block, "section", moves)

    mine_u = (section // reps // 2) * reps + section % reps
    order_row = order.reshape(1, panel)
    feature_grad = None
    for h in range(cuts):
        spread = [reduced[h]] + [over_reps(reduced[h], d) for d in range(1, reps)]
        parts = [to_owner(block, k) for k, block in enumerate(route(spread, chips))]
        ids = jnp.stack([(mine_u ^ k) * cuts + h for k in range(chips)]).astype(jnp.int32)
        kind = BF16 if h == cuts - 1 else F32
        feature_grad = restore(ids, order_row, parts, feature_grad, kind)

    grad_part = grad_part + over_cores(grad_part)
    weight_grad = tree_sum([grad_part] + [over_chips(grad_part, d) for d in range(1, chips)])
    weight_grad = weight_grad * (1.0 / math.sqrt(panel * sections))
    return (hidden, weight_grad, feature_grad)


def solution(mesh):
    placed = (
        P("section", None),
        P("section"),
        P("section", "rep", None, None, None, None),
        P("section", "rep", None, None),
        P("section", "rep", None, None),
        P("section", "rep", None),
        P(),
        P("section", None),
    )
    return jax.shard_map(
        shards,
        mesh=mesh,
        in_specs=placed,
        out_specs=(P("section", None), P(), P("section", None)),
        check_vma=False,
    )
```

```python
import functools
import math

import jax
import jax.numpy as jnp
from jax import lax
from jax.experimental import pallas as pl
from jax.experimental.pallas import tpu as pltpu
from jax.sharding import PartitionSpec as P

F32 = jnp.float32
BF16 = jnp.bfloat16
MIB = 1 << 20


def params(mib):
    return pltpu.CompilerParams(vmem_limit_bytes=mib * MIB)


def cost(flops, nbytes):
    return pl.CostEstimate(flops=int(flops), bytes_accessed=int(nbytes), transcendentals=0)


def whole_spec(array):
    zeros = (0,) * array.ndim
    return pl.BlockSpec(array.shape, lambda *_: zeros)


HALVES = 2
GROUP = 16


class Place:
    def __init__(self):
        reps = lax.axis_size("rep")
        section = lax.axis_index("section")
        self.rep = lax.axis_index("rep")
        self.chip = section // 2
        self.core = section % 2
        self.side = (section + self.rep) % 2
        self.row = section // reps
        self.low = ((section % reps) // 2) ^ (self.rep // 2)


def in_vmem(array):
    return pltpu.with_memory_space_constraint(array, pltpu.VMEM)


def call(body, operands, outs, scalars=(), scratch=(), vmem=(), mib=12, estimate=None, name=None):
    specs = [
        pl.BlockSpec(memory_space=pltpu.VMEM) if n in vmem else whole_spec(x)
        for n, x in enumerate(operands)
    ]
    operands = [in_vmem(x) if n in vmem else x for n, x in enumerate(operands)]
    return pl.pallas_call(
        body,
        out_shape=outs,
        grid_spec=pltpu.PrefetchScalarGridSpec(
            num_scalar_prefetch=len(scalars),
            grid=(1,),
            in_specs=specs,
            out_specs=jax.tree.map(whole_spec, outs),
            scratch_shapes=list(scratch),
        ),
        compiler_params=params(mib),
        cost_estimate=estimate or cost(0, MIB),
        name=name,
    )(*scalars, *operands)


def like(array, dtype=None):
    return jax.ShapeDtypeStruct(array.shape, dtype or array.dtype)


def reorder_body(order_ref, feat_ref, *outs):
    panel = feat_ref.shape[0]
    order = jnp.broadcast_to(order_ref[...], (8, panel)).T
    rows = outs[0].shape[0]
    step = min(256, rows)
    for i in range(panel // step):
        hot = lax.broadcasted_iota(jnp.int32, (step, panel), 1) == order[i * step : (i + 1) * step, :1]
        hot = jnp.where(hot, 1.0, 0.0).astype(BF16)
        at = i * step % rows
        outs[i * step // rows][at : at + step, :] = jnp.dot(
            hot, feat_ref[...], preferred_element_type=F32
        ).astype(BF16)


def reorder(order_row, features):
    panel, width = features.shape
    outs = [jax.ShapeDtypeStruct((panel // HALVES, width), BF16)] * HALVES
    return call(
        reorder_body,
        [order_row, features],
        outs,
        estimate=cost(2 * panel * panel * width, 4 * panel * width),
        name="reorder",
    )


def entry_body(rows_ref, cols_ref, _, out_ref, *, bits):
    out_ref[...] = (rows_ref[0, 0] << bits) | cols_ref[0, 0]


def entries_of(rows, cols, bits, after):
    out = jax.ShapeDtypeStruct(rows.shape[2:], jnp.int32)
    return call(
        functools.partial(entry_body, bits=bits), [rows, cols, after], out, name="entries_of"
    )


def pick_body(*refs, near):
    options, out_ref = refs[:-1], refs[-1]
    place = Place()
    for n, option in enumerate(options):

        @pl.when((place.side == n // near) & (place.low == n % near))
        def _():
            out_ref[...] = option[...]


def pick(options, near):
    return call(functools.partial(pick_body, near=near), options, like(options[0]), name="pick")


def walk(live_ref, entry_ref, j, slots, step):
    count = live_ref[j]

    @pl.loop(0, (count + GROUP - 1) // GROUP)
    def _(g):
        entries = [entry_ref[j, g * GROUP + t] for t in range(GROUP)]
        alive = [g * GROUP + t < count for t in range(GROUP)]
        step(j * slots + g * GROUP, entries, alive)


def forward_body(live_ref, entry_ref, tiles_ref, *refs, slots, pairs, last):
    place = Place()
    xs, rest = refs[: pairs * HALVES], refs[pairs * HALVES :]
    panel_ref, acc = rest[-2:]
    blocks, block, width = panel_ref.shape
    bits = (blocks - 1).bit_length()
    if last:
        start, outs = rest[0], rest[1:-2]
        acc[pl.ds(0, blocks)] = start[...]
        acc[blocks] = jnp.zeros((block, width), F32)
    else:
        outs = rest[:-2]
        acc[...] = jnp.zeros_like(acc)
    per = blocks // HALVES
    for p in range(pairs):
        for h in range(HALVES):
            panel_ref[h * per : (h + 1) * per] = xs[p * HALVES + h][...].reshape(per, block, width)

        def step(first, entries, alive):
            terms = []
            for t in range(GROUP):
                x = panel_ref[entries[t] & (blocks - 1)]
                terms.append(jnp.dot(tiles_ref[first + t], x, preferred_element_type=F32))
            for t in range(GROUP):
                acc[jnp.where(alive[t], entries[t] >> bits, blocks)] += terms[t]

        j = place.row ^ (2 * p + (1 - place.side if last else place.side))
        walk(live_ref, entry_ref, j, slots, step)
    if last:
        span = blocks // len(outs)
        for d, out in enumerate(outs):
            at = (place.rep ^ d) * span
            out[...] = acc[pl.ds(at, span)].reshape(out.shape).astype(out.dtype)
    else:
        outs[0][...] = acc[pl.ds(0, blocks)]


def forward(plan, tiles, xs, start, reps):
    block = tiles.shape[1]
    width = xs[0].shape[1]
    pairs = len(xs) // HALVES
    blocks = xs[0].shape[0] * HALVES // block
    last = start is not None
    if last:
        rows = blocks * block // reps
        outs = [jax.ShapeDtypeStruct((rows, width), BF16 if d else F32) for d in range(reps)]
    else:
        outs = [jax.ShapeDtypeStruct((blocks, block, width), F32)]
    body = functools.partial(
        forward_body, slots=plan[1].shape[1], pairs=pairs, last=last
    )
    got = call(
        body,
        [tiles, *xs] + ([start] if last else []),
        outs,
        scalars=plan,
        scratch=[pltpu.VMEM((blocks, block, width), BF16), pltpu.VMEM((blocks + 1, block, width), F32)],
        vmem=(0,),
        estimate=cost(2 * 64 * block * block * width, 12 * MIB),
        name="forward",
    )
    return got if last else got[0]


def total_body(own_ref, *refs):
    total = own_ref[...]
    for ref in refs[:-1]:
        total = total + ref[...].astype(F32)
    refs[-1][...] = total.astype(BF16)


def total_of(own, others):
    return call(total_body, [own, *others], like(own, BF16), name="total_of")


def gradient_of(agg, co, weight):
    pre = jnp.dot(agg, weight, preferred_element_type=F32)
    gate = 1.0 / (1.0 + jnp.exp(-pre))
    grad_pre = (co.astype(F32) * gate * (1.0 + pre * (1.0 - gate))).astype(BF16)
    return pre, gate, grad_pre


def two_parts(value):
    high = value.astype(BF16)
    return high, (value - high.astype(F32)).astype(BF16)


def sum_of_parts(ref, at, rows):
    return ref[at : at + rows, :].astype(F32) + ref[at + rows : at + 2 * rows, :].astype(F32)


def up_body(w_ref, co_ref, *refs, first, count):
    place = Place()
    shares, out_ref = refs[:count], refs[count]
    weight = w_ref[...]
    rows = shares[0].shape[0]
    for n, share in enumerate(shares):
        at = pl.multiple_of((place.rep ^ (first + n)) * rows, rows)
        _, _, grad_pre = gradient_of(share[...], co_ref[pl.ds(at, rows), :], weight)
        if first + n == 0:
            grad = lax.dot_general(
                share[...], grad_pre, (((0,), (0,)), ((), ())), preferred_element_type=F32
            )
            width = grad.shape[0]
            refs[count + 1][:width, :], refs[count + 1][width:, :] = two_parts(grad)
        out_ref[n] = lax.dot_general(
            weight, grad_pre, (((1,), (1,)), ((), ())), preferred_element_type=F32
        ).astype(BF16)


def up_shares(weight, cotangent, shares, first):
    rows, width = shares[0].shape
    outs = [jax.ShapeDtypeStruct((len(shares), width, rows), BF16)]
    if first == 0:
        outs.append(jax.ShapeDtypeStruct((2 * width, width), BF16))
    return call(
        functools.partial(up_body, first=first, count=len(shares)),
        [weight, cotangent, *shares],
        outs,
        estimate=cost(4 * len(shares) * rows * width * width, 2 * MIB),
        name="up_shares",
    )


def finish_body(w_ref, *refs):
    place = Place()
    shares, (hidden_ref, token_ref) = refs[:-2], refs[-2:]
    rows = shares[0].shape[0]
    for n, share in enumerate(shares):
        at = pl.multiple_of((place.rep ^ n) * rows, rows)
        pre = jnp.dot(share[...], w_ref[...], preferred_element_type=F32)
        hidden_ref[pl.ds(at, rows), :] = (pre * (1.0 / (1.0 + jnp.exp(-pre)))).astype(BF16)
    token_ref[...] = jnp.zeros_like(token_ref)


def finish(weight, shares):
    rows, width = shares[0].shape
    outs = (
        jax.ShapeDtypeStruct((rows * len(shares), width), BF16),
        jax.ShapeDtypeStruct((8, 128), jnp.int32),
    )
    return call(finish_body, [weight, *shares], outs, estimate=cost(0, 4 * MIB), name="finish")


def backward_body(live_ref, entry_ref, tiles_ref, *refs, slots, keep, shape):
    refs, (out_ref, up_all, acc) = refs[:-3], refs[-3:]
    ups = refs if keep else refs[:-1]
    place = Place()
    cuts, chips, pairs, per, width, block = shape
    blocks = cuts * chips * per
    bits = (blocks - 1).bit_length()
    count, _, rows = ups[0].shape
    for m, up in enumerate(ups):
        for n in range(count):
            at = pl.multiple_of((place.rep ^ (m * count + n)) * rows, rows)
            up_all[:, pl.ds(at, rows)] = up[n]
    for p in range(pairs):
        acc[...] = jnp.zeros_like(acc)

        def step(first, entries, alive):
            terms = []
            for t in range(GROUP):
                at = pl.multiple_of((entries[t] >> bits) * block, block)
                terms.append(
                    jnp.dot(
                        up_all[:, pl.ds(at, block)],
                        tiles_ref[first + t],
                        preferred_element_type=F32,
                    )
                )
            for t in range(GROUP):
                acc[jnp.where(alive[t], entries[t] & (blocks - 1), blocks)] += terms[t]

        core = place.core
        walk(live_ref, entry_ref, 2 * p + (core if keep else 1 - core), slots, step)
        for h in range(cuts):
            for d in range(chips):
                at = ((place.chip ^ d) * cuts + h) * per
                to = ((h * chips + d) * pairs + p) * per
                out_ref[to : to + per] = acc[pl.ds(at, per)].astype(out_ref.dtype)
    if not keep:
        for n in range(2):
            out_ref[pairs * blocks + n] = refs[-1][n * width : (n + 1) * width, :]


def backward(plan, tiles, ups, pairs, chips, cuts, term=None):
    block = tiles.shape[1]
    count, width, rows = ups[0].shape
    panel = len(ups) * count * rows
    blocks = panel // block
    shape = (cuts, chips, pairs, blocks // chips // cuts, width, block)
    keep = term is None
    out_shape = (pairs * blocks + (0 if keep else 2), width, block)
    return call(
        functools.partial(backward_body, slots=plan[1].shape[1], keep=keep, shape=shape),
        [tiles, *ups] + ([] if keep else [term]),
        jax.ShapeDtypeStruct(out_shape, F32 if keep else BF16),
        scalars=plan,
        scratch=[pltpu.VMEM((width, panel), BF16), pltpu.VMEM((blocks + 1, width, block), F32)],
        vmem=(0,),
        estimate=cost(2 * 64 * block * block * width, 12 * MIB),
        name="backward",
    )


def join_body(kept_ref, given_ref, term_ref, *refs, cuts, chips):
    outs, grad = refs[:-1], refs[-1]
    place = Place()
    width = grad.shape[0]
    blocks = kept_ref.shape[0]
    mate = given_ref[blocks].astype(F32) + given_ref[blocks + 1].astype(F32)
    grad[...] = sum_of_parts(term_ref, 0, width) + mate
    per = blocks // (cuts * chips)
    for h in range(cuts):
        for d in range(chips):
            out = outs[h * chips + d]
            for b in range(per):
                n = (h * chips + d) * per + b
                out[b * width : (b + 1) * width, :] = (
                    kept_ref[n] + given_ref[n].astype(F32)
                ).astype(out.dtype)
            if h == 0:
                rows, end = width // chips, per * width
                high, low = two_parts(grad[pl.ds((place.chip ^ d) * rows, rows), :])
                if d == 0:
                    out[end : end + rows, :] = high.astype(F32) + low.astype(F32)
                else:
                    out[end : end + rows, :] = high
                    out[end + rows : end + 2 * rows, :] = low


def join(kept, given, term, cuts, chips):
    blocks, width, block = kept.shape
    rows = blocks // (cuts * chips) * width
    extra = width // chips
    outs = [
        jax.ShapeDtypeStruct(
            (rows + (0 if h else 2 * extra if d else extra), block), BF16 if d else F32
        )
        for h in range(cuts)
        for d in range(chips)
    ]
    got = call(
        functools.partial(join_body, cuts=cuts, chips=chips),
        [kept, given, term],
        outs,
        scratch=[pltpu.VMEM((width, width), F32)],
        name="join",
    )
    return [got[h * chips : (h + 1) * chips] for h in range(cuts)]


def gather_body(*refs, count, rows):
    out_ref = refs[-1]
    terms = [ref[:rows, :].astype(F32) for ref in refs[:count]]
    out_ref[:rows, :] = tree_sum(terms).astype(BF16)
    extra = (out_ref.shape[0] - rows) // 2
    if extra:
        terms = [refs[0][rows : rows + extra, :]]
        terms += [sum_of_parts(ref, rows, extra) for ref in refs[1:count]]
        high, low = two_parts(tree_sum(terms))
        out_ref[rows : rows + extra, :] = high
        out_ref[rows + extra : rows + 2 * extra, :] = low


def gather_sum(terms, after, rows):
    return call(
        functools.partial(gather_body, count=len(terms), rows=rows),
        [*terms, *after],
        like(terms[-1]),
        name="gather_sum",
    )


def route_body(*refs, reps, chips, rows, pairs):
    spread, outs = refs[:reps], refs[reps:]
    place = Place()
    each = rows // pairs
    extra = (spread[0].shape[0] - rows) // 2
    if extra:
        high, low = two_parts(tree_sum([sum_of_parts(ref, rows, extra) for ref in spread]))
    for k in range(chips):
        u = place.chip ^ k
        for d in range(reps):

            @pl.when(((u % reps) ^ place.rep) == d)
            def _():
                at = pl.multiple_of(u // reps * each, each)
                outs[k][:each, :] = spread[d][pl.ds(at, each), :]

        if extra:
            outs[k][each : each + extra, :] = high
            outs[k][each + extra : each + 2 * extra, :] = low


def route(spread, chips, rows, pairs):
    height, width = spread[0].shape
    outs = [jax.ShapeDtypeStruct((height - rows + rows // pairs, width), BF16)] * chips
    body = functools.partial(route_body, reps=len(spread), chips=chips, rows=rows, pairs=pairs)
    return call(body, spread, outs, name="route")


def grad_body(*refs, reps, pairs, rows, scale):
    parts, out_ref = refs[:-1], refs[-1]
    section = lax.axis_index("section")
    extra = out_ref.shape[0] // len(parts)
    for k, part in enumerate(parts):
        chip = ((section // reps // 2) * reps + section % reps) ^ k
        out_ref[pl.ds(chip * extra, extra), :] = sum_of_parts(part, rows, extra) * scale


def grad_of(parts, reps, pairs, rows, scale):
    width = parts[0].shape[1]
    body = functools.partial(grad_body, reps=reps, pairs=pairs, rows=rows, scale=scale)
    return call(body, parts, jax.ShapeDtypeStruct((width, width), F32), name="grad_of")


def restore_body(ids_ref, order_ref, *refs, count, per):
    parts, out_ref = refs[:count], refs[-1]
    rows = out_ref.shape[0]
    block = parts[0].shape[1]
    base = pl.program_id(0) * rows
    acc = refs[count][...] if len(refs) > count + 1 else None
    for n, part in enumerate(parts):
        length = per * block
        at = pl.multiple_of(ids_ref[n] * length, length)
        target = order_ref[:, pl.ds(at, length)]
        hot = lax.broadcasted_iota(jnp.int32, (rows, length), 0) + base == target
        hot = jnp.where(hot, 1.0, 0.0).astype(BF16)
        columns = jnp.concatenate(
            [part[b * block : (b + 1) * block, :] for b in range(per)], axis=1
        )
        term = lax.dot_general(
            hot, columns, (((1,), (1,)), ((), ())), preferred_element_type=F32
        )
        acc = term if acc is None else acc + term
    out_ref[...] = acc.astype(out_ref.dtype)


def restore(ids, order_row, parts, start, per, dtype):
    panel = order_row.shape[1]
    width = parts[0].shape[1]
    rows = 512
    row_spec = pl.BlockSpec((rows, width), lambda i, ids: (i, 0))
    extra = () if start is None else (start,)
    return pl.pallas_call(
        functools.partial(restore_body, count=len(parts), per=per),
        out_shape=jax.ShapeDtypeStruct((panel, width), dtype),
        grid_spec=pltpu.PrefetchScalarGridSpec(
            num_scalar_prefetch=1,
            grid=(panel // rows,),
            in_specs=[whole_spec(order_row)]
            + [whole_spec(p) for p in parts]
            + [row_spec for _ in extra],
            out_specs=row_spec,
        ),
        compiler_params=params(24),
        cost_estimate=cost(2 * panel * panel * width, 4 * panel * width),
        name="restore",
    )(ids, order_row, *parts, *extra)


def tree_sum(terms):
    while len(terms) > 1:
        terms = [terms[i] + terms[i + 1] for i in range(0, len(terms), 2)]
    return terms[0]


def shards(features, order, tiles, tile_rows, tile_cols, live, weight, cotangent):
    reps = lax.axis_size("rep")
    sections = lax.axis_size("section")
    section = lax.axis_index("section")
    panel, width = features.shape
    rounds, slots, block, _ = tiles.shape[2:]
    blocks = panel // block
    chips = sections // 2
    pairs = rounds // 2
    near = reps // 2

    def over_chips(x, d):
        return lax.ppermute(x, "section", [(s, s ^ (2 * d)) for s in range(sections)])

    def over_cores(x):
        return lax.ppermute(x, "section", [(s, s ^ 1) for s in range(sections)])

    def over_reps(x, d):
        return lax.ppermute(x, "rep", [(r, r ^ d) for r in range(reps)])

    def from_owner(x, d):
        moves = []
        for r in range(reps):
            for j in range(rounds):
                source = j * reps + r
                target = (source ^ (2 * d)) ^ ((d // near) & 1)
                moves.append((source * reps + r, target * reps + r))
        return lax.ppermute(x, ("section", "rep"), moves)

    order_row = order.reshape(1, panel)
    owns = reorder(order_row, features)
    gots = [[own] + [from_owner(own, d) for d in range(1, chips)] for own in owns]
    bits = (blocks - 1).bit_length()
    plan = (live.reshape(rounds), entries_of(tile_rows, tile_cols, bits, owns[-1][:16]))
    own_tiles = tiles.reshape(rounds * slots, block, block)

    mine, mate = [], []
    for p in range(pairs):
        for h in range(HALVES):
            picked = pick(gots[h][2 * p * near : 2 * (p + 1) * near], near)
            mine.append(picked)
            mate.append(over_cores(picked))

    started = forward(plan, own_tiles, mine, None, reps)
    own, *others = forward(plan, own_tiles, mate, started, reps)
    sent = {d: over_reps(others[d - 1], d) for d in reversed(range(1, reps))}
    aggregated = total_of(own, [sent[d] for d in range(1, reps)])
    shares = [aggregated] + [over_reps(aggregated, d) for d in range(1, reps)]

    up_early, term = up_shares(weight, cotangent, shares[:near], 0)
    ups = [up_early, *up_shares(weight, cotangent, shares[near:], near)]
    cuts = math.gcd(2, blocks // chips)
    given = over_cores(backward(plan, own_tiles, ups, pairs, chips, cuts, term))
    kept = backward(plan, own_tiles, ups, pairs, chips, cuts)
    chunks = join(kept, given, term, cuts, chips)
    arrived = [[over_chips(c[d], d) for d in range(1, chips)] for c in chunks]
    late_shares = lax.optimization_barrier((shares, chunks[-1][-1]))[0]
    hidden, token = finish(weight, late_shares)
    per = blocks // chips // cuts
    height = pairs * per * width
    reduced = [
        gather_sum([c[0], *a], [token] if h == cuts - 1 else [], height)
        for h, (c, a) in enumerate(zip(chunks, arrived, strict=True))
    ]

    def to_owner(block, k):
        moves = []
        for s in range(sections):
            u = (s // 2) ^ k
            moves.append((s, (2 * (u // reps) + s % 2) * reps + u % reps))
        return lax.ppermute(block, "section", moves)

    mine_u = (section // reps // 2) * reps + section % reps
    feature_grad = None
    for h in range(cuts):
        spread = [reduced[h]] + [over_reps(reduced[h], d) for d in range(1, reps)]
        routed = route(spread, chips, height, pairs)
        parts = [to_owner(block, k) for k, block in enumerate(routed)]
        if h == 0:
            scale = 1.0 / math.sqrt(panel * sections)
            weight_grad = grad_of(parts, reps, pairs, per * width, scale)
        ids = jnp.stack([(mine_u ^ k) * cuts + h for k in range(chips)]).astype(jnp.int32)
        kind = BF16 if h == cuts - 1 else F32
        feature_grad = restore(ids, order_row, parts, feature_grad, per, kind)
    return (hidden, weight_grad, feature_grad)


def solution(mesh):
    placed = (
        P("section", None),
        P("section"),
        P("section", "rep", None, None, None, None),
        P("section", "rep", None, None),
        P("section", "rep", None, None),
        P("section", "rep", None),
        P(),
        P("section", None),
    )
    return jax.shard_map(
        shards,
        mesh=mesh,
        in_specs=placed,
        out_specs=(P("section", None), P(), P("section", None)),
        check_vma=False,
    )
```

```python
import functools
import math

import jax
import jax.numpy as jnp
from jax import lax
from jax.experimental import pallas as pl
from jax.experimental.pallas import tpu as pltpu
from jax.sharding import PartitionSpec as P

F32 = jnp.float32
BF16 = jnp.bfloat16
MIB = 1 << 20


def params(mib):
    return pltpu.CompilerParams(vmem_limit_bytes=mib * MIB)


def cost(flops, nbytes):
    return pl.CostEstimate(flops=int(flops), bytes_accessed=int(nbytes), transcendentals=0)


def whole_spec(array):
    zeros = (0,) * array.ndim
    return pl.BlockSpec(array.shape, lambda *_: zeros)


HALVES = 2
GROUP = 16


class Place:
    def __init__(self):
        reps = lax.axis_size("rep")
        section = lax.axis_index("section")
        self.rep = lax.axis_index("rep")
        self.chip = section // 2
        self.core = section % 2
        self.side = (section + self.rep) % 2
        self.row = section // reps
        self.low = ((section % reps) // 2) ^ (self.rep // 2)


def in_vmem(array):
    return pltpu.with_memory_space_constraint(array, pltpu.VMEM)


def call(body, operands, outs, scalars=(), scratch=(), vmem=(), mib=12, estimate=None, name=None):
    specs = [
        pl.BlockSpec(memory_space=pltpu.VMEM) if n in vmem else whole_spec(x)
        for n, x in enumerate(operands)
    ]
    operands = [in_vmem(x) if n in vmem else x for n, x in enumerate(operands)]
    return pl.pallas_call(
        body,
        out_shape=outs,
        grid_spec=pltpu.PrefetchScalarGridSpec(
            num_scalar_prefetch=len(scalars),
            grid=(1,),
            in_specs=specs,
            out_specs=jax.tree.map(whole_spec, outs),
            scratch_shapes=list(scratch),
        ),
        compiler_params=params(mib),
        cost_estimate=estimate or cost(0, MIB),
        name=name,
    )(*scalars, *operands)


def like(array, dtype=None):
    return jax.ShapeDtypeStruct(array.shape, dtype or array.dtype)


def reorder_body(order_ref, feat_ref, *outs):
    panel = feat_ref.shape[0]
    rows = outs[0].shape[0]
    step = min(256, rows)
    for i in range(panel // step):
        hot = lax.broadcasted_iota(jnp.int32, (step, panel), 1) == order_ref[pl.ds(i * step, step), :]
        hot = jnp.where(hot, 1.0, 0.0).astype(BF16)
        at = i * step % rows
        outs[i * step // rows][at : at + step, :] = jnp.dot(
            hot, feat_ref[...], preferred_element_type=F32
        ).astype(BF16)


def reorder(order_col, features):
    panel, width = features.shape
    outs = [jax.ShapeDtypeStruct((panel // HALVES, width), BF16)] * HALVES
    return call(
        reorder_body,
        [order_col, features],
        outs,
        estimate=cost(2 * panel * panel * width, 4 * panel * width),
        name="reorder",
    )


def entry_body(rows_ref, cols_ref, _, out_ref, *, bits):
    out_ref[...] = (rows_ref[0, 0] << bits) | cols_ref[0, 0]


def entries_of(rows, cols, bits, after):
    out = jax.ShapeDtypeStruct(rows.shape[2:], jnp.int32)
    return call(
        functools.partial(entry_body, bits=bits), [rows, cols, after], out, name="entries_of"
    )


def pick_body(*refs, near):
    options, out_ref = refs[:-1], refs[-1]
    place = Place()
    for n, option in enumerate(options):

        @pl.when((place.side == n // near) & (place.low == n % near))
        def _():
            out_ref[...] = option[...]


def pick(options, near):
    return call(functools.partial(pick_body, near=near), options, like(options[0]), name="pick")


def walk(live_ref, entry_ref, j, slots, step):
    count = live_ref[j]

    @pl.loop(0, (count + GROUP - 1) // GROUP)
    def _(g):
        entries = [entry_ref[j, g * GROUP + t] for t in range(GROUP)]
        alive = [g * GROUP + t < count for t in range(GROUP)]
        step(j * slots + g * GROUP, entries, alive)


def forward_body(live_ref, entry_ref, tiles_ref, *refs, slots, pairs, last):
    place = Place()
    xs, rest = refs[: pairs * HALVES], refs[pairs * HALVES :]
    panel_ref, acc = rest[-2:]
    blocks, block, width = panel_ref.shape
    bits = (blocks - 1).bit_length()
    if last:
        start, outs = rest[0], rest[1:-2]
        acc[pl.ds(0, blocks)] = start[...]
        acc[blocks] = jnp.zeros((block, width), F32)
    else:
        outs = rest[:-2]
        acc[...] = jnp.zeros_like(acc)
    per = blocks // HALVES
    for p in range(pairs):
        for h in range(HALVES):
            panel_ref[h * per : (h + 1) * per] = xs[p * HALVES + h][...].reshape(per, block, width)

        def step(first, entries, alive):
            terms = []
            for t in range(GROUP):
                x = panel_ref[entries[t] & (blocks - 1)]
                terms.append(jnp.dot(tiles_ref[first + t], x, preferred_element_type=F32))
            for t in range(GROUP):
                acc[jnp.where(alive[t], entries[t] >> bits, blocks)] += terms[t]

        j = place.row ^ (2 * p + (1 - place.side if last else place.side))
        walk(live_ref, entry_ref, j, slots, step)
    if last:
        span = blocks // len(outs)
        for d, out in enumerate(outs):
            at = (place.rep ^ d) * span
            out[...] = acc[pl.ds(at, span)].reshape(out.shape).astype(out.dtype)
    else:
        outs[0][...] = acc[pl.ds(0, blocks)]


def forward(plan, tiles, xs, start, reps):
    block = tiles.shape[1]
    width = xs[0].shape[1]
    pairs = len(xs) // HALVES
    blocks = xs[0].shape[0] * HALVES // block
    last = start is not None
    if last:
        rows = blocks * block // reps
        outs = [jax.ShapeDtypeStruct((rows, width), BF16 if d else F32) for d in range(reps)]
    else:
        outs = [jax.ShapeDtypeStruct((blocks, block, width), F32)]
    body = functools.partial(
        forward_body, slots=plan[1].shape[1], pairs=pairs, last=last
    )
    got = call(
        body,
        [tiles, *xs] + ([start] if last else []),
        outs,
        scalars=plan,
        scratch=[pltpu.VMEM((blocks, block, width), BF16), pltpu.VMEM((blocks + 1, block, width), F32)],
        vmem=(0,),
        estimate=cost(2 * 64 * block * block * width, 12 * MIB),
        name="forward",
    )
    return got if last else got[0]


def total_body(own_ref, *refs):
    total = own_ref[...]
    for ref in refs[:-1]:
        total = total + ref[...].astype(F32)
    refs[-1][...] = total.astype(BF16)


def total_of(own, others):
    return call(total_body, [own, *others], like(own, BF16), name="total_of")


def gradient_of(agg, co, weight):
    pre = jnp.dot(agg, weight, preferred_element_type=F32)
    gate = 1.0 / (1.0 + jnp.exp(-pre))
    grad_pre = (co.astype(F32) * gate * (1.0 + pre * (1.0 - gate))).astype(BF16)
    return pre, gate, grad_pre


def two_parts(value):
    high = value.astype(BF16)
    return high, (value - high.astype(F32)).astype(BF16)


def sum_of_parts(ref, at, rows):
    return ref[at : at + rows, :].astype(F32) + ref[at + rows : at + 2 * rows, :].astype(F32)


def up_body(w_ref, co_ref, *refs, first, count):
    place = Place()
    shares, out_ref = refs[:count], refs[count]
    weight = w_ref[...]
    rows = shares[0].shape[0]
    for n, share in enumerate(shares):
        at = pl.multiple_of((place.rep ^ (first + n)) * rows, rows)
        _, _, grad_pre = gradient_of(share[...], co_ref[pl.ds(at, rows), :], weight)
        if first + n == 0:
            grad = lax.dot_general(
                share[...], grad_pre, (((0,), (0,)), ((), ())), preferred_element_type=F32
            )
            width = grad.shape[0]
            refs[count + 1][:width, :], refs[count + 1][width:, :] = two_parts(grad)
        out_ref[n] = lax.dot_general(
            weight, grad_pre, (((1,), (1,)), ((), ())), preferred_element_type=F32
        ).astype(BF16)


def up_shares(weight, cotangent, shares, first):
    rows, width = shares[0].shape
    outs = [jax.ShapeDtypeStruct((len(shares), width, rows), BF16)]
    if first == 0:
        outs.append(jax.ShapeDtypeStruct((2 * width, width), BF16))
    return call(
        functools.partial(up_body, first=first, count=len(shares)),
        [weight, cotangent, *shares],
        outs,
        estimate=cost(4 * len(shares) * rows * width * width, 2 * MIB),
        name="up_shares",
    )


def finish_body(w_ref, *refs):
    place = Place()
    shares, (hidden_ref, token_ref) = refs[:-2], refs[-2:]
    rows = shares[0].shape[0]
    for n, share in enumerate(shares):
        at = pl.multiple_of((place.rep ^ n) * rows, rows)
        pre = jnp.dot(share[...], w_ref[...], preferred_element_type=F32)
        hidden_ref[pl.ds(at, rows), :] = (pre * (1.0 / (1.0 + jnp.exp(-pre)))).astype(BF16)
    token_ref[...] = jnp.zeros_like(token_ref)


def finish(weight, shares):
    rows, width = shares[0].shape
    outs = (
        jax.ShapeDtypeStruct((rows * len(shares), width), BF16),
        jax.ShapeDtypeStruct((8, 128), jnp.int32),
    )
    return call(finish_body, [weight, *shares], outs, estimate=cost(0, 4 * MIB), name="finish")


def backward_body(live_ref, entry_ref, tiles_ref, *refs, slots, keep, shape):
    refs, (out_ref, up_all, acc) = refs[:-3], refs[-3:]
    ups = refs if keep else refs[:-1]
    place = Place()
    cuts, chips, pairs, per, width, block = shape
    blocks = cuts * chips * per
    bits = (blocks - 1).bit_length()
    count, _, rows = ups[0].shape
    for m, up in enumerate(ups):
        for n in range(count):
            at = pl.multiple_of((place.rep ^ (m * count + n)) * rows, rows)
            up_all[:, pl.ds(at, rows)] = up[n]
    for p in range(pairs):
        acc[...] = jnp.zeros_like(acc)

        def step(first, entries, alive):
            terms = []
            for t in range(GROUP):
                at = pl.multiple_of((entries[t] >> bits) * block, block)
                terms.append(
                    jnp.dot(
                        up_all[:, pl.ds(at, block)],
                        tiles_ref[first + t],
                        preferred_element_type=F32,
                    )
                )
            for t in range(GROUP):
                acc[jnp.where(alive[t], entries[t] & (blocks - 1), blocks)] += terms[t]

        core = place.core
        walk(live_ref, entry_ref, 2 * p + (core if keep else 1 - core), slots, step)
        for h in range(cuts):
            for d in range(chips):
                at = ((place.chip ^ d) * cuts + h) * per
                to = ((h * chips + d) * pairs + p) * per
                out_ref[to : to + per] = acc[pl.ds(at, per)].astype(out_ref.dtype)
    if not keep:
        for n in range(2):
            out_ref[pairs * blocks + n] = refs[-1][n * width : (n + 1) * width, :]


def backward(plan, tiles, ups, pairs, chips, cuts, term=None):
    block = tiles.shape[1]
    count, width, rows = ups[0].shape
    panel = len(ups) * count * rows
    blocks = panel // block
    shape = (cuts, chips, pairs, blocks // chips // cuts, width, block)
    keep = term is None
    out_shape = (pairs * blocks + (0 if keep else 2), width, block)
    return call(
        functools.partial(backward_body, slots=plan[1].shape[1], keep=keep, shape=shape),
        [tiles, *ups] + ([] if keep else [term]),
        jax.ShapeDtypeStruct(out_shape, F32 if keep else BF16),
        scalars=plan,
        scratch=[pltpu.VMEM((width, panel), BF16), pltpu.VMEM((blocks + 1, width, block), F32)],
        vmem=(0,),
        estimate=cost(2 * 64 * block * block * width, 12 * MIB),
        name="backward",
    )


def join_body(kept_ref, given_ref, term_ref, *refs, cuts, chips):
    outs, grad = refs[:-1], refs[-1]
    place = Place()
    width = grad.shape[0]
    blocks = kept_ref.shape[0]
    mate = given_ref[blocks].astype(F32) + given_ref[blocks + 1].astype(F32)
    grad[...] = sum_of_parts(term_ref, 0, width) + mate
    per = blocks // (cuts * chips)
    for h in range(cuts):
        for d in range(chips):
            out = outs[h * chips + d]
            for b in range(per):
                n = (h * chips + d) * per + b
                out[b * width : (b + 1) * width, :] = (
                    kept_ref[n] + given_ref[n].astype(F32)
                ).astype(out.dtype)
            if h == 0:
                rows, end = width // chips, per * width
                high, low = two_parts(grad[pl.ds((place.chip ^ d) * rows, rows), :])
                if d == 0:
                    out[end : end + rows, :] = high.astype(F32) + low.astype(F32)
                else:
                    out[end : end + rows, :] = high
                    out[end + rows : end + 2 * rows, :] = low


def join(kept, given, term, cuts, chips):
    blocks, width, block = kept.shape
    rows = blocks // (cuts * chips) * width
    extra = width // chips
    outs = [
        jax.ShapeDtypeStruct(
            (rows + (0 if h else 2 * extra if d else extra), block), BF16 if d else F32
        )
        for h in range(cuts)
        for d in range(chips)
    ]
    got = call(
        functools.partial(join_body, cuts=cuts, chips=chips),
        [kept, given, term],
        outs,
        scratch=[pltpu.VMEM((width, width), F32)],
        name="join",
    )
    return [got[h * chips : (h + 1) * chips] for h in range(cuts)]


def gather_body(*refs, count, rows):
    out_ref = refs[-1]
    terms = [ref[:rows, :].astype(F32) for ref in refs[:count]]
    out_ref[:rows, :] = tree_sum(terms).astype(BF16)
    extra = (out_ref.shape[0] - rows) // 2
    if extra:
        terms = [refs[0][rows : rows + extra, :]]
        terms += [sum_of_parts(ref, rows, extra) for ref in refs[1:count]]
        high, low = two_parts(tree_sum(terms))
        out_ref[rows : rows + extra, :] = high
        out_ref[rows + extra : rows + 2 * extra, :] = low


def gather_sum(terms, after, rows):
    return call(
        functools.partial(gather_body, count=len(terms), rows=rows),
        [*terms, *after],
        like(terms[-1]),
        name="gather_sum",
    )


def route_body(*refs, reps, chips, rows, pairs):
    spread, outs = refs[:reps], refs[reps:]
    place = Place()
    each = rows // pairs
    extra = (spread[0].shape[0] - rows) // 2
    if extra:
        high, low = two_parts(tree_sum([sum_of_parts(ref, rows, extra) for ref in spread]))
    for k in range(chips):
        u = place.chip ^ k
        for d in range(reps):

            @pl.when(((u % reps) ^ place.rep) == d)
            def _():
                at = pl.multiple_of(u // reps * each, each)
                outs[k][:each, :] = spread[d][pl.ds(at, each), :]

        if extra:
            outs[k][each : each + extra, :] = high
            outs[k][each + extra : each + 2 * extra, :] = low


def route(spread, chips, rows, pairs):
    height, width = spread[0].shape
    outs = [jax.ShapeDtypeStruct((height - rows + rows // pairs, width), BF16)] * chips
    body = functools.partial(route_body, reps=len(spread), chips=chips, rows=rows, pairs=pairs)
    return call(body, spread, outs, name="route")


def restore_body(order_ref, *refs, first, count, per, scale, reps):
    parts, refs = refs[:count], refs[count:]
    start, (out_ref, grad_ref) = refs[:-2], refs[-2:]
    section = lax.axis_index("section")
    base_u = (section // reps // 2) * reps + section % reps
    rows = out_ref.shape[0]
    block = parts[0].shape[1]
    step = pl.program_id(0)
    acc = start[0][...] if start else None

    @pl.when(step == 0)
    def _():
        grad_ref[...] = start[1][...] if start else jnp.zeros_like(grad_ref)
        extra = (parts[0].shape[0] - per * block) // 2
        for n, part in enumerate(parts):
            at = pl.multiple_of((base_u ^ (first + n)) * extra, extra)
            grad_ref[pl.ds(at, extra), :] = sum_of_parts(part, per * block, extra) * scale

    for n, part in enumerate(parts):
        length = per * block
        at = pl.multiple_of((base_u ^ (first + n)) * length, length)
        target = order_ref[:, pl.ds(at, length)]
        hot = lax.broadcasted_iota(jnp.int32, (rows, length), 0) + step * rows == target
        hot = jnp.where(hot, 1.0, 0.0).astype(BF16)
        columns = jnp.concatenate(
            [part[b * block : (b + 1) * block, :] for b in range(per)], axis=1
        )
        term = lax.dot_general(
            hot, columns, (((1,), (1,)), ((), ())), preferred_element_type=F32
        )
        acc = term if acc is None else acc + term
    out_ref[...] = acc.astype(out_ref.dtype)


def restore(order_row, parts, first, start, per, scale, reps):
    panel = order_row.shape[1]
    width = parts[0].shape[1]
    rows = 512
    row_spec = pl.BlockSpec((rows, width), lambda i: (i, 0))
    grad_spec = pl.BlockSpec((width, width), lambda i: (0, 0))
    body = functools.partial(
        restore_body, first=first, count=len(parts), per=per, scale=scale, reps=reps
    )
    return pl.pallas_call(
        body,
        out_shape=(
            jax.ShapeDtypeStruct((panel, width), BF16 if start else F32),
            jax.ShapeDtypeStruct((width, width), F32),
        ),
        grid=(panel // rows,),
        in_specs=[whole_spec(x) for x in (order_row, *parts)]
        + ([row_spec, grad_spec] if start else []),
        out_specs=(row_spec, grad_spec),
        compiler_params=params(24),
        cost_estimate=cost(2 * panel * panel * width, 4 * panel * width),
        name="restore",
    )(order_row, *parts, *start)


def tree_sum(terms):
    while len(terms) > 1:
        terms = [terms[i] + terms[i + 1] for i in range(0, len(terms), 2)]
    return terms[0]


def shards(features, order, tiles, tile_rows, tile_cols, live, weight, cotangent):
    reps = lax.axis_size("rep")
    sections = lax.axis_size("section")
    panel, width = features.shape
    rounds, slots, block, _ = tiles.shape[2:]
    blocks = panel // block
    chips = sections // 2
    pairs = rounds // 2
    near = reps // 2

    def over_chips(x, d):
        return lax.ppermute(x, "section", [(s, s ^ (2 * d)) for s in range(sections)])

    def over_cores(x):
        return lax.ppermute(x, "section", [(s, s ^ 1) for s in range(sections)])

    def over_reps(x, d):
        return lax.ppermute(x, "rep", [(r, r ^ d) for r in range(reps)])

    def from_owner(x, d):
        moves = []
        for r in range(reps):
            for j in range(rounds):
                source = j * reps + r
                target = (source ^ (2 * d)) ^ ((d // near) & 1)
                moves.append((source * reps + r, target * reps + r))
        return lax.ppermute(x, ("section", "rep"), moves)

    order_row = order.reshape(1, panel)
    owns = reorder(order.reshape(panel, 1), features)
    gots = [[own] + [from_owner(own, d) for d in range(1, chips)] for own in owns]
    bits = (blocks - 1).bit_length()
    plan = (live.reshape(rounds), entries_of(tile_rows, tile_cols, bits, owns[-1][:16]))
    own_tiles = tiles.reshape(rounds * slots, block, block)

    mine, mate = [], []
    for p in range(pairs):
        for h in range(HALVES):
            picked = pick(gots[h][2 * p * near : 2 * (p + 1) * near], near)
            mine.append(picked)
            mate.append(over_cores(picked))

    started = forward(plan, own_tiles, mine, None, reps)
    own, *others = forward(plan, own_tiles, mate, started, reps)
    sent = {d: over_reps(others[d - 1], d) for d in reversed(range(1, reps))}
    aggregated = total_of(own, [sent[d] for d in range(1, reps)])
    shares = [aggregated] + [over_reps(aggregated, d) for d in range(1, reps)]

    up_early, term = up_shares(weight, cotangent, shares[:near], 0)
    ups = [up_early, *up_shares(weight, cotangent, shares[near:], near)]
    cuts = 1
    given = over_cores(backward(plan, own_tiles, ups, pairs, chips, cuts, term))
    kept = backward(plan, own_tiles, ups, pairs, chips, cuts)
    chunks = join(kept, given, term, cuts, chips)
    arrived = [[over_chips(c[d], d) for d in range(1, chips)] for c in chunks]
    late_shares = lax.optimization_barrier((shares, chunks[-1][-1]))[0]
    hidden, token = finish(weight, late_shares)
    per = blocks // chips // cuts
    height = pairs * per * width
    reduced = gather_sum([chunks[0][0], *arrived[0]], [token], height)

    def to_owner(block, k):
        moves = []
        for s in range(sections):
            u = (s // 2) ^ k
            moves.append((s, (2 * (u // reps) + s % 2) * reps + u % reps))
        return lax.ppermute(block, "section", moves)

    spread = [reduced] + [over_reps(reduced, d) for d in range(1, reps)]
    parts = [to_owner(block, k) for k, block in enumerate(route(spread, chips, height, pairs))]
    scale = 1.0 / math.sqrt(panel * sections)
    half = chips // 2
    begun = restore(order_row, parts[:half], 0, (), per, scale, reps)
    feature_grad, weight_grad = restore(order_row, parts[half:], half, begun, per, scale, reps)
    return (hidden, weight_grad, feature_grad)


def solution(mesh):
    placed = (
        P("section", None),
        P("section"),
        P("section", "rep", None, None, None, None),
        P("section", "rep", None, None),
        P("section", "rep", None, None),
        P("section", "rep", None),
        P(),
        P("section", None),
    )
    return jax.shard_map(
        shards,
        mesh=mesh,
        in_specs=placed,
        out_specs=(P("section", None), P(), P("section", None)),
        check_vma=False,
    )
```

```python
import functools
import math

import jax
import jax.numpy as jnp
from jax import lax
from jax.experimental import pallas as pl
from jax.experimental.pallas import tpu as pltpu
from jax.sharding import PartitionSpec as P

F32 = jnp.float32
BF16 = jnp.bfloat16
MIB = 1 << 20


def params(mib):
    return pltpu.CompilerParams(vmem_limit_bytes=mib * MIB)


def cost(flops, nbytes):
    return pl.CostEstimate(flops=int(flops), bytes_accessed=int(nbytes), transcendentals=0)


def whole_spec(array):
    zeros = (0,) * array.ndim
    return pl.BlockSpec(array.shape, lambda *_: zeros)


HALVES = 2
GROUP = 16


class Place:
    def __init__(self):
        reps = lax.axis_size("rep")
        section = lax.axis_index("section")
        self.rep = lax.axis_index("rep")
        self.chip = section // 2
        self.core = section % 2
        self.side = (section + self.rep) % 2
        self.row = section // reps
        self.low = ((section % reps) // 2) ^ (self.rep // 2)


def in_vmem(array):
    return pltpu.with_memory_space_constraint(array, pltpu.VMEM)


def in_hbm(array):
    return pltpu.with_memory_space_constraint(array, pltpu.HBM)


def call(body, operands, outs, scalars=(), scratch=(), vmem=(), mib=12, estimate=None, name=None):
    specs = [
        pl.BlockSpec(memory_space=pltpu.VMEM) if n in vmem else whole_spec(x)
        for n, x in enumerate(operands)
    ]
    operands = [in_vmem(x) if n in vmem else x for n, x in enumerate(operands)]
    return pl.pallas_call(
        body,
        out_shape=outs,
        grid_spec=pltpu.PrefetchScalarGridSpec(
            num_scalar_prefetch=len(scalars),
            grid=(1,),
            in_specs=specs,
            out_specs=jax.tree.map(whole_spec, outs),
            scratch_shapes=list(scratch),
        ),
        compiler_params=params(mib),
        cost_estimate=estimate or cost(0, MIB),
        name=name,
    )(*scalars, *operands)


def like(array, dtype=None):
    return jax.ShapeDtypeStruct(array.shape, dtype or array.dtype)


def reorder_body(order_ref, feat_ref, out_ref, *, first):
    panel = feat_ref.shape[0]
    rows = out_ref.shape[0]
    step = min(256, rows)
    for i in range(first // step, (first + rows) // step):
        hot = lax.broadcasted_iota(jnp.int32, (step, panel), 1) == order_ref[pl.ds(i * step, step), :]
        hot = jnp.where(hot, 1.0, 0.0).astype(BF16)
        at = i * step - first
        out_ref[at : at + step, :] = jnp.dot(
            hot, feat_ref[...], preferred_element_type=F32
        ).astype(BF16)


def reorder(order_col, features, half):
    panel, width = features.shape
    rows = panel // HALVES
    return call(
        functools.partial(reorder_body, first=half * rows),
        [order_col, features],
        jax.ShapeDtypeStruct((rows, width), BF16),
        estimate=cost(2 * rows * panel * width, 4 * rows * width),
        name="reorder",
    )


def entry_body(rows_ref, cols_ref, live_ref, _, out_ref, *, bits):
    rounds, slots = rows_ref.shape[2:]
    out_ref[:, :slots] = (rows_ref[0, 0] << bits) | cols_ref[0, 0]
    for j in range(rounds):
        out_ref[j : j + 1, slots:] = jnp.full((1, 1), live_ref[0, 0, j], jnp.int32)


def entries_of(rows, cols, live, bits, after):
    rounds, slots = rows.shape[2:]
    shape = (rounds, slots + 1)
    return pl.pallas_call(
        functools.partial(entry_body, bits=bits),
        out_shape=jax.ShapeDtypeStruct(shape, jnp.int32),
        grid=(1,),
        in_specs=[
            whole_spec(rows),
            whole_spec(cols),
            pl.BlockSpec(memory_space=pltpu.SMEM),
            whole_spec(after),
        ],
        out_specs=pl.BlockSpec(shape, lambda i: (0, 0)),
        compiler_params=params(12),
        cost_estimate=cost(0, MIB),
        name="entries_of",
    )(*map(in_hbm, (rows, cols, live)), after)


def pick_body(*refs, near, count):
    options, out_ref = refs[:count], refs[-1]
    place = Place()
    for n, option in enumerate(options):

        @pl.when((place.side == n // near) & (place.low == n % near))
        def _():
            out_ref[...] = option[...]


def pick(options, near, after):
    body = functools.partial(pick_body, near=near, count=len(options))
    return call(body, [*options, *after], like(options[0]), name="pick")


def walk(entry_ref, j, slots, step):
    count = entry_ref[j, slots]

    @pl.loop(0, (count + GROUP - 1) // GROUP)
    def _(g):
        entries = [entry_ref[j, g * GROUP + t] for t in range(GROUP)]
        alive = [g * GROUP + t < count for t in range(GROUP)]
        step(j * slots + g * GROUP, entries, alive)


def forward_body(entry_ref, tiles_ref, *refs, slots, pairs, last):
    place = Place()
    xs, rest = refs[: pairs * HALVES], refs[pairs * HALVES :]
    panel_ref, acc = rest[-2:]
    blocks, block, width = panel_ref.shape
    bits = (blocks - 1).bit_length()
    if last:
        start, outs = rest[0], rest[1:-2]
        acc[pl.ds(0, blocks)] = start[...]
        acc[blocks] = jnp.zeros((block, width), F32)
    else:
        outs = rest[:-2]
        acc[...] = jnp.zeros_like(acc)
    per = blocks // HALVES
    for p in range(pairs):
        for h in range(HALVES):
            panel_ref[h * per : (h + 1) * per] = xs[p * HALVES + h][...].reshape(per, block, width)

        def step(first, entries, alive):
            terms = []
            for t in range(GROUP):
                x = panel_ref[entries[t] & (blocks - 1)]
                terms.append(jnp.dot(tiles_ref[first + t], x, preferred_element_type=F32))
            for t in range(GROUP):
                acc[jnp.where(alive[t], entries[t] >> bits, blocks)] += terms[t]

        j = place.row ^ (2 * p + (1 - place.side if last else place.side))
        walk(entry_ref, j, slots, step)
    if last:
        span = blocks // len(outs)
        for d, out in enumerate(outs):
            at = (place.rep ^ d) * span
            out[...] = acc[pl.ds(at, span)].reshape(out.shape).astype(out.dtype)
    else:
        outs[0][...] = acc[pl.ds(0, blocks)]


def forward(plan, tiles, xs, start, reps):
    block = tiles.shape[1]
    width = xs[0].shape[1]
    pairs = len(xs) // HALVES
    blocks = xs[0].shape[0] * HALVES // block
    last = start is not None
    if last:
        rows = blocks * block // reps
        outs = [jax.ShapeDtypeStruct((rows, width), BF16 if d else F32) for d in range(reps)]
    else:
        outs = [jax.ShapeDtypeStruct((blocks, block, width), F32)]
    body = functools.partial(
        forward_body, slots=plan.shape[1] - 1, pairs=pairs, last=last
    )
    got = call(
        body,
        [tiles, *xs] + ([start] if last else []),
        outs,
        scalars=(plan,),
        scratch=[pltpu.VMEM((blocks, block, width), BF16), pltpu.VMEM((blocks + 1, block, width), F32)],
        vmem=(0,),
        estimate=cost(2 * 64 * block * block * width, 12 * MIB),
        name="forward",
    )
    return got if last else got[0]


def total_body(own_ref, *refs):
    total = own_ref[...]
    for ref in refs[:-1]:
        total = total + ref[...].astype(F32)
    refs[-1][...] = total.astype(BF16)


def total_of(own, others):
    return call(total_body, [own, *others], like(own, BF16), name="total_of")


def gradient_of(agg, co, weight):
    pre = jnp.dot(agg, weight, preferred_element_type=F32)
    gate = 1.0 / (1.0 + jnp.exp(-pre))
    grad_pre = (co.astype(F32) * gate * (1.0 + pre * (1.0 - gate))).astype(BF16)
    return pre, gate, grad_pre


def two_parts(value):
    high = value.astype(BF16)
    return high, (value - high.astype(F32)).astype(BF16)


def sum_of_parts(ref, at, rows):
    return ref[at : at + rows, :].astype(F32) + ref[at + rows : at + 2 * rows, :].astype(F32)


def up_body(w_ref, co_ref, *refs, first, count):
    place = Place()
    shares, out_ref = refs[:count], refs[count]
    weight = w_ref[...]
    rows = shares[0].shape[0]
    for n, share in enumerate(shares):
        at = pl.multiple_of((place.rep ^ (first + n)) * rows, rows)
        _, _, grad_pre = gradient_of(share[...], co_ref[pl.ds(at, rows), :], weight)
        if first + n == 0:
            grad = lax.dot_general(
                share[...], grad_pre, (((0,), (0,)), ((), ())), preferred_element_type=F32
            )
            width = grad.shape[0]
            refs[count + 1][:width, :], refs[count + 1][width:, :] = two_parts(grad)
        out_ref[n] = lax.dot_general(
            weight, grad_pre, (((1,), (1,)), ((), ())), preferred_element_type=F32
        ).astype(BF16)


def up_shares(weight, cotangent, shares, first):
    rows, width = shares[0].shape
    outs = [jax.ShapeDtypeStruct((len(shares), width, rows), BF16)]
    if first == 0:
        outs.append(jax.ShapeDtypeStruct((2 * width, width), BF16))
    return call(
        functools.partial(up_body, first=first, count=len(shares)),
        [weight, cotangent, *shares],
        outs,
        estimate=cost(4 * len(shares) * rows * width * width, 2 * MIB),
        name="up_shares",
    )


def finish_body(w_ref, *refs):
    place = Place()
    shares, (hidden_ref, token_ref) = refs[:-2], refs[-2:]
    rows = shares[0].shape[0]
    for n, share in enumerate(shares):
        at = pl.multiple_of((place.rep ^ n) * rows, rows)
        pre = jnp.dot(share[...], w_ref[...], preferred_element_type=F32)
        hidden_ref[pl.ds(at, rows), :] = (pre * (1.0 / (1.0 + jnp.exp(-pre)))).astype(BF16)
    token_ref[...] = jnp.zeros_like(token_ref)


def finish(weight, shares):
    rows, width = shares[0].shape
    outs = (
        jax.ShapeDtypeStruct((rows * len(shares), width), BF16),
        jax.ShapeDtypeStruct((8, 128), jnp.int32),
    )
    return call(finish_body, [weight, *shares], outs, estimate=cost(0, 4 * MIB), name="finish")


def backward_body(entry_ref, tiles_ref, *refs, slots, keep, shape):
    refs, (out_ref, up_all, acc) = refs[:-3], refs[-3:]
    ups = refs if keep else refs[:-1]
    place = Place()
    cuts, chips, pairs, per, width, block = shape
    blocks = cuts * chips * per
    bits = (blocks - 1).bit_length()
    count, _, rows = ups[0].shape
    for m, up in enumerate(ups):
        for n in range(count):
            at = pl.multiple_of((place.rep ^ (m * count + n)) * rows, rows)
            up_all[:, pl.ds(at, rows)] = up[n]
    for p in range(pairs):
        acc[...] = jnp.zeros_like(acc)

        def step(first, entries, alive):
            terms = []
            for t in range(GROUP):
                at = pl.multiple_of((entries[t] >> bits) * block, block)
                terms.append(
                    jnp.dot(
                        up_all[:, pl.ds(at, block)],
                        tiles_ref[first + t],
                        preferred_element_type=F32,
                    )
                )
            for t in range(GROUP):
                acc[jnp.where(alive[t], entries[t] & (blocks - 1), blocks)] += terms[t]

        core = place.core
        walk(entry_ref, 2 * p + (core if keep else 1 - core), slots, step)
        for h in range(cuts):
            for d in range(chips):
                at = ((place.chip ^ d) * cuts + h) * per
                to = ((h * chips + d) * pairs + p) * per
                out_ref[to : to + per] = acc[pl.ds(at, per)].astype(out_ref.dtype)
    if not keep:
        for n in range(2):
            out_ref[pairs * blocks + n] = refs[-1][n * width : (n + 1) * width, :]


def backward(plan, tiles, ups, pairs, chips, cuts, term=None):
    block = tiles.shape[1]
    count, width, rows = ups[0].shape
    panel = len(ups) * count * rows
    blocks = panel // block
    shape = (cuts, chips, pairs, blocks // chips // cuts, width, block)
    keep = term is None
    out_shape = (pairs * blocks + (0 if keep else 2), width, block)
    return call(
        functools.partial(backward_body, slots=plan.shape[1] - 1, keep=keep, shape=shape),
        [tiles, *ups] + ([] if keep else [term]),
        jax.ShapeDtypeStruct(out_shape, F32 if keep else BF16),
        scalars=(plan,),
        scratch=[pltpu.VMEM((width, panel), BF16), pltpu.VMEM((blocks + 1, width, block), F32)],
        vmem=(0,),
        estimate=cost(2 * 64 * block * block * width, 12 * MIB),
        name="backward",
    )


def join_body(kept_ref, given_ref, term_ref, *refs, cuts, chips):
    outs, grad = refs[:-1], refs[-1]
    place = Place()
    width = grad.shape[0]
    blocks = kept_ref.shape[0]
    mate = given_ref[blocks].astype(F32) + given_ref[blocks + 1].astype(F32)
    grad[...] = sum_of_parts(term_ref, 0, width) + mate
    per = blocks // (cuts * chips)
    for h in range(cuts):
        for d in range(chips):
            out = outs[h * chips + d]
            for b in range(per):
                n = (h * chips + d) * per + b
                out[b * width : (b + 1) * width, :] = (
                    kept_ref[n] + given_ref[n].astype(F32)
                ).astype(out.dtype)
            if h == 0:
                rows, end = width // chips, per * width
                high, low = two_parts(grad[pl.ds((place.chip ^ d) * rows, rows), :])
                if d == 0:
                    out[end : end + rows, :] = high.astype(F32) + low.astype(F32)
                else:
                    out[end : end + rows, :] = high
                    out[end + rows : end + 2 * rows, :] = low


def join(kept, given, term, cuts, chips):
    blocks, width, block = kept.shape
    rows = blocks // (cuts * chips) * width
    extra = width // chips
    outs = [
        jax.ShapeDtypeStruct(
            (rows + (0 if h else 2 * extra if d else extra), block), BF16 if d else F32
        )
        for h in range(cuts)
        for d in range(chips)
    ]
    got = call(
        functools.partial(join_body, cuts=cuts, chips=chips),
        [kept, given, term],
        outs,
        scratch=[pltpu.VMEM((width, width), F32)],
        name="join",
    )
    return [got[h * chips : (h + 1) * chips] for h in range(cuts)]


def gather_body(*refs, count, rows):
    out_ref = refs[-1]
    terms = [ref[:rows, :].astype(F32) for ref in refs[:count]]
    out_ref[:rows, :] = tree_sum(terms).astype(BF16)
    extra = (out_ref.shape[0] - rows) // 2
    if extra:
        terms = [refs[0][rows : rows + extra, :]]
        terms += [sum_of_parts(ref, rows, extra) for ref in refs[1:count]]
        high, low = two_parts(tree_sum(terms))
        out_ref[rows : rows + extra, :] = high
        out_ref[rows + extra : rows + 2 * extra, :] = low


def gather_sum(terms, after, rows):
    return call(
        functools.partial(gather_body, count=len(terms), rows=rows),
        [*terms, *after],
        like(terms[-1]),
        name="gather_sum",
    )


def route_body(*refs, reps, chips, rows, pairs):
    spread, outs = refs[:reps], refs[reps + 1 :]
    place = Place()
    each = rows // pairs
    extra = (spread[0].shape[0] - rows) // 2
    if extra:
        high, low = two_parts(tree_sum([sum_of_parts(ref, rows, extra) for ref in spread]))
    for k in range(chips):
        u = place.chip ^ k
        for d in range(reps):

            @pl.when(((u % reps) ^ place.rep) == d)
            def _():
                at = pl.multiple_of(u // reps * each, each)
                outs[k][:each, :] = spread[d][pl.ds(at, each), :]

        if extra:
            outs[k][each : each + extra, :] = high
            outs[k][each + extra : each + 2 * extra, :] = low


def route(spread, after, chips, rows, pairs):
    height, width = spread[0].shape
    outs = [jax.ShapeDtypeStruct((height - rows + rows // pairs, width), BF16)] * chips
    body = functools.partial(route_body, reps=len(spread), chips=chips, rows=rows, pairs=pairs)
    return call(body, [*spread, after], outs, name="route")


def hot_body(order_ref, _, out_ref, token_ref):
    panel = out_ref.shape[0]
    rows = 256
    target = order_ref[...]
    token_ref[...] = jnp.zeros_like(token_ref)

    @pl.loop(0, panel // rows)
    def _(i):
        at = pl.multiple_of(i * rows, rows)
        hot = lax.broadcasted_iota(jnp.int32, (rows, panel), 0) + at == target
        out_ref[pl.ds(at, rows), :] = jnp.where(hot, 1.0, 0.0).astype(BF16)


def inverse_hot(order_row, after):
    panel = order_row.shape[1]
    return pl.pallas_call(
        hot_body,
        out_shape=(
            pltpu.VMEM((panel, panel), BF16),
            jax.ShapeDtypeStruct((8, 128), jnp.int32),
        ),
        grid=(1,),
        in_specs=[whole_spec(order_row), pl.BlockSpec(memory_space=pl.ANY)],
        out_specs=(
            pl.BlockSpec(memory_space=pltpu.VMEM),
            pl.BlockSpec((8, 128), lambda i: (0, 0)),
        ),
        compiler_params=params(8),
        cost_estimate=cost(0, 6 * MIB),
        name="inverse_hot",
    )(order_row, after)


def restore_body(hot_ref, *refs, first, count, per, scale, reps):
    parts, refs = refs[:count], refs[count:]
    start, (out_ref, grad_ref) = refs[:-2], refs[-2:]
    section = lax.axis_index("section")
    base_u = (section // reps // 2) * reps + section % reps
    block = parts[0].shape[1]
    extra = (parts[0].shape[0] - per * block) // 2
    length = per * block
    grad_ref[...] = start[1][...] if start else jnp.zeros_like(grad_ref)
    columns, places = [], []
    for n, part in enumerate(parts):
        u = base_u ^ (first + n)
        at = pl.multiple_of(u * extra, extra)
        grad_ref[pl.ds(at, extra), :] = sum_of_parts(part, length, extra) * scale
        columns.append(
            jnp.concatenate([part[b * block : (b + 1) * block, :] for b in range(per)], axis=1)
        )
        places.append(pl.multiple_of(u * length, length))
    rows = 512
    for i in range(out_ref.shape[0] // rows):
        span = slice(i * rows, (i + 1) * rows)
        acc = start[0][span, :] if start else None
        for n, at in enumerate(places):
            term = lax.dot_general(
                hot_ref[span, pl.ds(at, length)],
                columns[n],
                (((1,), (1,)), ((), ())),
                preferred_element_type=F32,
            )
            acc = term if acc is None else acc + term
        out_ref[span, :] = acc.astype(out_ref.dtype)


def restore(hot, parts, first, start, per, scale, reps):
    panel = hot.shape[0]
    width = parts[0].shape[1]
    body = functools.partial(
        restore_body, first=first, count=len(parts), per=per, scale=scale, reps=reps
    )
    outs = (
        jax.ShapeDtypeStruct((panel, width), BF16 if start else F32),
        jax.ShapeDtypeStruct((width, width), F32),
    )
    return call(
        body,
        [hot, *parts, *start],
        outs,
        vmem=(0,),
        estimate=cost(2 * panel * panel * width, 4 * panel * width),
        name="restore",
    )


def tree_sum(terms):
    while len(terms) > 1:
        terms = [terms[i] + terms[i + 1] for i in range(0, len(terms), 2)]
    return terms[0]


def shards(features, order, tiles, tile_rows, tile_cols, live, weight, cotangent):
    reps = lax.axis_size("rep")
    sections = lax.axis_size("section")
    panel, width = features.shape
    rounds, slots, block, _ = tiles.shape[2:]
    blocks = panel // block
    chips = sections // 2
    pairs = rounds // 2
    near = reps // 2

    def over_chips(x, d):
        return lax.ppermute(x, "section", [(s, s ^ (2 * d)) for s in range(sections)])

    def over_cores(x):
        return lax.ppermute(x, "section", [(s, s ^ 1) for s in range(sections)])

    def over_reps(x, d):
        return lax.ppermute(x, "rep", [(r, r ^ d) for r in range(reps)])

    def from_owner(x, d):
        moves = []
        for r in range(reps):
            for j in range(rounds):
                source = j * reps + r
                target = (source ^ (2 * d)) ^ ((d // near) & 1)
                moves.append((source * reps + r, target * reps + r))
        return lax.ppermute(x, ("section", "rep"), moves)

    order_col, order_row = order.reshape(panel, 1), order.reshape(1, panel)
    owns = [reorder(order_col, features, h) for h in range(HALVES)]
    gots = [[own] + [from_owner(own, d) for d in range(1, chips)] for own in owns]
    bits = (blocks - 1).bit_length()
    plan = entries_of(tile_rows, tile_cols, live, bits, owns[-1][:16])
    own_tiles = tiles.reshape(rounds * slots, block, block)

    mine, mate = [], []
    for p in range(pairs):
        for h in range(HALVES):
            first = 2 * p * near
            picked = pick(gots[h][first : first + 2 * near], near, [] if h else [plan])
            mine.append(picked)
            mate.append(over_cores(picked))

    started = forward(plan, own_tiles, mine, None, reps)
    own, *others = forward(plan, own_tiles, mate, started, reps)
    sent = {d: over_reps(others[d - 1], d) for d in reversed(range(1, reps))}
    aggregated = total_of(own, [sent[d] for d in range(1, reps)])
    shares = [aggregated] + [over_reps(aggregated, d) for d in range(1, reps)]

    up_early, term = up_shares(weight, cotangent, shares[:near], 0)
    ups = [up_early, *up_shares(weight, cotangent, shares[near:], near)]
    cuts = 1
    given = over_cores(backward(plan, own_tiles, ups, pairs, chips, cuts, term))
    kept = backward(plan, own_tiles, ups, pairs, chips, cuts)
    chunks = join(kept, given, term, cuts, chips)
    arrived = [[over_chips(c[d], d) for d in range(1, chips)] for c in chunks]
    late_shares = lax.optimization_barrier((shares, chunks[-1][-1]))[0]
    hidden, token = finish(weight, late_shares)
    per = blocks // chips // cuts
    height = pairs * per * width
    reduced = gather_sum([chunks[0][0], *arrived[0]], [token], height)

    def to_owner(block, k):
        moves = []
        for s in range(sections):
            u = (s // 2) ^ k
            moves.append((s, (2 * (u // reps) + s % 2) * reps + u % reps))
        return lax.ppermute(block, "section", moves)

    spread = [reduced] + [over_reps(reduced, d) for d in range(1, reps)]
    hot, ready = inverse_hot(order_row, reduced)
    routed = route(spread, ready, chips, height, pairs)
    parts = [to_owner(block, k) for k, block in enumerate(routed)]
    scale = 1.0 / math.sqrt(panel * sections)
    half = chips // 2
    begun = restore(hot, parts[:half], 0, (), per, scale, reps)
    feature_grad, weight_grad = restore(hot, parts[half:], half, begun, per, scale, reps)
    return (hidden, weight_grad, feature_grad)


def solution(mesh):
    placed = (
        P("section", None),
        P("section"),
        P("section", "rep", None, None, None, None),
        P("section", "rep", None, None),
        P("section", "rep", None, None),
        P("section", "rep", None),
        P(),
        P("section", None),
    )
    return jax.shard_map(
        shards,
        mesh=mesh,
        in_specs=placed,
        out_specs=(P("section", None), P(), P("section", None)),
        check_vma=False,
    )
```

```python
import functools
import math

import jax
import jax.numpy as jnp
from jax import lax
from jax.experimental import pallas as pl
from jax.experimental.pallas import tpu as pltpu
from jax.sharding import PartitionSpec as P

F32 = jnp.float32
BF16 = jnp.bfloat16
MIB = 1 << 20


def params(mib):
    return pltpu.CompilerParams(vmem_limit_bytes=mib * MIB)


def cost(flops, nbytes):
    return pl.CostEstimate(flops=int(flops), bytes_accessed=int(nbytes), transcendentals=0)


def whole_spec(array):
    zeros = (0,) * array.ndim
    return pl.BlockSpec(array.shape, lambda *_: zeros)


HALVES = 2
GROUP = 16


class Place:
    def __init__(self):
        reps = lax.axis_size("rep")
        section = lax.axis_index("section")
        self.rep = lax.axis_index("rep")
        self.chip = section // 2
        self.core = section % 2
        self.side = (section + self.rep) % 2
        self.row = section // reps
        self.low = ((section % reps) // 2) ^ (self.rep // 2)


def in_vmem(array):
    return pltpu.with_memory_space_constraint(array, pltpu.VMEM)


def in_hbm(array):
    return pltpu.with_memory_space_constraint(array, pltpu.HBM)


def call(body, operands, outs, scalars=(), scratch=(), vmem=(), mib=12, estimate=None, name=None):
    specs = [
        pl.BlockSpec(memory_space=pltpu.VMEM) if n in vmem else whole_spec(x)
        for n, x in enumerate(operands)
    ]
    operands = [in_vmem(x) if n in vmem else x for n, x in enumerate(operands)]
    return pl.pallas_call(
        body,
        out_shape=outs,
        grid_spec=pltpu.PrefetchScalarGridSpec(
            num_scalar_prefetch=len(scalars),
            grid=(1,),
            in_specs=specs,
            out_specs=jax.tree.map(whole_spec, outs),
            scratch_shapes=list(scratch),
        ),
        compiler_params=params(mib),
        cost_estimate=estimate or cost(0, MIB),
        name=name,
    )(*scalars, *operands)


def like(array, dtype=None):
    return jax.ShapeDtypeStruct(array.shape, dtype or array.dtype)


def reorder_body(order_ref, feat_ref, out_ref, *, first):
    panel = feat_ref.shape[0]
    rows = out_ref.shape[0]
    step = order_ref.shape[1]
    order = order_ref[...].T
    for i in range(first // step, (first + rows) // step):
        hot = lax.broadcasted_iota(jnp.int32, (step, panel), 1) == order[:, i : i + 1]
        hot = jnp.where(hot, 1.0, 0.0).astype(BF16)
        at = i * step - first
        out_ref[at : at + step, :] = jnp.dot(
            hot, feat_ref[...], preferred_element_type=F32
        ).astype(BF16)


def reorder(order_rows, features, half):
    panel, width = features.shape
    rows = panel // HALVES
    return call(
        functools.partial(reorder_body, first=half * rows),
        [in_hbm(order_rows), in_hbm(features)],
        jax.ShapeDtypeStruct((rows, width), BF16),
        estimate=cost(2 * rows * panel * width, 4 * rows * width),
        name="reorder",
    )


def entry_body(rows_ref, cols_ref, live_ref, _, out_ref, *, bits):
    rounds, slots = rows_ref.shape[2:]
    out_ref[:, :slots] = (rows_ref[0, 0] << bits) | cols_ref[0, 0]
    for j in range(rounds):
        out_ref[j : j + 1, slots:] = jnp.full((1, 1), live_ref[0, 0, j], jnp.int32)


def entries_of(rows, cols, live, bits, after):
    rounds, slots = rows.shape[2:]
    shape = (rounds, slots + 1)
    return pl.pallas_call(
        functools.partial(entry_body, bits=bits),
        out_shape=jax.ShapeDtypeStruct(shape, jnp.int32),
        grid=(1,),
        in_specs=[
            whole_spec(rows),
            whole_spec(cols),
            pl.BlockSpec(memory_space=pltpu.SMEM),
            whole_spec(after),
        ],
        out_specs=pl.BlockSpec(shape, lambda i: (0, 0)),
        compiler_params=params(12),
        cost_estimate=cost(0, MIB),
        name="entries_of",
    )(*map(in_hbm, (rows, cols, live)), after)


def pick_body(*refs, near, count):
    options, out_ref = refs[:count], refs[-1]
    place = Place()
    for n, option in enumerate(options):

        @pl.when((place.side == n // near) & (place.low == n % near))
        def _():
            out_ref[...] = option[...]


def pick(options, near, after):
    body = functools.partial(pick_body, near=near, count=len(options))
    return call(body, [*options, *after], like(options[0]), name="pick")


def walk(entry_ref, j, slots, step):
    count = entry_ref[j, slots]

    @pl.loop(0, (count + GROUP - 1) // GROUP)
    def _(g):
        entries = [entry_ref[j, g * GROUP + t] for t in range(GROUP)]
        alive = [g * GROUP + t < count for t in range(GROUP)]
        step(j * slots + g * GROUP, entries, alive)


def forward_body(entry_ref, tiles_ref, *refs, slots, pairs, last):
    place = Place()
    xs, rest = refs[: pairs * HALVES], refs[pairs * HALVES :]
    panel_ref, acc = rest[-2:]
    blocks, block, width = panel_ref.shape
    bits = (blocks - 1).bit_length()
    if last:
        start, outs = rest[0], rest[1:-2]
        acc[pl.ds(0, blocks)] = start[...]
        acc[blocks] = jnp.zeros((block, width), F32)
    else:
        outs = rest[:-2]
        acc[...] = jnp.zeros_like(acc)
    per = blocks // HALVES
    for p in range(pairs):
        for h in range(HALVES):
            panel_ref[h * per : (h + 1) * per] = xs[p * HALVES + h][...].reshape(per, block, width)

        def step(first, entries, alive):
            terms = []
            for t in range(GROUP):
                x = panel_ref[entries[t] & (blocks - 1)]
                terms.append(jnp.dot(tiles_ref[first + t], x, preferred_element_type=F32))
            for t in range(GROUP):
                acc[jnp.where(alive[t], entries[t] >> bits, blocks)] += terms[t]

        j = place.row ^ (2 * p + (1 - place.side if last else place.side))
        walk(entry_ref, j, slots, step)
    if last:
        span = blocks // len(outs)
        for d, out in enumerate(outs):
            at = (place.rep ^ d) * span
            out[...] = acc[pl.ds(at, span)].reshape(out.shape).astype(out.dtype)
    else:
        outs[0][...] = acc[pl.ds(0, blocks)]


def forward(plan, tiles, xs, start, reps):
    block = tiles.shape[1]
    width = xs[0].shape[1]
    pairs = len(xs) // HALVES
    blocks = xs[0].shape[0] * HALVES // block
    last = start is not None
    if last:
        rows = blocks * block // reps
        outs = [jax.ShapeDtypeStruct((rows, width), BF16 if d else F32) for d in range(reps)]
    else:
        outs = [jax.ShapeDtypeStruct((blocks, block, width), F32)]
    body = functools.partial(
        forward_body, slots=plan.shape[1] - 1, pairs=pairs, last=last
    )
    got = call(
        body,
        [tiles, *xs] + ([start] if last else []),
        outs,
        scalars=(plan,),
        scratch=[pltpu.VMEM((blocks, block, width), BF16), pltpu.VMEM((blocks + 1, block, width), F32)],
        vmem=(0,),
        estimate=cost(2 * 64 * block * block * width, 12 * MIB),
        name="forward",
    )
    return got if last else got[0]


def total_body(own_ref, *refs):
    total = own_ref[...]
    for ref in refs[:-1]:
        total = total + ref[...].astype(F32)
    refs[-1][...] = total.astype(BF16)


def total_of(own, others):
    return call(total_body, [own, *others], like(own, BF16), name="total_of")


def gradient_of(agg, co, weight):
    pre = jnp.dot(agg, weight, preferred_element_type=F32)
    gate = 1.0 / (1.0 + jnp.exp(-pre))
    grad_pre = (co.astype(F32) * gate * (1.0 + pre * (1.0 - gate))).astype(BF16)
    return pre, gate, grad_pre


def two_parts(value):
    high = value.astype(BF16)
    return high, (value - high.astype(F32)).astype(BF16)


def sum_of_parts(ref, at, rows):
    return ref[at : at + rows, :].astype(F32) + ref[at + rows : at + 2 * rows, :].astype(F32)


def up_body(w_ref, co_ref, *refs, first, count):
    place = Place()
    shares, out_ref = refs[:count], refs[count]
    weight = w_ref[...]
    rows = shares[0].shape[0]
    for n, share in enumerate(shares):
        at = pl.multiple_of((place.rep ^ (first + n)) * rows, rows)
        _, _, grad_pre = gradient_of(share[...], co_ref[pl.ds(at, rows), :], weight)
        if first + n == 0:
            grad = lax.dot_general(
                share[...], grad_pre, (((0,), (0,)), ((), ())), preferred_element_type=F32
            )
            width = grad.shape[0]
            refs[count + 1][:width, :], refs[count + 1][width:, :] = two_parts(grad)
        out_ref[n] = lax.dot_general(
            weight, grad_pre, (((1,), (1,)), ((), ())), preferred_element_type=F32
        ).astype(BF16)


def up_shares(weight, cotangent, shares, first):
    rows, width = shares[0].shape
    outs = [jax.ShapeDtypeStruct((len(shares), width, rows), BF16)]
    if first == 0:
        outs.append(jax.ShapeDtypeStruct((2 * width, width), BF16))
    return call(
        functools.partial(up_body, first=first, count=len(shares)),
        [weight, cotangent, *shares],
        outs,
        estimate=cost(4 * len(shares) * rows * width * width, 2 * MIB),
        name="up_shares",
    )


def finish_body(w_ref, *refs):
    place = Place()
    shares, (hidden_ref, token_ref) = refs[:-2], refs[-2:]
    rows = shares[0].shape[0]
    for n, share in enumerate(shares):
        at = pl.multiple_of((place.rep ^ n) * rows, rows)
        pre = jnp.dot(share[...], w_ref[...], preferred_element_type=F32)
        hidden_ref[pl.ds(at, rows), :] = (pre * (1.0 / (1.0 + jnp.exp(-pre)))).astype(BF16)
    token_ref[...] = jnp.zeros_like(token_ref)


def finish(weight, shares):
    rows, width = shares[0].shape
    outs = (
        jax.ShapeDtypeStruct((rows * len(shares), width), BF16),
        jax.ShapeDtypeStruct((8, 128), jnp.int32),
    )
    return call(finish_body, [weight, *shares], outs, estimate=cost(0, 4 * MIB), name="finish")


def backward_body(entry_ref, tiles_ref, *refs, slots, keep, shape):
    refs, (out_ref, up_all, acc) = refs[:-3], refs[-3:]
    ups = refs if keep else refs[:-1]
    place = Place()
    cuts, chips, pairs, per, width, block = shape
    blocks = cuts * chips * per
    bits = (blocks - 1).bit_length()
    count, _, rows = ups[0].shape
    for m, up in enumerate(ups):
        for n in range(count):
            at = pl.multiple_of((place.rep ^ (m * count + n)) * rows, rows)
            up_all[:, pl.ds(at, rows)] = up[n]
    for p in range(pairs):
        acc[...] = jnp.zeros_like(acc)

        def step(first, entries, alive):
            terms = []
            for t in range(GROUP):
                at = pl.multiple_of((entries[t] >> bits) * block, block)
                terms.append(
                    jnp.dot(
                        up_all[:, pl.ds(at, block)],
                        tiles_ref[first + t],
                        preferred_element_type=F32,
                    )
                )
            for t in range(GROUP):
                acc[jnp.where(alive[t], entries[t] & (blocks - 1), blocks)] += terms[t]

        walk(entry_ref, 2 * p + (place.side if keep else 1 - place.side), slots, step)
        for h in range(cuts):
            for d in range(chips):
                at = ((place.chip ^ d) * cuts + h) * per
                to = ((h * chips + d) * pairs + p) * per
                out_ref[to : to + per] = acc[pl.ds(at, per)].astype(out_ref.dtype)
    if not keep:
        for n in range(2):
            out_ref[pairs * blocks + n] = refs[-1][n * width : (n + 1) * width, :]


def backward(plan, tiles, ups, pairs, chips, cuts, term=None):
    block = tiles.shape[1]
    count, width, rows = ups[0].shape
    panel = len(ups) * count * rows
    blocks = panel // block
    shape = (cuts, chips, pairs, blocks // chips // cuts, width, block)
    keep = term is None
    out_shape = (pairs * blocks + (0 if keep else 2), width, block)
    return call(
        functools.partial(backward_body, slots=plan.shape[1] - 1, keep=keep, shape=shape),
        [tiles, *ups] + ([] if keep else [term]),
        jax.ShapeDtypeStruct(out_shape, F32 if keep else BF16),
        scalars=(plan,),
        scratch=[pltpu.VMEM((width, panel), BF16), pltpu.VMEM((blocks + 1, width, block), F32)],
        vmem=(0,),
        estimate=cost(2 * 64 * block * block * width, 12 * MIB),
        name="backward",
    )


def join_body(kept_ref, given_ref, term_ref, *refs, cuts, chips):
    outs, grad = refs[:-1], refs[-1]
    place = Place()
    width = grad.shape[0]
    blocks = kept_ref.shape[0]
    mate = given_ref[blocks].astype(F32) + given_ref[blocks + 1].astype(F32)
    grad[...] = sum_of_parts(term_ref, 0, width) + mate
    per = blocks // (cuts * chips)
    for h in range(cuts):
        for d in range(chips):
            out = outs[h * chips + d]
            for b in range(per):
                n = (h * chips + d) * per + b
                out[b * width : (b + 1) * width, :] = (
                    kept_ref[n] + given_ref[n].astype(F32)
                ).astype(out.dtype)
            if h == 0:
                rows, end = width // chips, per * width
                high, low = two_parts(grad[pl.ds((place.chip ^ d) * rows, rows), :])
                if d == 0:
                    out[end : end + rows, :] = high.astype(F32) + low.astype(F32)
                else:
                    out[end : end + rows, :] = high
                    out[end + rows : end + 2 * rows, :] = low


def join(kept, given, term, cuts, chips):
    blocks, width, block = kept.shape
    rows = blocks // (cuts * chips) * width
    extra = width // chips
    outs = [
        jax.ShapeDtypeStruct(
            (rows + (0 if h else 2 * extra if d else extra), block), BF16 if d else F32
        )
        for h in range(cuts)
        for d in range(chips)
    ]
    got = call(
        functools.partial(join_body, cuts=cuts, chips=chips),
        [kept, given, term],
        outs,
        scratch=[pltpu.VMEM((width, width), F32)],
        name="join",
    )
    return [got[h * chips : (h + 1) * chips] for h in range(cuts)]


def gather_body(*refs, count, rows):
    out_ref = refs[-1]
    terms = [ref[:rows, :].astype(F32) for ref in refs[:count]]
    out_ref[:rows, :] = tree_sum(terms).astype(BF16)
    extra = (out_ref.shape[0] - rows) // 2
    if extra:
        terms = [refs[0][rows : rows + extra, :]]
        terms += [sum_of_parts(ref, rows, extra) for ref in refs[1:count]]
        high, low = two_parts(tree_sum(terms))
        out_ref[rows : rows + extra, :] = high
        out_ref[rows + extra : rows + 2 * extra, :] = low


def gather_sum(terms, after, rows):
    return call(
        functools.partial(gather_body, count=len(terms), rows=rows),
        [*terms, *after],
        like(terms[-1]),
        name="gather_sum",
    )


def owner_of(chip, core, k, reps):
    to = chip ^ k
    return 2 * to + (core ^ (to // (reps // 2) % 2))


def route_body(*refs, reps, chips, rows, pairs):
    spread, outs = refs[:reps], refs[reps + 1 :]
    place = Place()
    each = rows // pairs
    extra = (spread[0].shape[0] - rows) // 2
    if extra:
        high, low = two_parts(tree_sum([sum_of_parts(ref, rows, extra) for ref in spread]))
    for k in range(chips):
        target = owner_of(place.chip, place.core, k, reps)
        for d in range(reps):

            @pl.when(((target % reps) ^ place.rep) == d)
            def _():
                at = pl.multiple_of(target // reps // 2 * each, each)
                outs[k][:each, :] = spread[d][pl.ds(at, each), :]

        if extra:
            outs[k][each : each + extra, :] = high
            outs[k][each + extra : each + 2 * extra, :] = low


def route(spread, after, chips, rows, pairs):
    height, width = spread[0].shape
    outs = [jax.ShapeDtypeStruct((height - rows + rows // pairs, width), BF16)] * chips
    body = functools.partial(route_body, reps=len(spread), chips=chips, rows=rows, pairs=pairs)
    return call(body, [*spread, after], outs, name="route")


def hot_body(order_ref, _, out_ref, token_ref):
    panel = out_ref.shape[0]
    rows = 256
    target = order_ref[...]
    token_ref[...] = jnp.zeros_like(token_ref)

    @pl.loop(0, panel // rows)
    def _(i):
        at = pl.multiple_of(i * rows, rows)
        hot = lax.broadcasted_iota(jnp.int32, (rows, panel), 0) + at == target
        out_ref[pl.ds(at, rows), :] = jnp.where(hot, 1.0, 0.0).astype(BF16)


def inverse_hot(order_row, after):
    panel = order_row.shape[1]
    return pl.pallas_call(
        hot_body,
        out_shape=(
            pltpu.VMEM((panel, panel), BF16),
            jax.ShapeDtypeStruct((8, 128), jnp.int32),
        ),
        grid=(1,),
        in_specs=[whole_spec(order_row), pl.BlockSpec(memory_space=pl.ANY)],
        out_specs=(
            pl.BlockSpec(memory_space=pltpu.VMEM),
            pl.BlockSpec((8, 128), lambda i: (0, 0)),
        ),
        compiler_params=params(8),
        cost_estimate=cost(0, 6 * MIB),
        name="inverse_hot",
    )(order_row, after)


def restore_body(hot_ref, *refs, first, count, per, scale):
    parts, refs = refs[:count], refs[count:]
    start, (out_ref, grad_ref) = refs[:-2], refs[-2:]
    chip = lax.axis_index("section") // 2
    block = parts[0].shape[1]
    extra = (parts[0].shape[0] - per * block) // 2
    length = per * block
    grad_ref[...] = start[1][...] if start else jnp.zeros_like(grad_ref)
    columns, places = [], []
    for n, part in enumerate(parts):
        u = chip ^ (first + n)
        at = pl.multiple_of(u * extra, extra)
        grad_ref[pl.ds(at, extra), :] = sum_of_parts(part, length, extra) * scale
        columns.append(
            jnp.concatenate([part[b * block : (b + 1) * block, :] for b in range(per)], axis=1)
        )
        places.append(pl.multiple_of(u * length, length))
    rows = 512
    for i in range(out_ref.shape[0] // rows):
        span = slice(i * rows, (i + 1) * rows)
        acc = start[0][span, :] if start else None
        for n, at in enumerate(places):
            term = lax.dot_general(
                hot_ref[span, pl.ds(at, length)],
                columns[n],
                (((1,), (1,)), ((), ())),
                preferred_element_type=F32,
            )
            acc = term if acc is None else acc + term
        out_ref[span, :] = acc.astype(out_ref.dtype)


def restore(hot, parts, first, start, per, scale):
    panel = hot.shape[0]
    width = parts[0].shape[1]
    body = functools.partial(
        restore_body, first=first, count=len(parts), per=per, scale=scale
    )
    outs = (
        jax.ShapeDtypeStruct((panel, width), BF16 if start else F32),
        jax.ShapeDtypeStruct((width, width), F32),
    )
    return call(
        body,
        [hot, *parts, *start],
        outs,
        vmem=(0,),
        estimate=cost(2 * panel * panel * width, 4 * panel * width),
        name="restore",
    )


def tree_sum(terms):
    while len(terms) > 1:
        terms = [terms[i] + terms[i + 1] for i in range(0, len(terms), 2)]
    return terms[0]


def shards(features, order, tiles, tile_rows, tile_cols, live, weight, cotangent):
    reps = lax.axis_size("rep")
    sections = lax.axis_size("section")
    panel, width = features.shape
    rounds, slots, block, _ = tiles.shape[2:]
    blocks = panel // block
    chips = sections // 2
    pairs = rounds // 2
    near = reps // 2

    def over_chips(x, d):
        return lax.ppermute(x, "section", [(s, s ^ (2 * d)) for s in range(sections)])

    def over_cores(x):
        return lax.ppermute(x, "section", [(s, s ^ 1) for s in range(sections)])

    def over_reps(x, d):
        return lax.ppermute(x, "rep", [(r, r ^ d) for r in range(reps)])

    def from_owner(x, d):
        moves = []
        for r in range(reps):
            for j in range(rounds):
                source = j * reps + r
                target = (source ^ (2 * d)) ^ ((d // near) & 1)
                moves.append((source * reps + r, target * reps + r))
        return lax.ppermute(x, ("section", "rep"), moves)

    order_rows, order_row = order.reshape(panel // block, block), order.reshape(1, panel)
    owns = [reorder(order_rows, features, h) for h in range(HALVES)]
    gots = [[own] + [from_owner(own, d) for d in range(1, chips)] for own in owns]
    bits = (blocks - 1).bit_length()
    plan = entries_of(tile_rows, tile_cols, live, bits, owns[-1][:16])
    own_tiles = tiles.reshape(rounds * slots, block, block)

    mine, mate = [], []
    for p in range(pairs):
        for h in range(HALVES):
            first = 2 * p * near
            picked = pick(gots[h][first : first + 2 * near], near, [] if h else [plan])
            mine.append(picked)
            mate.append(over_cores(picked))

    started = forward(plan, own_tiles, mine, None, reps)
    own, *others = forward(plan, own_tiles, mate, started, reps)
    sent = {d: over_reps(others[d - 1], d) for d in reversed(range(1, reps))}
    aggregated = total_of(own, [sent[d] for d in range(1, reps)])
    shares = [aggregated] + [over_reps(aggregated, d) for d in range(1, reps)]

    up_early, term = up_shares(weight, cotangent, shares[:near], 0)
    ups = [up_early, *up_shares(weight, cotangent, shares[near:], near)]
    cuts = 1
    given = over_cores(backward(plan, own_tiles, ups, pairs, chips, cuts, term))
    kept = backward(plan, own_tiles, ups, pairs, chips, cuts)
    chunks = join(kept, given, term, cuts, chips)
    arrived = [[over_chips(c[d], d) for d in range(1, chips)] for c in chunks]
    late_shares = lax.optimization_barrier((shares, chunks[-1][-1]))[0]
    hidden, token = finish(weight, late_shares)
    per = blocks // chips // cuts
    height = pairs * per * width
    reduced = gather_sum([chunks[0][0], *arrived[0]], [token], height)

    def to_owner(block, k):
        moves = [(s, owner_of(s // 2, s % 2, k, reps)) for s in range(sections)]
        return lax.ppermute(block, "section", moves)

    spread = [reduced] + [over_reps(reduced, d) for d in range(1, reps)]
    hot, ready = inverse_hot(order_row, reduced)
    routed = route(spread, ready, chips, height, pairs)
    parts = [to_owner(block, k) for k, block in enumerate(routed)]
    scale = 1.0 / math.sqrt(panel * sections)
    half = chips // 2
    begun = restore(hot, parts[:half], 0, (), per, scale)
    feature_grad, weight_grad = restore(hot, parts[half:], half, begun, per, scale)
    return (hidden, weight_grad, feature_grad)


def solution(mesh):
    placed = (
        P("section", None),
        P("section"),
        P("section", "rep", None, None, None, None),
        P("section", "rep", None, None),
        P("section", "rep", None, None),
        P("section", "rep", None),
        P(),
        P("section", None),
    )
    return jax.shard_map(
        shards,
        mesh=mesh,
        in_specs=placed,
        out_specs=(P("section", None), P(), P("section", None)),
        check_vma=False,
    )
```

```python
import functools
import math

import jax
import jax.numpy as jnp
from jax import lax
from jax.experimental import pallas as pl
from jax.experimental.pallas import tpu as pltpu
from jax.sharding import PartitionSpec as P

F32 = jnp.float32
BF16 = jnp.bfloat16
MIB = 1 << 20


def params(mib):
    return pltpu.CompilerParams(vmem_limit_bytes=mib * MIB)


def cost(flops, nbytes):
    return pl.CostEstimate(flops=int(flops), bytes_accessed=int(nbytes), transcendentals=0)


def whole_spec(array):
    zeros = (0,) * array.ndim
    return pl.BlockSpec(array.shape, lambda *_: zeros)


HALVES = 2
GROUP = 16


class Place:
    def __init__(self):
        reps = lax.axis_size("rep")
        section = lax.axis_index("section")
        self.rep = lax.axis_index("rep")
        self.chip = section // 2
        self.core = section % 2
        self.side = (section + self.rep) % 2
        self.row = section // reps
        self.low = ((section % reps) // 2) ^ (self.rep // 2)


def in_vmem(array):
    return pltpu.with_memory_space_constraint(array, pltpu.VMEM)


def in_hbm(array):
    return pltpu.with_memory_space_constraint(array, pltpu.HBM)


def call(
    body, operands, outs, scalars=(), scratch=(), blocked=(), results=(), mib=12, estimate=None, name=None
):
    in_place = pl.BlockSpec(memory_space=pltpu.VMEM)
    many = isinstance(outs, (list, tuple))
    outs = list(outs) if many else [outs]
    got = pl.pallas_call(
        body,
        out_shape=[
            out if n in results else pltpu.VMEM(out.shape, out.dtype) for n, out in enumerate(outs)
        ],
        grid_spec=pltpu.PrefetchScalarGridSpec(
            num_scalar_prefetch=len(scalars),
            grid=(1,),
            in_specs=[
                whole_spec(x) if n in blocked else in_place for n, x in enumerate(operands)
            ],
            out_specs=[
                whole_spec(out) if n in results else in_place for n, out in enumerate(outs)
            ],
            scratch_shapes=list(scratch),
        ),
        compiler_params=params(mib),
        cost_estimate=estimate or cost(0, MIB),
        name=name,
    )(*scalars, *[x if n in blocked else in_vmem(x) for n, x in enumerate(operands)])
    return got if many else got[0]


def like(array, dtype=None):
    return jax.ShapeDtypeStruct(array.shape, dtype or array.dtype)


def reorder_body(order_ref, feat_ref, out_ref, *, first):
    panel = feat_ref.shape[0]
    rows = out_ref.shape[0]
    step = order_ref.shape[1]
    order = order_ref[...].T
    for i in range(first // step, (first + rows) // step):
        hot = lax.broadcasted_iota(jnp.int32, (step, panel), 1) == order[:, i : i + 1]
        hot = jnp.where(hot, 1.0, 0.0).astype(BF16)
        at = i * step - first
        out_ref[at : at + step, :] = jnp.dot(
            hot, feat_ref[...], preferred_element_type=F32
        ).astype(BF16)


def reorder(order_rows, features, half):
    panel, width = features.shape
    rows = panel // HALVES
    return call(
        functools.partial(reorder_body, first=half * rows),
        [in_hbm(order_rows), in_hbm(features)],
        jax.ShapeDtypeStruct((rows, width), BF16),
        blocked=(0, 1),
        estimate=cost(2 * rows * panel * width, 4 * rows * width),
        name="reorder",
    )


def entry_body(rows_ref, cols_ref, live_ref, _, out_ref, *, bits):
    rounds, slots = rows_ref.shape[2:]
    out_ref[:, :slots] = (rows_ref[0, 0] << bits) | cols_ref[0, 0]
    for j in range(rounds):
        out_ref[j : j + 1, slots:] = jnp.full((1, 1), live_ref[0, 0, j], jnp.int32)


def entries_of(rows, cols, live, bits, after):
    rounds, slots = rows.shape[2:]
    shape = (rounds, slots + 1)
    return pl.pallas_call(
        functools.partial(entry_body, bits=bits),
        out_shape=jax.ShapeDtypeStruct(shape, jnp.int32),
        grid=(1,),
        in_specs=[
            whole_spec(rows),
            whole_spec(cols),
            pl.BlockSpec(memory_space=pltpu.SMEM),
            whole_spec(after),
        ],
        out_specs=pl.BlockSpec(shape, lambda i: (0, 0)),
        compiler_params=params(12),
        cost_estimate=cost(0, MIB),
        name="entries_of",
    )(*map(in_hbm, (rows, cols, live)), after)


def pick_body(*refs, near, count):
    options, out_ref = refs[:count], refs[-1]
    place = Place()
    for n, option in enumerate(options):

        @pl.when((place.side == n // near) & (place.low == n % near))
        def _():
            out_ref[...] = option[...]


def pick(options, near, after):
    body = functools.partial(pick_body, near=near, count=len(options))
    return call(body, [*options, *after], like(options[0]), name="pick")


def walk(entry_ref, j, slots, step):
    count = entry_ref[j, slots]

    @pl.loop(0, (count + GROUP - 1) // GROUP)
    def _(g):
        entries = [entry_ref[j, g * GROUP + t] for t in range(GROUP)]
        alive = [g * GROUP + t < count for t in range(GROUP)]
        step(j * slots + g * GROUP, entries, alive)


def forward_body(entry_ref, tiles_ref, *refs, slots, pairs, last):
    place = Place()
    xs, rest = refs[: pairs * HALVES], refs[pairs * HALVES :]
    panel_ref, acc = rest[-2:]
    blocks, block, width = panel_ref.shape
    bits = (blocks - 1).bit_length()
    if last:
        start, outs = rest[0], rest[1:-2]
        acc[pl.ds(0, blocks)] = start[...]
        acc[blocks] = jnp.zeros((block, width), F32)
    else:
        outs = rest[:-2]
        acc[...] = jnp.zeros_like(acc)
    per = blocks // HALVES
    for p in range(pairs):
        for h in range(HALVES):
            panel_ref[h * per : (h + 1) * per] = xs[p * HALVES + h][...].reshape(per, block, width)

        def step(first, entries, alive):
            terms = []
            for t in range(GROUP):
                x = panel_ref[entries[t] & (blocks - 1)]
                terms.append(jnp.dot(tiles_ref[first + t], x, preferred_element_type=F32))
            for t in range(GROUP):
                acc[jnp.where(alive[t], entries[t] >> bits, blocks)] += terms[t]

        j = place.row ^ (2 * p + (1 - place.side if last else place.side))
        walk(entry_ref, j, slots, step)
    if last:
        span = blocks // len(outs)
        for d, out in enumerate(outs):
            at = (place.rep ^ d) * span
            out[...] = acc[pl.ds(at, span)].reshape(out.shape).astype(out.dtype)
    else:
        outs[0][...] = acc[pl.ds(0, blocks)]


def forward(plan, tiles, xs, start, reps):
    block = tiles.shape[1]
    width = xs[0].shape[1]
    pairs = len(xs) // HALVES
    blocks = xs[0].shape[0] * HALVES // block
    last = start is not None
    if last:
        rows = blocks * block // reps
        outs = [jax.ShapeDtypeStruct((rows, width), BF16 if d else F32) for d in range(reps)]
    else:
        outs = [jax.ShapeDtypeStruct((blocks, block, width), F32)]
    body = functools.partial(
        forward_body, slots=plan.shape[1] - 1, pairs=pairs, last=last
    )
    got = call(
        body,
        [tiles, *xs] + ([start] if last else []),
        outs,
        scalars=(plan,),
        scratch=[pltpu.VMEM((blocks, block, width), BF16), pltpu.VMEM((blocks + 1, block, width), F32)],
        estimate=cost(2 * 64 * block * block * width, 12 * MIB),
        name="forward",
    )
    return got if last else got[0]


def total_body(own_ref, *refs):
    total = own_ref[...]
    for ref in refs[:-1]:
        total = total + ref[...].astype(F32)
    refs[-1][...] = total.astype(BF16)


def total_of(own, others):
    return call(total_body, [own, *others], like(own, BF16), name="total_of")


def gradient_of(agg, co, weight):
    pre = jnp.dot(agg, weight, preferred_element_type=F32)
    gate = 1.0 / (1.0 + jnp.exp(-pre))
    grad_pre = (co.astype(F32) * gate * (1.0 + pre * (1.0 - gate))).astype(BF16)
    return pre, gate, grad_pre


def two_parts(value):
    high = value.astype(BF16)
    return high, (value - high.astype(F32)).astype(BF16)


def sum_of_parts(ref, at, rows):
    return ref[at : at + rows, :].astype(F32) + ref[at + rows : at + 2 * rows, :].astype(F32)


def up_body(w_ref, co_ref, *refs, first, count):
    place = Place()
    shares, out_ref = refs[:count], refs[count]
    weight = w_ref[...]
    rows = shares[0].shape[0]
    for n, share in enumerate(shares):
        at = pl.multiple_of((place.rep ^ (first + n)) * rows, rows)
        _, _, grad_pre = gradient_of(share[...], co_ref[pl.ds(at, rows), :], weight)
        if first + n == 0:
            grad = lax.dot_general(
                share[...], grad_pre, (((0,), (0,)), ((), ())), preferred_element_type=F32
            )
            width = grad.shape[0]
            refs[count + 1][:width, :], refs[count + 1][width:, :] = two_parts(grad)
        out_ref[n] = lax.dot_general(
            weight, grad_pre, (((1,), (1,)), ((), ())), preferred_element_type=F32
        ).astype(BF16)


def up_shares(weight, cotangent, shares, first):
    rows, width = shares[0].shape
    outs = [jax.ShapeDtypeStruct((len(shares), width, rows), BF16)]
    if first == 0:
        outs.append(jax.ShapeDtypeStruct((2 * width, width), BF16))
    return call(
        functools.partial(up_body, first=first, count=len(shares)),
        [weight, cotangent, *shares],
        outs,
        estimate=cost(4 * len(shares) * rows * width * width, 2 * MIB),
        name="up_shares",
    )


def finish_body(w_ref, *refs):
    place = Place()
    shares, (hidden_ref, token_ref) = refs[:-2], refs[-2:]
    rows = shares[0].shape[0]
    for n, share in enumerate(shares):
        at = pl.multiple_of((place.rep ^ n) * rows, rows)
        pre = jnp.dot(share[...], w_ref[...], preferred_element_type=F32)
        hidden_ref[pl.ds(at, rows), :] = (pre * (1.0 / (1.0 + jnp.exp(-pre)))).astype(BF16)
    token_ref[...] = jnp.zeros_like(token_ref)


def finish(weight, shares):
    rows, width = shares[0].shape
    outs = (
        jax.ShapeDtypeStruct((rows * len(shares), width), BF16),
        jax.ShapeDtypeStruct((8, 128), jnp.int32),
    )
    return call(finish_body, [weight, *shares], outs, results=(0,), estimate=cost(0, 4 * MIB), name="finish")


def backward_body(entry_ref, tiles_ref, *refs, slots, keep, shape):
    refs, (out_ref, up_all, acc) = refs[:-3], refs[-3:]
    ups = refs if keep else refs[:-1]
    place = Place()
    cuts, chips, pairs, per, width, block = shape
    blocks = cuts * chips * per
    bits = (blocks - 1).bit_length()
    count, _, rows = ups[0].shape
    for m, up in enumerate(ups):
        for n in range(count):
            at = pl.multiple_of((place.rep ^ (m * count + n)) * rows, rows)
            up_all[:, pl.ds(at, rows)] = up[n]
    for p in range(pairs):
        acc[...] = jnp.zeros_like(acc)

        def step(first, entries, alive):
            terms = []
            for t in range(GROUP):
                at = pl.multiple_of((entries[t] >> bits) * block, block)
                terms.append(
                    jnp.dot(
                        up_all[:, pl.ds(at, block)],
                        tiles_ref[first + t],
                        preferred_element_type=F32,
                    )
                )
            for t in range(GROUP):
                acc[jnp.where(alive[t], entries[t] & (blocks - 1), blocks)] += terms[t]

        walk(entry_ref, 2 * p + (place.side if keep else 1 - place.side), slots, step)
        for h in range(cuts):
            for d in range(chips):
                at = ((place.chip ^ d) * cuts + h) * per
                to = ((h * chips + d) * pairs + p) * per
                out_ref[to : to + per] = acc[pl.ds(at, per)].astype(out_ref.dtype)
    if not keep:
        for n in range(2):
            out_ref[pairs * blocks + n] = refs[-1][n * width : (n + 1) * width, :]


def backward(plan, tiles, ups, pairs, chips, cuts, term=None):
    block = tiles.shape[1]
    count, width, rows = ups[0].shape
    panel = len(ups) * count * rows
    blocks = panel // block
    shape = (cuts, chips, pairs, blocks // chips // cuts, width, block)
    keep = term is None
    out_shape = (pairs * blocks + (0 if keep else 2), width, block)
    return call(
        functools.partial(backward_body, slots=plan.shape[1] - 1, keep=keep, shape=shape),
        [tiles, *ups] + ([] if keep else [term]),
        jax.ShapeDtypeStruct(out_shape, F32 if keep else BF16),
        scalars=(plan,),
        scratch=[pltpu.VMEM((width, panel), BF16), pltpu.VMEM((blocks + 1, width, block), F32)],
        estimate=cost(2 * 64 * block * block * width, 12 * MIB),
        name="backward",
    )


def join_body(kept_ref, given_ref, term_ref, *refs, cuts, chips):
    outs, grad = refs[:-1], refs[-1]
    place = Place()
    width = grad.shape[0]
    blocks = kept_ref.shape[0]
    mate = given_ref[blocks].astype(F32) + given_ref[blocks + 1].astype(F32)
    grad[...] = sum_of_parts(term_ref, 0, width) + mate
    per = blocks // (cuts * chips)
    for h in range(cuts):
        for d in range(chips):
            out = outs[h * chips + d]
            for b in range(per):
                n = (h * chips + d) * per + b
                out[b * width : (b + 1) * width, :] = (
                    kept_ref[n] + given_ref[n].astype(F32)
                ).astype(out.dtype)
            if h == 0:
                rows, end = width // chips, per * width
                high, low = two_parts(grad[pl.ds((place.chip ^ d) * rows, rows), :])
                if d == 0:
                    out[end : end + rows, :] = high.astype(F32) + low.astype(F32)
                else:
                    out[end : end + rows, :] = high
                    out[end + rows : end + 2 * rows, :] = low


def join(kept, given, term, cuts, chips):
    blocks, width, block = kept.shape
    rows = blocks // (cuts * chips) * width
    extra = width // chips
    outs = [
        jax.ShapeDtypeStruct(
            (rows + (0 if h else 2 * extra if d else extra), block), BF16 if d else F32
        )
        for h in range(cuts)
        for d in range(chips)
    ]
    got = call(
        functools.partial(join_body, cuts=cuts, chips=chips),
        [kept, given, term],
        outs,
        scratch=[pltpu.VMEM((width, width), F32)],
        name="join",
    )
    return [got[h * chips : (h + 1) * chips] for h in range(cuts)]


def gather_body(*refs, count, rows):
    out_ref = refs[-1]
    terms = [ref[:rows, :].astype(F32) for ref in refs[:count]]
    out_ref[:rows, :] = tree_sum(terms).astype(BF16)
    extra = (out_ref.shape[0] - rows) // 2
    if extra:
        terms = [refs[0][rows : rows + extra, :]]
        terms += [sum_of_parts(ref, rows, extra) for ref in refs[1:count]]
        high, low = two_parts(tree_sum(terms))
        out_ref[rows : rows + extra, :] = high
        out_ref[rows + extra : rows + 2 * extra, :] = low


def gather_sum(terms, after, rows):
    return call(
        functools.partial(gather_body, count=len(terms), rows=rows),
        [*terms, *after],
        like(terms[-1]),
        name="gather_sum",
    )


def owner_of(chip, core, k, reps):
    to = chip ^ k
    return 2 * to + (core ^ (to // (reps // 2) % 2))


def route_body(*refs, reps, chips, rows, pairs):
    spread, outs = refs[:reps], refs[reps + 1 :]
    place = Place()
    each = rows // pairs
    extra = (spread[0].shape[0] - rows) // 2
    if extra:
        high, low = two_parts(tree_sum([sum_of_parts(ref, rows, extra) for ref in spread]))
    for k in range(chips):
        target = owner_of(place.chip, place.core, k, reps)
        for d in range(reps):

            @pl.when(((target % reps) ^ place.rep) == d)
            def _():
                at = pl.multiple_of(target // reps // 2 * each, each)
                outs[k][:each, :] = spread[d][pl.ds(at, each), :]

        if extra:
            outs[k][each : each + extra, :] = high
            outs[k][each + extra : each + 2 * extra, :] = low


def route(spread, after, chips, rows, pairs):
    height, width = spread[0].shape
    outs = [jax.ShapeDtypeStruct((height - rows + rows // pairs, width), BF16)] * chips
    body = functools.partial(route_body, reps=len(spread), chips=chips, rows=rows, pairs=pairs)
    return call(body, [*spread, after], outs, name="route")


def hot_body(order_ref, _, out_ref, token_ref):
    panel = out_ref.shape[0]
    rows = 256
    target = order_ref[...]
    token_ref[...] = jnp.zeros_like(token_ref)

    @pl.loop(0, panel // rows)
    def _(i):
        at = pl.multiple_of(i * rows, rows)
        hot = lax.broadcasted_iota(jnp.int32, (rows, panel), 0) + at == target
        out_ref[pl.ds(at, rows), :] = jnp.where(hot, 1.0, 0.0).astype(BF16)


def inverse_hot(order_row, after):
    panel = order_row.shape[1]
    return pl.pallas_call(
        hot_body,
        out_shape=(
            pltpu.VMEM((panel, panel), BF16),
            jax.ShapeDtypeStruct((8, 128), jnp.int32),
        ),
        grid=(1,),
        in_specs=[whole_spec(order_row), pl.BlockSpec(memory_space=pl.ANY)],
        out_specs=(
            pl.BlockSpec(memory_space=pltpu.VMEM),
            pl.BlockSpec((8, 128), lambda i: (0, 0)),
        ),
        compiler_params=params(8),
        cost_estimate=cost(0, 6 * MIB),
        name="inverse_hot",
    )(order_row, after)


def restore_body(hot_ref, *refs, first, count, per, scale):
    parts, refs = refs[:count], refs[count:]
    start, (out_ref, grad_ref) = refs[:-2], refs[-2:]
    chip = lax.axis_index("section") // 2
    block = parts[0].shape[1]
    extra = (parts[0].shape[0] - per * block) // 2
    length = per * block
    grad_ref[...] = start[1][...] if start else jnp.zeros_like(grad_ref)
    columns, places = [], []
    for n, part in enumerate(parts):
        u = chip ^ (first + n)
        at = pl.multiple_of(u * extra, extra)
        grad_ref[pl.ds(at, extra), :] = sum_of_parts(part, length, extra) * scale
        columns.append(
            jnp.concatenate([part[b * block : (b + 1) * block, :] for b in range(per)], axis=1)
        )
        places.append(pl.multiple_of(u * length, length))
    rows = 512
    for i in range(out_ref.shape[0] // rows):
        span = slice(i * rows, (i + 1) * rows)
        acc = start[0][span, :] if start else None
        for n, at in enumerate(places):
            term = lax.dot_general(
                hot_ref[span, pl.ds(at, length)],
                columns[n],
                (((1,), (1,)), ((), ())),
                preferred_element_type=F32,
            )
            acc = term if acc is None else acc + term
        out_ref[span, :] = acc.astype(out_ref.dtype)


def restore(hot, parts, first, start, per, scale):
    panel = hot.shape[0]
    width = parts[0].shape[1]
    body = functools.partial(
        restore_body, first=first, count=len(parts), per=per, scale=scale
    )
    outs = (
        jax.ShapeDtypeStruct((panel, width), BF16 if start else F32),
        jax.ShapeDtypeStruct((width, width), F32),
    )
    return call(
        body,
        [hot, *parts, *start],
        outs,
        results=(0, 1) if start else (),
        estimate=cost(2 * panel * panel * width, 4 * panel * width),
        name="restore",
    )


def tree_sum(terms):
    while len(terms) > 1:
        terms = [terms[i] + terms[i + 1] for i in range(0, len(terms), 2)]
    return terms[0]


def shards(features, order, tiles, tile_rows, tile_cols, live, weight, cotangent):
    reps = lax.axis_size("rep")
    sections = lax.axis_size("section")
    panel, width = features.shape
    rounds, slots, block, _ = tiles.shape[2:]
    blocks = panel // block
    chips = sections // 2
    pairs = rounds // 2
    near = reps // 2

    def over_chips(x, d):
        return lax.ppermute(x, "section", [(s, s ^ (2 * d)) for s in range(sections)])

    def over_cores(x):
        return lax.ppermute(x, "section", [(s, s ^ 1) for s in range(sections)])

    def over_reps(x, d):
        return lax.ppermute(x, "rep", [(r, r ^ d) for r in range(reps)])

    def from_owner(x, d):
        moves = []
        for r in range(reps):
            for j in range(rounds):
                source = j * reps + r
                target = (source ^ (2 * d)) ^ ((d // near) & 1)
                moves.append((source * reps + r, target * reps + r))
        return lax.ppermute(x, ("section", "rep"), moves)

    order_rows, order_row = order.reshape(panel // block, block), order.reshape(1, panel)
    owns = [reorder(order_rows, features, h) for h in range(HALVES)]
    gots = [[own] + [from_owner(own, d) for d in range(1, chips)] for own in owns]
    bits = (blocks - 1).bit_length()
    plan = entries_of(tile_rows, tile_cols, live, bits, owns[-1][:16])
    own_tiles = tiles.reshape(rounds * slots, block, block)

    mine, mate = [], []
    for p in range(pairs):
        for h in range(HALVES):
            first = 2 * p * near
            picked = pick(gots[h][first : first + 2 * near], near, [] if h else [plan])
            mine.append(picked)
            mate.append(over_cores(picked))

    started = forward(plan, own_tiles, mine, None, reps)
    own, *others = forward(plan, own_tiles, mate, started, reps)
    sent = {d: over_reps(others[d - 1], d) for d in reversed(range(1, reps))}
    aggregated = total_of(own, [sent[d] for d in range(1, reps)])
    shares = [aggregated] + [over_reps(aggregated, d) for d in range(1, reps)]

    up_early, term = up_shares(weight, cotangent, shares[:near], 0)
    ups = [up_early, *up_shares(weight, cotangent, shares[near:], near)]
    cuts = 1
    given = over_cores(backward(plan, own_tiles, ups, pairs, chips, cuts, term))
    kept = backward(plan, own_tiles, ups, pairs, chips, cuts)
    chunks = join(kept, given, term, cuts, chips)
    arrived = [[over_chips(c[d], d) for d in range(1, chips)] for c in chunks]
    late_shares = lax.optimization_barrier((shares, chunks[-1][-1]))[0]
    hidden, token = finish(weight, late_shares)
    per = blocks // chips // cuts
    height = pairs * per * width
    reduced = gather_sum([chunks[0][0], *arrived[0]], [token], height)

    def to_owner(block, k):
        moves = [(s, owner_of(s // 2, s % 2, k, reps)) for s in range(sections)]
        return lax.ppermute(block, "section", moves)

    spread = [reduced] + [over_reps(reduced, d) for d in range(1, reps)]
    hot, ready = inverse_hot(order_row, reduced)
    routed = route(spread, ready, chips, height, pairs)
    parts = [to_owner(block, k) for k, block in enumerate(routed)]
    scale = 1.0 / math.sqrt(panel * sections)
    half = chips // 2
    begun = restore(hot, parts[:half], 0, (), per, scale)
    feature_grad, weight_grad = restore(hot, parts[half:], half, begun, per, scale)
    return (hidden, weight_grad, feature_grad)


def solution(mesh):
    placed = (
        P("section", None),
        P("section"),
        P("section", "rep", None, None, None, None),
        P("section", "rep", None, None),
        P("section", "rep", None, None),
        P("section", "rep", None),
        P(),
        P("section", None),
    )
    return jax.shard_map(
        shards,
        mesh=mesh,
        in_specs=placed,
        out_specs=(P("section", None), P(), P("section", None)),
        check_vma=False,
    )
```

```python
import functools
import math

import jax
import jax.numpy as jnp
from jax import lax
from jax.experimental import pallas as pl
from jax.experimental.pallas import tpu as pltpu
from jax.sharding import PartitionSpec as P

F32 = jnp.float32
BF16 = jnp.bfloat16
MIB = 1 << 20


def params(mib):
    return pltpu.CompilerParams(vmem_limit_bytes=mib * MIB)


def cost(flops, nbytes):
    return pl.CostEstimate(flops=int(flops), bytes_accessed=int(nbytes), transcendentals=0)


def whole_spec(array):
    zeros = (0,) * array.ndim
    return pl.BlockSpec(array.shape, lambda *_: zeros)


HALVES = 2
GROUP = 16


class Place:
    def __init__(self):
        reps = lax.axis_size("rep")
        section = lax.axis_index("section")
        self.rep = lax.axis_index("rep")
        self.chip = section // 2
        self.core = section % 2
        self.side = (section + self.rep) % 2
        self.row = section // reps
        self.low = ((section % reps) // 2) ^ (self.rep // 2)


def row_spec(array, steps):
    rest = (0,) * (array.ndim - 1)
    return pl.BlockSpec((array.shape[0] // steps, *array.shape[1:]), lambda i, *_: (i, *rest))


def in_vmem(array):
    return pltpu.with_memory_space_constraint(array, pltpu.VMEM)


def in_hbm(array):
    return pltpu.with_memory_space_constraint(array, pltpu.HBM)


def call(
    body, operands, outs, scalars=(), scratch=(), blocked=(), results=(), steps=1, mib=12,
    estimate=None, name=None
):
    in_place = pl.BlockSpec(memory_space=pltpu.VMEM)
    many = isinstance(outs, (list, tuple))
    outs = list(outs) if many else [outs]
    got = pl.pallas_call(
        body,
        out_shape=[
            out if n in results else pltpu.VMEM(out.shape, out.dtype) for n, out in enumerate(outs)
        ],
        grid_spec=pltpu.PrefetchScalarGridSpec(
            num_scalar_prefetch=len(scalars),
            grid=(steps,),
            in_specs=[
                whole_spec(x) if n in blocked else in_place for n, x in enumerate(operands)
            ],
            out_specs=[
                (row_spec(out, steps) if n == 0 else whole_spec(out)) if n in results else in_place
                for n, out in enumerate(outs)
            ],
            scratch_shapes=list(scratch),
        ),
        compiler_params=params(mib),
        cost_estimate=estimate or cost(0, MIB),
        name=name,
    )(*scalars, *[x if n in blocked else in_vmem(x) for n, x in enumerate(operands)])
    return got if many else got[0]


def like(array, dtype=None):
    return jax.ShapeDtypeStruct(array.shape, dtype or array.dtype)


def reorder_body(order_ref, feat_ref, out_ref, *kept, first):
    if kept:
        kept[0][...], kept[1][...] = order_ref[...], feat_ref[...]
    panel = feat_ref.shape[0]
    rows = out_ref.shape[0]
    step = order_ref.shape[1]
    order = order_ref[...].T
    for i in range(first // step, (first + rows) // step):
        hot = lax.broadcasted_iota(jnp.int32, (step, panel), 1) == order[:, i : i + 1]
        hot = jnp.where(hot, 1.0, 0.0).astype(BF16)
        at = i * step - first
        out_ref[at : at + step, :] = jnp.dot(
            hot, feat_ref[...], preferred_element_type=F32
        ).astype(BF16)


def reorder(order_rows, features):
    panel, width = features.shape
    rows = panel // HALVES
    half = jax.ShapeDtypeStruct((rows, width), BF16)
    halves, kept = [], [in_hbm(order_rows), in_hbm(features)]
    for h in range(HALVES):
        got = call(
            functools.partial(reorder_body, first=h * rows),
            kept,
            [half] if h else [half, like(order_rows), like(features)],
            blocked=() if h else (0, 1),
            estimate=cost(2 * rows * panel * width, 4 * rows * width),
            name="reorder",
        )
        halves.append(got[0])
        kept = kept if h else got[1:]
    return halves


def entry_body(rows_ref, cols_ref, live_ref, _, out_ref, *, bits):
    rounds, slots = rows_ref.shape[2:]
    out_ref[:, :slots] = (rows_ref[0, 0] << bits) | cols_ref[0, 0]
    for j in range(rounds):
        out_ref[j : j + 1, slots:] = jnp.full((1, 1), live_ref[0, 0, j], jnp.int32)


def entries_of(rows, cols, live, bits, after):
    rounds, slots = rows.shape[2:]
    shape = (rounds, slots + 1)
    return pl.pallas_call(
        functools.partial(entry_body, bits=bits),
        out_shape=jax.ShapeDtypeStruct(shape, jnp.int32),
        grid=(1,),
        in_specs=[
            whole_spec(rows),
            whole_spec(cols),
            pl.BlockSpec(memory_space=pltpu.SMEM),
            whole_spec(after),
        ],
        out_specs=pl.BlockSpec(shape, lambda i: (0, 0)),
        compiler_params=params(12),
        cost_estimate=cost(0, MIB),
        name="entries_of",
    )(*map(in_hbm, (rows, cols, live)), after)


def pick_body(*refs, near, count):
    options, out_ref = refs[:count], refs[-1]
    place = Place()
    for n, option in enumerate(options):

        @pl.when((place.side == n // near) & (place.low == n % near))
        def _():
            out_ref[...] = option[...]


def pick(options, near, after):
    body = functools.partial(pick_body, near=near, count=len(options))
    return call(body, [*options, *after], like(options[0]), name="pick")


def walk(entry_ref, j, slots, step):
    count = entry_ref[j, slots]

    @pl.loop(0, (count + GROUP - 1) // GROUP)
    def _(g):
        entries = [entry_ref[j, g * GROUP + t] for t in range(GROUP)]
        alive = [g * GROUP + t < count for t in range(GROUP)]
        step(j * slots + g * GROUP, entries, alive)


def forward_body(entry_ref, tiles_ref, *refs, slots, pairs, last):
    place = Place()
    xs, rest = refs[: pairs * HALVES], refs[pairs * HALVES :]
    panel_ref, acc = rest[-2:]
    blocks, block, width = panel_ref.shape
    bits = (blocks - 1).bit_length()
    if last:
        start, outs = rest[0], rest[1:-2]
        acc[pl.ds(0, blocks)] = start[...]
        acc[blocks] = jnp.zeros((block, width), F32)
    else:
        outs = rest[:-2]
        acc[...] = jnp.zeros_like(acc)
    per = blocks // HALVES
    for p in range(pairs):
        for h in range(HALVES):
            panel_ref[h * per : (h + 1) * per] = xs[p * HALVES + h][...].reshape(per, block, width)

        def step(first, entries, alive):
            terms = []
            for t in range(GROUP):
                x = panel_ref[entries[t] & (blocks - 1)]
                terms.append(jnp.dot(tiles_ref[first + t], x, preferred_element_type=F32))
            for t in range(GROUP):
                acc[jnp.where(alive[t], entries[t] >> bits, blocks)] += terms[t]

        j = place.row ^ (2 * p + (1 - place.side if last else place.side))
        walk(entry_ref, j, slots, step)
    if last:
        span = blocks // len(outs)
        for d, out in enumerate(outs):
            at = (place.rep ^ d) * span
            out[...] = acc[pl.ds(at, span)].reshape(out.shape).astype(out.dtype)
    else:
        outs[0][...] = acc[pl.ds(0, blocks)]


def forward(plan, tiles, xs, start, reps):
    block = tiles.shape[1]
    width = xs[0].shape[1]
    pairs = len(xs) // HALVES
    blocks = xs[0].shape[0] * HALVES // block
    last = start is not None
    if last:
        rows = blocks * block // reps
        outs = [jax.ShapeDtypeStruct((rows, width), BF16 if d else F32) for d in range(reps)]
    else:
        outs = [jax.ShapeDtypeStruct((blocks, block, width), F32)]
    body = functools.partial(
        forward_body, slots=plan.shape[1] - 1, pairs=pairs, last=last
    )
    got = call(
        body,
        [tiles, *xs] + ([start] if last else []),
        outs,
        scalars=(plan,),
        scratch=[pltpu.VMEM((blocks, block, width), BF16), pltpu.VMEM((blocks + 1, block, width), F32)],
        estimate=cost(2 * 64 * block * block * width, 12 * MIB),
        name="forward",
    )
    return got if last else got[0]


def total_body(own_ref, *refs):
    total = own_ref[...]
    for ref in refs[:-1]:
        total = total + ref[...].astype(F32)
    refs[-1][...] = total.astype(BF16)


def total_of(own, others):
    return call(total_body, [own, *others], like(own, BF16), name="total_of")


def gradient_of(agg, co, weight):
    pre = jnp.dot(agg, weight, preferred_element_type=F32)
    gate = 1.0 / (1.0 + jnp.exp(-pre))
    grad_pre = (co.astype(F32) * gate * (1.0 + pre * (1.0 - gate))).astype(BF16)
    return pre, gate, grad_pre


def two_parts(value):
    high = value.astype(BF16)
    return high, (value - high.astype(F32)).astype(BF16)


def sum_of_parts(ref, at, rows):
    return ref[at : at + rows, :].astype(F32) + ref[at + rows : at + 2 * rows, :].astype(F32)


def up_body(w_ref, co_ref, *refs, first, count):
    place = Place()
    shares, out_ref = refs[:count], refs[count]
    weight = w_ref[...]
    rows = shares[0].shape[0]
    for n, share in enumerate(shares):
        at = pl.multiple_of((place.rep ^ (first + n)) * rows, rows)
        _, _, grad_pre = gradient_of(share[...], co_ref[pl.ds(at, rows), :], weight)
        if first + n == 0:
            grad = lax.dot_general(
                share[...], grad_pre, (((0,), (0,)), ((), ())), preferred_element_type=F32
            )
            width = grad.shape[0]
            refs[count + 1][:width, :], refs[count + 1][width:, :] = two_parts(grad)
        out_ref[n] = lax.dot_general(
            weight, grad_pre, (((1,), (1,)), ((), ())), preferred_element_type=F32
        ).astype(BF16)


def up_shares(weight, cotangent, shares, first):
    rows, width = shares[0].shape
    outs = [jax.ShapeDtypeStruct((len(shares), width, rows), BF16)]
    if first == 0:
        outs.append(jax.ShapeDtypeStruct((2 * width, width), BF16))
    return call(
        functools.partial(up_body, first=first, count=len(shares)),
        [weight, cotangent, *shares],
        outs,
        estimate=cost(4 * len(shares) * rows * width * width, 2 * MIB),
        name="up_shares",
    )


def finish_body(w_ref, *refs):
    place = Place()
    shares, (hidden_ref, token_ref) = refs[:-2], refs[-2:]
    rows = shares[0].shape[0]
    for n, share in enumerate(shares):
        at = pl.multiple_of((place.rep ^ n) * rows, rows)
        pre = jnp.dot(share[...], w_ref[...], preferred_element_type=F32)
        hidden_ref[pl.ds(at, rows), :] = (pre * (1.0 / (1.0 + jnp.exp(-pre)))).astype(BF16)
    token_ref[...] = jnp.zeros_like(token_ref)


def finish(weight, shares):
    rows, width = shares[0].shape
    outs = (
        jax.ShapeDtypeStruct((rows * len(shares), width), BF16),
        jax.ShapeDtypeStruct((8, 128), jnp.int32),
    )
    return call(finish_body, [weight, *shares], outs, results=(0,), estimate=cost(0, 4 * MIB), name="finish")


def backward_body(entry_ref, tiles_ref, *refs, slots, keep, shape):
    refs, (out_ref, up_all, acc) = refs[:-3], refs[-3:]
    ups = refs if keep else refs[:-1]
    place = Place()
    cuts, chips, pairs, per, width, block = shape
    blocks = cuts * chips * per
    bits = (blocks - 1).bit_length()
    count, _, rows = ups[0].shape
    for m, up in enumerate(ups):
        for n in range(count):
            at = pl.multiple_of((place.rep ^ (m * count + n)) * rows, rows)
            up_all[:, pl.ds(at, rows)] = up[n]
    for p in range(pairs):
        acc[...] = jnp.zeros_like(acc)

        def step(first, entries, alive):
            terms = []
            for t in range(GROUP):
                at = pl.multiple_of((entries[t] >> bits) * block, block)
                terms.append(
                    jnp.dot(
                        up_all[:, pl.ds(at, block)],
                        tiles_ref[first + t],
                        preferred_element_type=F32,
                    )
                )
            for t in range(GROUP):
                acc[jnp.where(alive[t], entries[t] & (blocks - 1), blocks)] += terms[t]

        walk(entry_ref, 2 * p + (place.side if keep else 1 - place.side), slots, step)
        for h in range(cuts):
            for d in range(chips):
                at = ((place.chip ^ d) * cuts + h) * per
                to = ((h * chips + d) * pairs + p) * per
                out_ref[to : to + per] = acc[pl.ds(at, per)].astype(out_ref.dtype)
    if not keep:
        for n in range(2):
            out_ref[pairs * blocks + n] = refs[-1][n * width : (n + 1) * width, :]


def backward(plan, tiles, ups, pairs, chips, cuts, term=None):
    block = tiles.shape[1]
    count, width, rows = ups[0].shape
    panel = len(ups) * count * rows
    blocks = panel // block
    shape = (cuts, chips, pairs, blocks // chips // cuts, width, block)
    keep = term is None
    out_shape = (pairs * blocks + (0 if keep else 2), width, block)
    return call(
        functools.partial(backward_body, slots=plan.shape[1] - 1, keep=keep, shape=shape),
        [tiles, *ups] + ([] if keep else [term]),
        jax.ShapeDtypeStruct(out_shape, F32 if keep else BF16),
        scalars=(plan,),
        scratch=[pltpu.VMEM((width, panel), BF16), pltpu.VMEM((blocks + 1, width, block), F32)],
        estimate=cost(2 * 64 * block * block * width, 12 * MIB),
        name="backward",
    )


def join_body(kept_ref, given_ref, term_ref, *refs, cuts, chips):
    outs, grad = refs[:-1], refs[-1]
    place = Place()
    width = grad.shape[0]
    blocks = kept_ref.shape[0]
    mate = given_ref[blocks].astype(F32) + given_ref[blocks + 1].astype(F32)
    grad[...] = sum_of_parts(term_ref, 0, width) + mate
    per = blocks // (cuts * chips)
    for h in range(cuts):
        for d in range(chips):
            out = outs[h * chips + d]
            for b in range(per):
                n = (h * chips + d) * per + b
                out[b * width : (b + 1) * width, :] = (
                    kept_ref[n] + given_ref[n].astype(F32)
                ).astype(out.dtype)
            if h == 0:
                rows, end = width // chips, per * width
                high, low = two_parts(grad[pl.ds((place.chip ^ d) * rows, rows), :])
                if d == 0:
                    out[end : end + rows, :] = high.astype(F32) + low.astype(F32)
                else:
                    out[end : end + rows, :] = high
                    out[end + rows : end + 2 * rows, :] = low


def join(kept, given, term, cuts, chips):
    blocks, width, block = kept.shape
    rows = blocks // (cuts * chips) * width
    extra = width // chips
    outs = [
        jax.ShapeDtypeStruct(
            (rows + (0 if h else 2 * extra if d else extra), block), BF16 if d else F32
        )
        for h in range(cuts)
        for d in range(chips)
    ]
    got = call(
        functools.partial(join_body, cuts=cuts, chips=chips),
        [kept, given, term],
        outs,
        scratch=[pltpu.VMEM((width, width), F32)],
        name="join",
    )
    return [got[h * chips : (h + 1) * chips] for h in range(cuts)]


def gather_body(*refs, count, rows):
    out_ref = refs[-1]
    terms = [ref[:rows, :].astype(F32) for ref in refs[:count]]
    out_ref[:rows, :] = tree_sum(terms).astype(BF16)
    extra = (out_ref.shape[0] - rows) // 2
    if extra:
        terms = [refs[0][rows : rows + extra, :]]
        terms += [sum_of_parts(ref, rows, extra) for ref in refs[1:count]]
        high, low = two_parts(tree_sum(terms))
        out_ref[rows : rows + extra, :] = high
        out_ref[rows + extra : rows + 2 * extra, :] = low


def gather_sum(terms, after, rows):
    return call(
        functools.partial(gather_body, count=len(terms), rows=rows),
        [*terms, *after],
        like(terms[-1]),
        name="gather_sum",
    )


def owner_of(chip, core, k, reps):
    to = chip ^ k
    return 2 * to + (core ^ (to // (reps // 2) % 2))


def route_body(*refs, reps, chips, rows, pairs):
    spread, outs = refs[:reps], refs[reps + 1 :]
    place = Place()
    each = rows // pairs
    extra = (spread[0].shape[0] - rows) // 2
    if extra:
        high, low = two_parts(tree_sum([sum_of_parts(ref, rows, extra) for ref in spread]))
    for k in range(chips):
        target = owner_of(place.chip, place.core, k, reps)
        for d in range(reps):

            @pl.when(((target % reps) ^ place.rep) == d)
            def _():
                at = pl.multiple_of(target // reps // 2 * each, each)
                outs[k][:each, :] = spread[d][pl.ds(at, each), :]

        if extra:
            outs[k][each : each + extra, :] = high
            outs[k][each + extra : each + 2 * extra, :] = low


def route(spread, after, chips, rows, pairs):
    height, width = spread[0].shape
    outs = [jax.ShapeDtypeStruct((height - rows + rows // pairs, width), BF16)] * chips
    body = functools.partial(route_body, reps=len(spread), chips=chips, rows=rows, pairs=pairs)
    return call(body, [*spread, after], outs, name="route")


def hot_body(order_ref, _, out_ref, token_ref):
    panel = out_ref.shape[0]
    rows = 256
    target = order_ref[...]
    token_ref[...] = jnp.zeros_like(token_ref)

    @pl.loop(0, panel // rows)
    def _(i):
        at = pl.multiple_of(i * rows, rows)
        hot = lax.broadcasted_iota(jnp.int32, (rows, panel), 0) + at == target
        out_ref[pl.ds(at, rows), :] = jnp.where(hot, 1.0, 0.0).astype(BF16)


def inverse_hot(order_row, after):
    panel = order_row.shape[1]
    return pl.pallas_call(
        hot_body,
        out_shape=(
            pltpu.VMEM((panel, panel), BF16),
            jax.ShapeDtypeStruct((8, 128), jnp.int32),
        ),
        grid=(1,),
        in_specs=[whole_spec(order_row), pl.BlockSpec(memory_space=pl.ANY)],
        out_specs=(
            pl.BlockSpec(memory_space=pltpu.VMEM),
            pl.BlockSpec((8, 128), lambda i: (0, 0)),
        ),
        compiler_params=params(8),
        cost_estimate=cost(0, 6 * MIB),
        name="inverse_hot",
    )(order_row, after)


def restore_body(hot_ref, *refs, first, count, per, scale):
    parts, refs = refs[:count], refs[count:]
    start, (out_ref, grad_ref) = refs[:-2], refs[-2:]
    chip = lax.axis_index("section") // 2
    block = parts[0].shape[1]
    extra = (parts[0].shape[0] - per * block) // 2
    length = per * block
    base = pl.program_id(0) * out_ref.shape[0]

    @pl.when(base == 0)
    def _():
        grad_ref[...] = start[1][...] if start else jnp.zeros_like(grad_ref)
        for n, part in enumerate(parts):
            at = pl.multiple_of((chip ^ (first + n)) * extra, extra)
            grad_ref[pl.ds(at, extra), :] = sum_of_parts(part, length, extra) * scale

    columns, places = [], []
    for n, part in enumerate(parts):
        columns.append(
            jnp.concatenate([part[b * block : (b + 1) * block, :] for b in range(per)], axis=1)
        )
        places.append(pl.multiple_of((chip ^ (first + n)) * length, length))
    rows = min(512, out_ref.shape[0])
    for i in range(out_ref.shape[0] // rows):
        span = pl.ds(pl.multiple_of(base + i * rows, rows), rows)
        acc = start[0][span, :] if start else None
        for n, at in enumerate(places):
            term = lax.dot_general(
                hot_ref[span, pl.ds(at, length)],
                columns[n],
                (((1,), (1,)), ((), ())),
                preferred_element_type=F32,
            )
            acc = term if acc is None else acc + term
        out_ref[i * rows : (i + 1) * rows, :] = acc.astype(out_ref.dtype)


def restore(hot, parts, first, start, per, scale):
    panel = hot.shape[0]
    width = parts[0].shape[1]
    body = functools.partial(
        restore_body, first=first, count=len(parts), per=per, scale=scale
    )
    outs = (
        jax.ShapeDtypeStruct((panel, width), BF16 if start else F32),
        jax.ShapeDtypeStruct((width, width), F32),
    )
    return call(
        body,
        [hot, *parts, *start],
        outs,
        results=(0, 1) if start else (),
        steps=4 if start else 1,
        estimate=cost(2 * panel * panel * width, 4 * panel * width),
        name="restore",
    )


def tree_sum(terms):
    while len(terms) > 1:
        terms = [terms[i] + terms[i + 1] for i in range(0, len(terms), 2)]
    return terms[0]


def shards(features, order, tiles, tile_rows, tile_cols, live, weight, cotangent):
    reps = lax.axis_size("rep")
    sections = lax.axis_size("section")
    panel, width = features.shape
    rounds, slots, block, _ = tiles.shape[2:]
    blocks = panel // block
    chips = sections // 2
    pairs = rounds // 2
    near = reps // 2

    def over_chips(x, d):
        return lax.ppermute(x, "section", [(s, s ^ (2 * d)) for s in range(sections)])

    def over_cores(x):
        return lax.ppermute(x, "section", [(s, s ^ 1) for s in range(sections)])

    def over_reps(x, d):
        return lax.ppermute(x, "rep", [(r, r ^ d) for r in range(reps)])

    def from_owner(x, d):
        moves = []
        for r in range(reps):
            for j in range(rounds):
                source = j * reps + r
                target = (source ^ (2 * d)) ^ ((d // near) & 1)
                moves.append((source * reps + r, target * reps + r))
        return lax.ppermute(x, ("section", "rep"), moves)

    order_rows, order_row = order.reshape(panel // block, block), order.reshape(1, panel)
    owns = reorder(order_rows, features)
    gots = [[own] + [from_owner(own, d) for d in range(1, chips)] for own in owns]
    bits = (blocks - 1).bit_length()
    plan = entries_of(tile_rows, tile_cols, live, bits, owns[-1][:16])
    own_tiles = tiles.reshape(rounds * slots, block, block)

    mine, mate = [], []
    for p in range(pairs):
        for h in range(HALVES):
            first = 2 * p * near
            picked = pick(gots[h][first : first + 2 * near], near, [] if h else [plan])
            mine.append(picked)
            mate.append(over_cores(picked))

    started = forward(plan, own_tiles, mine, None, reps)
    own, *others = forward(plan, own_tiles, mate, started, reps)
    sent = {d: over_reps(others[d - 1], d) for d in reversed(range(1, reps))}
    aggregated = total_of(own, [sent[d] for d in range(1, reps)])
    shares = [aggregated] + [over_reps(aggregated, d) for d in range(1, reps)]

    up_early, term = up_shares(weight, cotangent, shares[:near], 0)
    ups = [up_early, *up_shares(weight, cotangent, shares[near:], near)]
    cuts = 1
    given = over_cores(backward(plan, own_tiles, ups, pairs, chips, cuts, term))
    kept = backward(plan, own_tiles, ups, pairs, chips, cuts)
    chunks = join(kept, given, term, cuts, chips)
    arrived = [[over_chips(c[d], d) for d in range(1, chips)] for c in chunks]
    late_shares = lax.optimization_barrier((shares, chunks[-1][-1]))[0]
    hidden, token = finish(weight, late_shares)
    per = blocks // chips // cuts
    height = pairs * per * width
    reduced = gather_sum([chunks[0][0], *arrived[0]], [token], height)

    def to_owner(block, k):
        moves = [(s, owner_of(s // 2, s % 2, k, reps)) for s in range(sections)]
        return lax.ppermute(block, "section", moves)

    spread = [reduced] + [over_reps(reduced, d) for d in range(1, reps)]
    hot, ready = inverse_hot(order_row, reduced)
    routed = route(spread, ready, chips, height, pairs)
    parts = [to_owner(block, k) for k, block in enumerate(routed)]
    scale = 1.0 / math.sqrt(panel * sections)
    half = chips // 2
    begun = restore(hot, parts[:half], 0, (), per, scale)
    feature_grad, weight_grad = restore(hot, parts[half:], half, begun, per, scale)
    return (hidden, weight_grad, feature_grad)


def solution(mesh):
    placed = (
        P("section", None),
        P("section"),
        P("section", "rep", None, None, None, None),
        P("section", "rep", None, None),
        P("section", "rep", None, None),
        P("section", "rep", None),
        P(),
        P("section", None),
    )
    return jax.shard_map(
        shards,
        mesh=mesh,
        in_specs=placed,
        out_specs=(P("section", None), P(), P("section", None)),
        check_vma=False,
    )
```

```python
import functools
import math

import jax
import jax.numpy as jnp
from jax import lax
from jax.experimental import pallas as pl
from jax.experimental.pallas import tpu as pltpu
from jax.sharding import PartitionSpec as P

F32 = jnp.float32
BF16 = jnp.bfloat16
MIB = 1 << 20


def params(mib):
    return pltpu.CompilerParams(vmem_limit_bytes=mib * MIB)


def cost(flops, nbytes):
    return pl.CostEstimate(flops=int(flops), bytes_accessed=int(nbytes), transcendentals=0)


def whole_spec(array):
    zeros = (0,) * array.ndim
    return pl.BlockSpec(array.shape, lambda *_: zeros)


HALVES = 2
GROUP = 16


class Place:
    def __init__(self):
        reps = lax.axis_size("rep")
        section = lax.axis_index("section")
        self.rep = lax.axis_index("rep")
        self.chip = section // 2
        self.core = section % 2
        self.side = (section + self.rep) % 2
        self.row = section // reps
        self.low = ((section % reps) // 2) ^ (self.rep // 2)


def in_vmem(array):
    return pltpu.with_memory_space_constraint(array, pltpu.VMEM)


def in_hbm(array):
    return pltpu.with_memory_space_constraint(array, pltpu.HBM)


def call(
    body, operands, outs, scalars=(), scratch=(), blocked=(), results=(), mib=12, estimate=None, name=None
):
    in_place = pl.BlockSpec(memory_space=pltpu.VMEM)
    many = isinstance(outs, (list, tuple))
    outs = list(outs) if many else [outs]
    got = pl.pallas_call(
        body,
        out_shape=[
            out if n in results else pltpu.VMEM(out.shape, out.dtype) for n, out in enumerate(outs)
        ],
        grid_spec=pltpu.PrefetchScalarGridSpec(
            num_scalar_prefetch=len(scalars),
            grid=(1,),
            in_specs=[
                whole_spec(x) if n in blocked else in_place for n, x in enumerate(operands)
            ],
            out_specs=[
                whole_spec(out) if n in results else in_place for n, out in enumerate(outs)
            ],
            scratch_shapes=list(scratch),
        ),
        compiler_params=params(mib),
        cost_estimate=estimate or cost(0, MIB),
        name=name,
    )(*scalars, *[x if n in blocked else in_vmem(x) for n, x in enumerate(operands)])
    return got if many else got[0]


def like(array, dtype=None):
    return jax.ShapeDtypeStruct(array.shape, dtype or array.dtype)


def reorder_body(order_ref, feat_ref, out_ref, *, first):
    panel = feat_ref.shape[0]
    rows = out_ref.shape[0]
    step = order_ref.shape[1]
    order = order_ref[...].T
    for i in range(first // step, (first + rows) // step):
        hot = lax.broadcasted_iota(jnp.int32, (step, panel), 1) == order[:, i : i + 1]
        hot = jnp.where(hot, 1.0, 0.0).astype(BF16)
        at = i * step - first
        out_ref[at : at + step, :] = jnp.dot(
            hot, feat_ref[...], preferred_element_type=F32
        ).astype(BF16)


def reorder(order_rows, features, half):
    panel, width = features.shape
    rows = panel // HALVES
    return call(
        functools.partial(reorder_body, first=half * rows),
        [in_hbm(order_rows), in_hbm(features)],
        jax.ShapeDtypeStruct((rows, width), BF16),
        blocked=(0, 1),
        estimate=cost(2 * rows * panel * width, 4 * rows * width),
        name="reorder",
    )


def entry_body(rows_ref, cols_ref, live_ref, _, out_ref, *, bits):
    rounds, slots = rows_ref.shape[2:]
    out_ref[:, :slots] = (rows_ref[0, 0] << bits) | cols_ref[0, 0]
    for j in range(rounds):
        out_ref[j : j + 1, slots:] = jnp.full((1, 1), live_ref[0, 0, j], jnp.int32)


def entries_of(rows, cols, live, bits, after):
    rounds, slots = rows.shape[2:]
    shape = (rounds, slots + 1)
    return pl.pallas_call(
        functools.partial(entry_body, bits=bits),
        out_shape=jax.ShapeDtypeStruct(shape, jnp.int32),
        grid=(1,),
        in_specs=[
            whole_spec(rows),
            whole_spec(cols),
            pl.BlockSpec(memory_space=pltpu.SMEM),
            whole_spec(after),
        ],
        out_specs=pl.BlockSpec(shape, lambda i: (0, 0)),
        compiler_params=params(12),
        cost_estimate=cost(0, MIB),
        name="entries_of",
    )(*map(in_hbm, (rows, cols, live)), after)


def pick_body(*refs, near, count):
    options, out_ref = refs[:count], refs[-1]
    place = Place()
    for n, option in enumerate(options):

        @pl.when((place.side == n // near) & (place.low == n % near))
        def _():
            out_ref[...] = option[...]


def pick(options, near, after):
    body = functools.partial(pick_body, near=near, count=len(options))
    return call(body, [*options, *after], like(options[0]), name="pick")


def walk(entry_ref, j, slots, step):
    count = entry_ref[j, slots]

    @pl.loop(0, (count + GROUP - 1) // GROUP)
    def _(g):
        entries = [entry_ref[j, g * GROUP + t] for t in range(GROUP)]
        alive = [g * GROUP + t < count for t in range(GROUP)]
        step(j * slots + g * GROUP, entries, alive)


def forward_body(entry_ref, tiles_ref, *refs, slots, pairs, last):
    place = Place()
    xs, rest = refs[: pairs * HALVES], refs[pairs * HALVES :]
    panel_ref, acc = rest[-2:]
    blocks, block, width = panel_ref.shape
    bits = (blocks - 1).bit_length()
    if last:
        start, outs = rest[0], rest[1:-2]
        acc[pl.ds(0, blocks)] = start[...]
        acc[blocks] = jnp.zeros((block, width), F32)
    else:
        outs = rest[:-2]
        acc[...] = jnp.zeros_like(acc)
    per = blocks // HALVES
    for p in range(pairs):
        for h in range(HALVES):
            panel_ref[h * per : (h + 1) * per] = xs[p * HALVES + h][...].reshape(per, block, width)

        def step(first, entries, alive):
            terms = []
            for t in range(GROUP):
                x = panel_ref[entries[t] & (blocks - 1)]
                terms.append(jnp.dot(tiles_ref[first + t], x, preferred_element_type=F32))
            for t in range(GROUP):
                acc[jnp.where(alive[t], entries[t] >> bits, blocks)] += terms[t]

        j = place.row ^ (2 * p + (1 - place.side if last else place.side))
        walk(entry_ref, j, slots, step)
    if last:
        span = blocks // len(outs)
        for d, out in enumerate(outs):
            at = (place.rep ^ d) * span
            out[...] = acc[pl.ds(at, span)].reshape(out.shape).astype(out.dtype)
    else:
        outs[0][...] = acc[pl.ds(0, blocks)]


def forward(plan, tiles, xs, start, reps):
    block = tiles.shape[1]
    width = xs[0].shape[1]
    pairs = len(xs) // HALVES
    blocks = xs[0].shape[0] * HALVES // block
    last = start is not None
    if last:
        rows = blocks * block // reps
        outs = [jax.ShapeDtypeStruct((rows, width), BF16 if d else F32) for d in range(reps)]
    else:
        outs = [jax.ShapeDtypeStruct((blocks, block, width), F32)]
    body = functools.partial(
        forward_body, slots=plan.shape[1] - 1, pairs=pairs, last=last
    )
    got = call(
        body,
        [tiles, *xs] + ([start] if last else []),
        outs,
        scalars=(plan,),
        scratch=[pltpu.VMEM((blocks, block, width), BF16), pltpu.VMEM((blocks + 1, block, width), F32)],
        estimate=cost(2 * 64 * block * block * width, 12 * MIB),
        name="forward",
    )
    return got if last else got[0]


def total_body(own_ref, *refs):
    total = own_ref[...]
    for ref in refs[:-1]:
        total = total + ref[...].astype(F32)
    refs[-1][...] = total.astype(BF16)


def total_of(own, others):
    return call(total_body, [own, *others], like(own, BF16), name="total_of")


def gradient_of(agg, co, weight):
    pre = jnp.dot(agg, weight, preferred_element_type=F32)
    gate = 1.0 / (1.0 + jnp.exp(-pre))
    grad_pre = (co.astype(F32) * gate * (1.0 + pre * (1.0 - gate))).astype(BF16)
    return pre, gate, grad_pre


def two_parts(value):
    high = value.astype(BF16)
    return high, (value - high.astype(F32)).astype(BF16)


def sum_of_parts(ref, at, rows):
    return ref[at : at + rows, :].astype(F32) + ref[at + rows : at + 2 * rows, :].astype(F32)


def up_body(w_ref, co_ref, *refs, first, count):
    place = Place()
    shares, out_ref = refs[:count], refs[count]
    weight = w_ref[...]
    rows = shares[0].shape[0]
    for n, share in enumerate(shares):
        at = pl.multiple_of((place.rep ^ (first + n)) * rows, rows)
        _, _, grad_pre = gradient_of(share[...], co_ref[pl.ds(at, rows), :], weight)
        if first + n == 0:
            grad = lax.dot_general(
                share[...], grad_pre, (((0,), (0,)), ((), ())), preferred_element_type=F32
            )
            width = grad.shape[0]
            refs[count + 1][:width, :], refs[count + 1][width:, :] = two_parts(grad)
        out_ref[n] = lax.dot_general(
            weight, grad_pre, (((1,), (1,)), ((), ())), preferred_element_type=F32
        ).astype(BF16)


def up_shares(weight, cotangent, shares, first):
    rows, width = shares[0].shape
    outs = [jax.ShapeDtypeStruct((len(shares), width, rows), BF16)]
    if first == 0:
        outs.append(jax.ShapeDtypeStruct((2 * width, width), BF16))
    return call(
        functools.partial(up_body, first=first, count=len(shares)),
        [weight, cotangent, *shares],
        outs,
        estimate=cost(4 * len(shares) * rows * width * width, 2 * MIB),
        name="up_shares",
    )


def finish_body(w_ref, *refs):
    place = Place()
    shares, (hidden_ref, token_ref) = refs[:-2], refs[-2:]
    rows = shares[0].shape[0]
    for n, share in enumerate(shares):
        at = pl.multiple_of((place.rep ^ n) * rows, rows)
        pre = jnp.dot(share[...], w_ref[...], preferred_element_type=F32)
        hidden_ref[pl.ds(at, rows), :] = (pre * (1.0 / (1.0 + jnp.exp(-pre)))).astype(BF16)
    token_ref[...] = jnp.zeros_like(token_ref)


def finish(weight, shares):
    rows, width = shares[0].shape
    outs = (
        jax.ShapeDtypeStruct((rows * len(shares), width), BF16),
        jax.ShapeDtypeStruct((8, 128), jnp.int32),
    )
    return call(finish_body, [weight, *shares], outs, results=(0,), estimate=cost(0, 4 * MIB), name="finish")


def backward_body(entry_ref, tiles_ref, *refs, slots, keep, shape):
    refs, (out_ref, up_all, acc) = refs[:-3], refs[-3:]
    ups = refs if keep else refs[:-1]
    place = Place()
    cuts, chips, pairs, per, width, block = shape
    blocks = cuts * chips * per
    bits = (blocks - 1).bit_length()
    count, _, rows = ups[0].shape
    for m, up in enumerate(ups):
        for n in range(count):
            at = pl.multiple_of((place.rep ^ (m * count + n)) * rows, rows)
            up_all[:, pl.ds(at, rows)] = up[n]
    for p in range(pairs):
        acc[...] = jnp.zeros_like(acc)

        def step(first, entries, alive):
            terms = []
            for t in range(GROUP):
                at = pl.multiple_of((entries[t] >> bits) * block, block)
                terms.append(
                    jnp.dot(
                        up_all[:, pl.ds(at, block)],
                        tiles_ref[first + t],
                        preferred_element_type=F32,
                    )
                )
            for t in range(GROUP):
                acc[jnp.where(alive[t], entries[t] & (blocks - 1), blocks)] += terms[t]

        walk(entry_ref, 2 * p + (place.side if keep else 1 - place.side), slots, step)
        for h in range(cuts):
            for d in range(chips):
                at = ((place.chip ^ d) * cuts + h) * per
                to = ((h * chips + d) * pairs + p) * per
                out_ref[to : to + per] = acc[pl.ds(at, per)].astype(out_ref.dtype)
    if not keep:
        for n in range(2):
            out_ref[pairs * blocks + n] = refs[-1][n * width : (n + 1) * width, :]


def backward(plan, tiles, ups, pairs, chips, cuts, term=None):
    block = tiles.shape[1]
    count, width, rows = ups[0].shape
    panel = len(ups) * count * rows
    blocks = panel // block
    shape = (cuts, chips, pairs, blocks // chips // cuts, width, block)
    keep = term is None
    out_shape = (pairs * blocks + (0 if keep else 2), width, block)
    return call(
        functools.partial(backward_body, slots=plan.shape[1] - 1, keep=keep, shape=shape),
        [tiles, *ups] + ([] if keep else [term]),
        jax.ShapeDtypeStruct(out_shape, F32 if keep else BF16),
        scalars=(plan,),
        scratch=[pltpu.VMEM((width, panel), BF16), pltpu.VMEM((blocks + 1, width, block), F32)],
        estimate=cost(2 * 64 * block * block * width, 12 * MIB),
        name="backward",
    )


def join_body(kept_ref, given_ref, term_ref, *refs, cuts, chips):
    outs, grad = refs[:-1], refs[-1]
    place = Place()
    width = grad.shape[0]
    blocks = kept_ref.shape[0]
    mate = given_ref[blocks].astype(F32) + given_ref[blocks + 1].astype(F32)
    grad[...] = sum_of_parts(term_ref, 0, width) + mate
    per = blocks // (cuts * chips)
    for h in range(cuts):
        for d in range(chips):
            out = outs[h * chips + d]
            for b in range(per):
                n = (h * chips + d) * per + b
                out[b * width : (b + 1) * width, :] = (
                    kept_ref[n] + given_ref[n].astype(F32)
                ).astype(out.dtype)
            if h == 0:
                rows, end = width // chips, per * width
                high, low = two_parts(grad[pl.ds((place.chip ^ d) * rows, rows), :])
                if d == 0:
                    out[end : end + rows, :] = high.astype(F32) + low.astype(F32)
                else:
                    out[end : end + rows, :] = high
                    out[end + rows : end + 2 * rows, :] = low


def join(kept, given, term, cuts, chips):
    blocks, width, block = kept.shape
    rows = blocks // (cuts * chips) * width
    extra = width // chips
    outs = [
        jax.ShapeDtypeStruct(
            (rows + (0 if h else 2 * extra if d else extra), block), BF16 if d else F32
        )
        for h in range(cuts)
        for d in range(chips)
    ]
    got = call(
        functools.partial(join_body, cuts=cuts, chips=chips),
        [kept, given, term],
        outs,
        scratch=[pltpu.VMEM((width, width), F32)],
        name="join",
    )
    return [got[h * chips : (h + 1) * chips] for h in range(cuts)]


def gather_body(*refs, count, rows):
    out_ref = refs[-1]
    terms = [ref[:rows, :].astype(F32) for ref in refs[:count]]
    out_ref[:rows, :] = tree_sum(terms).astype(BF16)
    extra = (out_ref.shape[0] - rows) // 2
    if extra:
        terms = [refs[0][rows : rows + extra, :]]
        terms += [sum_of_parts(ref, rows, extra) for ref in refs[1:count]]
        high, low = two_parts(tree_sum(terms))
        out_ref[rows : rows + extra, :] = high
        out_ref[rows + extra : rows + 2 * extra, :] = low


def gather_sum(terms, after, rows):
    return call(
        functools.partial(gather_body, count=len(terms), rows=rows),
        [*terms, *after],
        like(terms[-1]),
        name="gather_sum",
    )


def owner_of(chip, core, k, reps):
    to = chip ^ k
    return 2 * to + (core ^ (to // (reps // 2) % 2))


def route_body(*refs, reps, chips, rows, pairs):
    spread, outs = refs[:reps], refs[reps + 1 :]
    place = Place()
    each = rows // pairs
    extra = (spread[0].shape[0] - rows) // 2
    if extra:
        high, low = two_parts(tree_sum([sum_of_parts(ref, rows, extra) for ref in spread]))
    for k in range(chips):
        target = owner_of(place.chip, place.core, k, reps)
        for d in range(reps):

            @pl.when(((target % reps) ^ place.rep) == d)
            def _():
                at = pl.multiple_of(target // reps // 2 * each, each)
                outs[k][:each, :] = spread[d][pl.ds(at, each), :]

        if extra:
            outs[k][each : each + extra, :] = high
            outs[k][each + extra : each + 2 * extra, :] = low


def route(spread, after, chips, rows, pairs):
    height, width = spread[0].shape
    outs = [jax.ShapeDtypeStruct((height - rows + rows // pairs, width), BF16)] * chips
    body = functools.partial(route_body, reps=len(spread), chips=chips, rows=rows, pairs=pairs)
    return call(body, [*spread, after], outs, name="route")


def hot_body(order_ref, _, out_ref, token_ref):
    panel = out_ref.shape[0]
    rows = 256
    target = order_ref[...]
    token_ref[...] = jnp.zeros_like(token_ref)

    @pl.loop(0, panel // rows)
    def _(i):
        at = pl.multiple_of(i * rows, rows)
        hot = lax.broadcasted_iota(jnp.int32, (rows, panel), 0) + at == target
        out_ref[pl.ds(at, rows), :] = jnp.where(hot, 1.0, 0.0).astype(BF16)


def inverse_hot(order_row, after):
    panel = order_row.shape[1]
    return pl.pallas_call(
        hot_body,
        out_shape=(
            pltpu.VMEM((panel, panel), BF16),
            jax.ShapeDtypeStruct((8, 128), jnp.int32),
        ),
        grid=(1,),
        in_specs=[whole_spec(order_row), pl.BlockSpec(memory_space=pl.ANY)],
        out_specs=(
            pl.BlockSpec(memory_space=pltpu.VMEM),
            pl.BlockSpec((8, 128), lambda i: (0, 0)),
        ),
        compiler_params=params(8),
        cost_estimate=cost(0, 6 * MIB),
        name="inverse_hot",
    )(order_row, after)


def restore_body(hot_ref, *refs, hops, count, per, scale):
    parts, refs = refs[:count], refs[count:]
    start, (out_ref, grad_ref) = refs[:-2], refs[-2:]
    chip = lax.axis_index("section") // 2
    block = parts[0].shape[1]
    extra = (parts[0].shape[0] - per * block) // 2
    length = per * block
    grad_ref[...] = start[1][...] if start else jnp.zeros_like(grad_ref)
    columns, places = [], []
    for n, part in enumerate(parts):
        u = chip ^ hops[n]
        at = pl.multiple_of(u * extra, extra)
        grad_ref[pl.ds(at, extra), :] = sum_of_parts(part, length, extra) * scale
        columns.append(
            jnp.concatenate([part[b * block : (b + 1) * block, :] for b in range(per)], axis=1)
        )
        places.append(pl.multiple_of(u * length, length))
    rows = 512
    for i in range(out_ref.shape[0] // rows):
        span = slice(i * rows, (i + 1) * rows)
        acc = start[0][span, :] if start else None
        for n, at in enumerate(places):
            term = lax.dot_general(
                hot_ref[span, pl.ds(at, length)],
                columns[n],
                (((1,), (1,)), ((), ())),
                preferred_element_type=F32,
            )
            acc = term if acc is None else acc + term
        out_ref[span, :] = acc.astype(out_ref.dtype)


def restore(hot, parts, hops, start, per, scale):
    panel = hot.shape[0]
    width = parts[0].shape[1]
    body = functools.partial(
        restore_body, hops=hops, count=len(parts), per=per, scale=scale
    )
    outs = (
        jax.ShapeDtypeStruct((panel, width), BF16 if start else F32),
        jax.ShapeDtypeStruct((width, width), F32),
    )
    return call(
        body,
        [hot, *parts, *start],
        outs,
        results=(0, 1) if start else (),
        estimate=cost(2 * panel * panel * width, 4 * panel * width),
        name="restore",
    )


def tree_sum(terms):
    while len(terms) > 1:
        terms = [terms[i] + terms[i + 1] for i in range(0, len(terms), 2)]
    return terms[0]


def shards(features, order, tiles, tile_rows, tile_cols, live, weight, cotangent):
    reps = lax.axis_size("rep")
    sections = lax.axis_size("section")
    panel, width = features.shape
    rounds, slots, block, _ = tiles.shape[2:]
    blocks = panel // block
    chips = sections // 2
    pairs = rounds // 2
    near = reps // 2

    def over_chips(x, d):
        return lax.ppermute(x, "section", [(s, s ^ (2 * d)) for s in range(sections)])

    def over_cores(x):
        return lax.ppermute(x, "section", [(s, s ^ 1) for s in range(sections)])

    def over_reps(x, d):
        return lax.ppermute(x, "rep", [(r, r ^ d) for r in range(reps)])

    def from_owner(x, d):
        moves = []
        for r in range(reps):
            for j in range(rounds):
                source = j * reps + r
                target = (source ^ (2 * d)) ^ ((d // near) & 1)
                moves.append((source * reps + r, target * reps + r))
        return lax.ppermute(x, ("section", "rep"), moves)

    order_rows, order_row = order.reshape(panel // block, block), order.reshape(1, panel)
    owns = [reorder(order_rows, features, h) for h in range(HALVES)]
    gots = [[own] + [from_owner(own, d) for d in range(1, chips)] for own in owns]
    bits = (blocks - 1).bit_length()
    plan = entries_of(tile_rows, tile_cols, live, bits, owns[-1][:16])
    own_tiles = tiles.reshape(rounds * slots, block, block)

    mine, mate = [], []
    for p in range(pairs):
        for h in range(HALVES):
            first = 2 * p * near
            picked = pick(gots[h][first : first + 2 * near], near, [] if h else [plan])
            mine.append(picked)
            mate.append(over_cores(picked))

    started = forward(plan, own_tiles, mine, None, reps)
    own, *others = forward(plan, own_tiles, mate, started, reps)
    sent = {d: over_reps(others[d - 1], d) for d in reversed(range(1, reps))}
    aggregated = total_of(own, [sent[d] for d in range(1, reps)])
    shares = [aggregated] + [over_reps(aggregated, d) for d in range(1, reps)]

    up_early, term = up_shares(weight, cotangent, shares[:near], 0)
    ups = [up_early, *up_shares(weight, cotangent, shares[near:], near)]
    cuts = 1
    given = over_cores(backward(plan, own_tiles, ups, pairs, chips, cuts, term))
    kept = backward(plan, own_tiles, ups, pairs, chips, cuts)
    chunks = join(kept, given, term, cuts, chips)
    arrived = [[over_chips(c[d], d) for d in range(1, chips)] for c in chunks]
    late_shares = lax.optimization_barrier((shares, chunks[-1][-1]))[0]
    hidden, token = finish(weight, late_shares)
    per = blocks // chips // cuts
    height = pairs * per * width
    reduced = gather_sum([chunks[0][0], *arrived[0]], [token], height)

    def to_owner(block, k):
        moves = [(s, owner_of(s // 2, s % 2, k, reps)) for s in range(sections)]
        return lax.ppermute(block, "section", moves)

    spread = [reduced] + [over_reps(reduced, d) for d in range(1, reps)]
    hot, ready = inverse_hot(order_row, reduced)
    routed = route(spread, ready, chips, height, pairs)
    parts = [to_owner(block, k) for k, block in enumerate(routed)]
    scale = 1.0 / math.sqrt(panel * sections)
    half = chips // 2
    hops = [0, *reversed(range(1, chips))]
    begun = restore(hot, [parts[k] for k in hops[:half]], hops[:half], (), per, scale)
    feature_grad, weight_grad = restore(hot, [parts[k] for k in hops[half:]], hops[half:], begun, per, scale)
    return (hidden, weight_grad, feature_grad)


def solution(mesh):
    placed = (
        P("section", None),
        P("section"),
        P("section", "rep", None, None, None, None),
        P("section", "rep", None, None),
        P("section", "rep", None, None),
        P("section", "rep", None),
        P(),
        P("section", None),
    )
    return jax.shard_map(
        shards,
        mesh=mesh,
        in_specs=placed,
        out_specs=(P("section", None), P(), P("section", None)),
        check_vma=False,
    )
```
